128 devices in a mesh: patch: 128 (over z, y, x, core).
Axes of the slice: x: 4, y: 4, z: 4, core: 2. Of those that a mesh axis runs over, the one named last changes fastest.
Arguments:
- fine_state: bfloat16 [4096, 32, 512], P('patch'), may hold values from -6 to 6
- weight_in: bfloat16 [7, 32, 32], replicated, may hold values from -0.375 to 0.375
- weight_out: bfloat16 [7, 32, 32], replicated, may hold values from -0.375 to 0.375
- weight_coarse: bfloat16 [7, 32, 32], replicated, may hold values from -0.375 to 0.375
- cotangent: bfloat16 [4096, 32, 512], P('patch'), may hold values from -6 to 6
- owner_count: int32 [128], replicated, may hold values from 8 to 32, as said below
- neighbour: int32 [4096, 6], P('patch'), may hold values from 0 to 4095, as said below
- level_tag: int32 [4096, 6], P('patch'), may hold values from 0 to 1, as said below
- octant: int32 [4096], P('patch'), may hold values from -1 to 7, as said below
Outputs:
- output: bfloat16 [4096, 32, 512], P('patch')
- grad_state: bfloat16 [4096, 32, 512], P('patch')
- grad_in: float32 [7, 32, 32], replicated
- grad_out: float32 [7, 32, 32], replicated
- grad_coarse: float32 [7, 32, 32], replicated
The draws below stay inside these ranges and needn't reach their ends.
Inputs may be any that keep to these rules, and one draw needn't show every extreme that they name: `owner_count`: an owner's live patches take its first slots; the total over all owners is a multiple of 8. Where level_tag is 0 this names a live slot whose neighbour across face f XOR 1 is this slot; it lies earlier on the Morton curve across a low face and later across a high face, on an owner at most 2 indices away (exactly 2 for some pair). The Morton positions of two face neighbours differ by exactly 3 across dimension 0, 8 across dimension 1 and 16 across dimension 2. Elsewhere it names the slot itself. `level_tag`: 1 where the face borders a coarser region or the domain's edge (the patch's own layer stands in for the neighbour's) and on every face of an empty slot. `octant`: live patches at Morton positions 8q to 8q+7 form parent q and take the octants 0 to 7 once each; -1 in empty slots.
All inputs are finite; a program needn't handle non-finite values.
Results may differ from the reference program's by a relative error of at most 0.018.
Values may be sent and summed in bfloat16 or wider, within the bound.
No kernel may reach another device: no remote copies, remote signals or barrier semaphores. Data moves between devices by JAX's collectives and lax.ppermute only.
A program may use at most 320 MiB of HBM per device.

```python
import jax
import jax.numpy as jnp
from jax import lax

C = 32
EDGE = 8
SLOTS = 32
LMIN = 8
REACH = 2
CELLS = 512
PSLOTS = 4096
NPAR = 512
N_PATCH = 128


def geometry(key):
    key_list = [jax.random.fold_in(key, 101 + offset_id) for offset_id in range(7)]
    device_rank = jnp.arange(N_PATCH).astype(jnp.int32)
    counts = jax.random.randint(key_list[0], (N_PATCH,), LMIN, SLOTS + 1).astype(jnp.int32)
    low_block = jax.random.randint(key_list[1], (), 0, N_PATCH - REACH - 2).astype(jnp.int32)
    counts = jnp.where((device_rank > low_block) & (device_rank < low_block + REACH), LMIN, counts)
    counts = jnp.where(device_rank == low_block + REACH, SLOTS, counts)
    others = jnp.sum(jnp.where(device_rank < N_PATCH - 1, counts, 0))
    counts = jnp.where(device_rank == N_PATCH - 1, LMIN + jnp.mod(-(others + LMIN), 8), counts).astype(jnp.int32)
    patch_total = jnp.sum(counts)
    starts = jnp.cumsum(counts) - counts
    slot_ids = jnp.arange(PSLOTS).astype(jnp.int32)
    owner_ids = slot_ids // SLOTS
    within = slot_ids % SLOTS
    is_live = within < counts[owner_ids]
    position = starts[owner_ids] + within
    strides = [3, LMIN, REACH * LMIN]
    severed = jax.random.randint(key_list[5], (PSLOTS, 3), 0, 4) == 0
    special = starts[low_block + 1] - 1
    severed = severed & ~((slot_ids[:, None] == special) & (jnp.arange(3)[None, :] == 2))

    def slot_of(position_in):
        owner_here = jnp.sum(starts[None, :] <= position_in[:, None], axis=1).astype(jnp.int32) - 1
        return owner_here * SLOTS + position_in - starts[owner_here]
    columns = []
    tag_columns = []
    for face_axis in range(3):
        stride = strides[face_axis]
        lower_pos = position - stride
        higher = position + stride
        low_ok = is_live & (lower_pos >= 0) & ~severed[jnp.clip(lower_pos, 0, PSLOTS - 1), face_axis]
        high_ok = is_live & (higher < patch_total) & ~severed[jnp.clip(position, 0, PSLOTS - 1), face_axis]
        columns.append(jnp.where(low_ok, slot_of(jnp.clip(lower_pos, 0, patch_total - 1)), slot_ids))
        columns.append(jnp.where(high_ok, slot_of(jnp.clip(higher, 0, patch_total - 1)), slot_ids))
        tag_columns.append(jnp.where(low_ok, 0, 1))
        tag_columns.append(jnp.where(high_ok, 0, 1))
    scores = jax.random.randint(key_list[6], (PSLOTS // 8 + 1, 8), 0, 1 << 20) * 8 + jnp.arange(8)[None, :]
    orders = jnp.argsort(scores, axis=1).astype(jnp.int32)
    group = jnp.clip(position // 8, 0, PSLOTS // 8)
    octant = jnp.where(is_live, orders[group, position % 8], -1)
    return (counts, jnp.stack(columns, axis=1).astype(jnp.int32), jnp.stack(tag_columns, axis=1).astype(jnp.int32), octant.astype(jnp.int32))


def draw_owner_count(key, part):
    return geometry(key)[0]


def draw_neighbour(key, part):
    return geometry(key)[1]


def draw_level_tag(key, part):
    return geometry(key)[2]


def draw_octant(key, part):
    return geometry(key)[3]


def steps_of(own_key, shape, pieces, smallest, largest):
    def one(dim, shards_of):
        steps = jax.random.uniform(jax.random.fold_in(jax.random.fold_in(own_key, 6), dim), (shards_of,), jnp.float32, smallest / len(pieces), largest / len(pieces))
        return jnp.repeat(jnp.exp(steps), shape[dim] // shards_of).reshape((-1,) + (1,) * (len(shape) - dim - 1))

    factor_of = one(*pieces[0])
    for cut in pieces[1:]:
        factor_of = factor_of * one(*cut)
    return factor_of


def noise(own_key, dims, spread, bound, shards=(), dtype=jnp.bfloat16):
    loudness = steps_of(own_key, dims, shards, -0.22, 0.18) if shards else 1.0
    values = jax.random.normal(own_key, dims, jnp.float32) * spread * loudness
    return jnp.minimum(jnp.maximum(values, -bound), bound).astype(dtype)


def setup_inputs(seed: int = 0) -> dict:
    streams_of = jax.random.split(jax.random.key(seed), 10)
    fine_state = noise(streams_of[0], (PSLOTS, C, CELLS), 1.0, 6.0, ((0, 128),))
    weight_in = noise(streams_of[1], (7, C, C), (7 * C) ** -0.5, 0.375)
    weight_out = noise(streams_of[2], (7, C, C), (7 * C) ** -0.5, 0.375)
    weight_coarse = noise(streams_of[3], (7, C, C), (7 * C) ** -0.5, 0.375)
    cotangent = noise(streams_of[4], (PSLOTS, C, CELLS), 1.0, 6.0, ((0, 128),))
    owner_count = draw_owner_count(jax.random.fold_in(streams_of[9], 71), 0)
    neighbour = draw_neighbour(jax.random.fold_in(streams_of[9], 71), 0)
    level_tag = draw_level_tag(jax.random.fold_in(streams_of[9], 71), 0)
    octant = draw_octant(jax.random.fold_in(streams_of[9], 71), 0)
    return {"fine_state": fine_state, "weight_in": weight_in, "weight_out": weight_out, "weight_coarse": weight_coarse, "cotangent": cotangent, "owner_count": owner_count, "neighbour": neighbour, "level_tag": level_tag, "octant": octant}


def face_mask(face_id):
    cell_ids = jnp.arange(EDGE ** 3)
    coords = [cell_ids // (EDGE * EDGE), cell_ids // EDGE % EDGE, cell_ids % EDGE]
    return coords[face_id // 2] == (EDGE - 1 if face_id % 2 else 0)

def face_step(face_id):
    stride = EDGE ** (2 - face_id // 2)
    return stride if face_id % 2 else -stride

def face_layer(field, face_id):
    lead_dims = field.shape[:-1]
    cube = field.reshape(lead_dims + (EDGE, EDGE, EDGE))
    side = EDGE - 1 if face_id % 2 else 0
    if face_id // 2 == 0:
        sheet = cube[..., side, :, :]
    elif face_id // 2 == 1:
        sheet = cube[..., :, side, :]
    else:
        sheet = cube[..., side]
    return sheet.reshape(lead_dims + (EDGE * EDGE,))

def spread_layer(sheet, face_id):
    lead_dims = sheet.shape[:-1]
    square = sheet.reshape(lead_dims + (EDGE, EDGE))
    if face_id // 2 == 0:
        square = square[..., None, :, :]
    elif face_id // 2 == 1:
        square = square[..., :, None, :]
    else:
        square = square[..., :, :, None]
    return jnp.broadcast_to(square, lead_dims + (EDGE, EDGE, EDGE)).reshape(lead_dims + (EDGE ** 3,))

def all_layers(field):
    return jnp.stack([face_layer(field, face_id) for face_id in range(6)], axis=1)

def tap_field(field, ghost, face_id):
    return jnp.where(face_mask(face_id), spread_layer(ghost, face_id), jnp.roll(field, -face_step(face_id), axis=-1))

def conv_forward(field, ghosts, weight):
    weight_f = weight.astype(jnp.float32)
    summed = jnp.einsum('io,sic->soc', weight_f[0], field.astype(jnp.float32))
    for face_id in range(6):
        tapped = tap_field(field, ghosts[:, face_id], face_id).astype(jnp.float32)
        summed = summed + jnp.einsum('io,sic->soc', weight_f[face_id + 1], tapped)
    return summed

def conv_backward(field, ghosts, weight, cotan, owned):
    weight_f = weight.astype(jnp.float32)
    cotan_f = cotan.astype(jnp.float32)
    weighed = cotan_f * owned.astype(jnp.float32)[:, None, None]
    grad_field = jnp.einsum('io,soc->sic', weight_f[0], cotan_f)
    grad_weight = [jnp.einsum('sic,soc->io', field.astype(jnp.float32), weighed)]
    sheets = []
    for face_id in range(6):
        moved = jnp.einsum('io,soc->sic', weight_f[face_id + 1], cotan_f)
        grad_field = grad_field + jnp.roll(jnp.where(face_mask(face_id), 0.0, moved), face_step(face_id), axis=-1)
        sheets.append(face_layer(moved, face_id))
        tapped = tap_field(field, ghosts[:, face_id], face_id).astype(jnp.float32)
        grad_weight.append(jnp.einsum('sic,soc->io', tapped, weighed))
    return (grad_field, jnp.stack(sheets, axis=1), jnp.stack(grad_weight))

def settle(grad_field, sheets):
    for face_id in range(6):
        grad_field = grad_field + jnp.where(face_mask(face_id), spread_layer(sheets[:, face_id].astype(jnp.float32), face_id), 0.0)
    return grad_field

def restrict_sum(field):
    lead_dims = field.shape[:-1]
    half = EDGE // 2
    groups = field.astype(jnp.float32).reshape(lead_dims + (half, 2, half, 2, half, 2))
    return groups.sum(axis=(-5, -3, -1)).reshape(lead_dims + (half ** 3,))

def spread_block(block):
    lead_dims = block.shape[:-1]
    half = EDGE // 2
    small = block.reshape(lead_dims + (half, 1, half, 1, half, 1))
    return jnp.broadcast_to(small, lead_dims + (half, 2, half, 2, half, 2)).reshape(lead_dims + (EDGE ** 3,))

def octants_to_cells(rows):
    lead_dims = rows.shape[:-3]
    width = rows.shape[-2]
    half = EDGE // 2
    count = len(lead_dims)
    parts = rows.reshape(lead_dims + (2, 2, 2, width, half, half, half))
    order = list(range(count)) + [count + 3, count, count + 4, count + 1, count + 5, count + 2, count + 6]
    return parts.transpose(order).reshape(lead_dims + (width, EDGE ** 3))

def cells_to_octants(field):
    lead_dims = field.shape[:-2]
    width = field.shape[-2]
    half = EDGE // 2
    count = len(lead_dims)
    parts = field.reshape(lead_dims + (width, 2, half, 2, half, 2, half))
    order = list(range(count)) + [count + 1, count + 3, count + 5, count, count + 2, count + 4, count + 6]
    return parts.transpose(order).reshape(lead_dims + (8, width, half ** 3))

def silu_slope(value):
    sigma = jax.nn.sigmoid(value)
    return sigma * (1.0 + value * (1.0 - sigma))

def per_owner(func, arrays):
    shaped = tuple((item.reshape((N_PATCH, SLOTS) + item.shape[1:]) for item in arrays))
    return lax.map(lambda group: func(*group), shaped)

def flat_slots(item):
    return item.reshape((N_PATCH * SLOTS,) + item.shape[2:])

def reference(fine_state, weight_in, weight_out, weight_coarse, cotangent, owner_count, neighbour, level_tag, octant):
    slot_ids = jnp.arange(PSLOTS).astype(jnp.int32)
    within = slot_ids % SLOTS
    owner_ids = slot_ids // SLOTS
    is_live = within < owner_count[owner_ids]
    starts = jnp.cumsum(owner_count) - owner_count
    position = starts[owner_ids] + within
    live_mask = is_live[:, None, None]
    state_zero = jnp.where(live_mask, fine_state, jnp.zeros_like(fine_state))
    cotan_zero = jnp.where(live_mask, cotangent, jnp.zeros_like(cotangent))
    tag_high = (level_tag == 1)[:, :, None, None]
    opposite = jnp.array([1, 0, 3, 2, 5, 4], jnp.int32)

    def pick(layer_pack):
        received = layer_pack[neighbour, opposite[None, :]]
        return jnp.where(tag_high, layer_pack, received)
    slot_ones = jnp.ones((SLOTS,), jnp.float32)

    def conv_in(field, ghosts):
        return conv_forward(field, ghosts, weight_in)

    def conv_out(field, ghosts):
        return conv_forward(field, ghosts, weight_out)
    ghosts_in = pick(all_layers(state_zero))
    pre_a = flat_slots(per_owner(conv_in, (state_zero, ghosts_in)))
    hidden = jax.nn.silu(pre_a).astype(jnp.bfloat16)
    restricted = (restrict_sum(hidden) * 0.125).astype(jnp.bfloat16)
    half_cells = (EDGE // 2) ** 3
    width = fine_state.shape[1]
    parent_rows = jnp.where(is_live, position // 8 * 8 + octant, NPAR * 8)
    coarse = jnp.zeros((NPAR * 8, width, half_cells), jnp.bfloat16).at[parent_rows].set(restricted, mode='drop')
    coarse = octants_to_cells(coarse.reshape(NPAR, 8, width, half_cells))
    coarse_ghosts = all_layers(coarse)
    pre_b = conv_forward(coarse, coarse_ghosts, weight_coarse)
    coarse_act = jax.nn.silu(pre_b).astype(jnp.bfloat16)
    act_rows = cells_to_octants(coarse_act).reshape(NPAR * 8, width, half_cells)
    safe_rows = jnp.clip(parent_rows, 0, NPAR * 8 - 1)
    upward = spread_block(act_rows[safe_rows])
    upward = jnp.where(live_mask, upward, jnp.zeros_like(upward))
    merged = (hidden.astype(jnp.float32) + upward.astype(jnp.float32)).astype(jnp.bfloat16)
    ghosts_out = pick(all_layers(merged))
    post = flat_slots(per_owner(conv_out, (merged, ghosts_out)))
    output = (state_zero.astype(jnp.float32) + post).astype(jnp.bfloat16)

    def back_out(field, ghosts, cotan):
        return conv_backward(field, ghosts, weight_out, cotan, slot_ones)

    def back_in(field, ghosts, cotan):
        return conv_backward(field, ghosts, weight_in, cotan, slot_ones)
    local_merged, ghost_out, dw_out = per_owner(back_out, (merged, ghosts_out, cotan_zero))
    local_merged = flat_slots(local_merged)
    ghost_out = flat_slots(ghost_out).astype(jnp.bfloat16)
    grad_merged = settle(local_merged, pick(ghost_out)).astype(jnp.bfloat16)
    grad_up = restrict_sum(grad_merged).astype(jnp.bfloat16)
    grad_act = jnp.zeros((NPAR * 8, width, half_cells), jnp.bfloat16).at[parent_rows].set(grad_up, mode='drop')
    grad_act = octants_to_cells(grad_act.reshape(NPAR, 8, width, half_cells))
    grad_pre_b = (grad_act.astype(jnp.float32) * silu_slope(pre_b)).astype(jnp.bfloat16)
    local_coarse, coarse_sheets, dw_coarse = conv_backward(coarse, coarse_ghosts, weight_coarse, grad_pre_b, jnp.ones((NPAR,), jnp.float32))
    grad_coarse_in = settle(local_coarse, coarse_sheets).astype(jnp.bfloat16)
    back_rows = cells_to_octants(grad_coarse_in).reshape(NPAR * 8, width, half_cells)
    downward = spread_block(back_rows[safe_rows]).astype(jnp.float32) * 0.125
    downward = jnp.where(live_mask, downward, 0.0)
    grad_hidden = grad_merged.astype(jnp.float32) + downward
    grad_pre_a = (grad_hidden * silu_slope(pre_a)).astype(jnp.bfloat16)
    local_state, ghost_in, dw_in = per_owner(back_in, (state_zero, ghosts_in, grad_pre_a))
    local_state = flat_slots(local_state)
    ghost_in = flat_slots(ghost_in).astype(jnp.bfloat16)
    grad_state = settle(cotan_zero.astype(jnp.float32) + local_state, pick(ghost_in)).astype(jnp.bfloat16)
    scale = 1.0 / jnp.sqrt(jnp.float32(PSLOTS * CELLS))
    return (output, grad_state, lax.optimization_barrier(jnp.sum(dw_in, axis=0)) * scale, lax.optimization_barrier(jnp.sum(dw_out, axis=0)) * scale, dw_coarse * scale)
```

```python
import functools
import math

import numpy as np
import jax
import jax.numpy as jnp
from jax import lax
from jax.experimental import pallas as pl
from jax.experimental.pallas import tpu as pltpu
from jax.sharding import PartitionSpec as P

BF = jnp.bfloat16
F32 = jnp.float32
EDGE = 8
CELLS = 512
SLOTS = 32
C = 32
PB = 8
STEPS = SLOTS // PB
NPAR = 5
STRIDES = (64, 8, 1)
MORTON = (3, 8, 16)
ROW0 = (24, 16, 0)
NEAR = 27
FAR = 8
BASE_A = 6 * SLOTS
BASE_B = BASE_A + NEAR
BASE_C = BASE_B + NEAR + FAR
ROWS = BASE_C + FAR
VMEM_LIMIT = 56 * 1024 * 1024


def cell_coords():
    ids = np.arange(CELLS)
    return [ids // 64, ids // 8 % 8, ids % 8]


def face_cells(face):
    coords = cell_coords()
    keep = coords[face // 2] == (EDGE - 1 if face % 2 else 0)
    return np.nonzero(keep)[0]


def constants():
    sel = np.zeros((3, 2, CELLS, 256), np.float32)
    spread = np.zeros((6, 128, 2 * CELLS), np.float32)
    for face in range(6):
        cells = face_cells(face)
        for j, cell in enumerate(cells):
            for kind in range(2):
                sel[face // 2, kind, cell, (face % 2) * 128 + kind * 64 + j] = 1
                spread[face, kind * 64 + j, kind * CELLS + cell] = 1
    c0, c1, c2 = cell_coords()
    group = (c0 // 2) * 16 + (c1 // 2) * 4 + c2 // 2
    rest = np.zeros((2, CELLS, 128), np.float32)
    up = np.zeros((128, 2 * CELLS), np.float32)
    for cell in range(CELLS):
        rest[0, cell, group[cell]] = 0.125
        rest[1, cell, 64 + group[cell]] = 1
        up[group[cell], cell] = 1
        up[64 + group[cell], CELLS + cell] = 1
    place = np.zeros((128, 2 * CELLS), np.float32)
    for a in range(64):
        cell = (a // 16) * 64 + (a // 4 % 4) * 8 + a % 4
        place[a, cell] = 1
        place[64 + a, CELLS + cell] = 1
    as_bf = lambda item: np.asarray(item, jnp.bfloat16)
    return (
        as_bf(sel.reshape(6, CELLS, 256)),
        as_bf(spread),
        as_bf(rest),
        as_bf(up),
        as_bf(place),
        as_bf(place.T),
    )


def dot(a, b):
    return jnp.dot(a, b, preferred_element_type=F32)


def dot_nt(a, b):
    return lax.dot_general(a, b, (((1,), (1,)), ((), ())), preferred_element_type=F32)


def inside(face, rows):
    lane = lax.broadcasted_iota(jnp.int32, (rows, CELLS), 1)
    stride = STRIDES[face // 2]
    coord = (lane // stride) % EDGE
    edge = EDGE - 1 if face % 2 else 0
    return jnp.where(coord == edge, 0.0, 1.0).astype(BF)


def toward(field, face):
    stride = STRIDES[face // 2]
    shift = CELLS - stride if face % 2 else stride
    return pltpu.roll(field, shift, 1)


def send_rows(side, count, v_ref, y_ref, sel_ref, v_rows, y_rows, out_ref):
    for dim in (2, 1, 0):
        depth = MORTON[dim]
        face = 2 * dim + side
        for i in range(depth):
            slot = jnp.clip(count - depth + i, 0, SLOTS - 1) if side else i
            v_rows[i] = v_ref[slot]
            y_rows[i] = y_ref[slot]
        cols = slice((face % 2) * 128, (face % 2) * 128 + 128)
        layers = dot(v_rows[:depth].reshape(depth * C, CELLS), sel_ref[2 * dim, :, cols])
        layers += dot(y_rows[:depth].reshape(depth * C, CELLS), sel_ref[2 * dim + 1, :, cols])
        layers = layers.astype(BF).reshape(depth, C, 128)
        if dim == 2 and side:
            out_ref[0:8] = layers[8:16]
            out_ref[8:16] = layers[0:8]
        else:
            out_ref[ROW0[dim] : ROW0[dim] + depth] = layers


def send_both(scal, v_ref, y_ref, sel_ref, v_rows, y_rows, inner_ref, outer_ref):
    count = scal[0]
    odd = scal[1]

    @pl.when(odd == 0)
    def _():
        send_rows(1, count, v_ref, y_ref, sel_ref, v_rows, y_rows, inner_ref)
        send_rows(0, count, v_ref, y_ref, sel_ref, v_rows, y_rows, outer_ref)

    @pl.when(odd == 1)
    def _():
        send_rows(0, count, v_ref, y_ref, sel_ref, v_rows, y_rows, inner_ref)
        send_rows(1, count, v_ref, y_ref, sel_ref, v_rows, y_rows, outer_ref)


def layers_kernel(scal, v_ref, y_ref, sel_ref, inner_ref, outer_ref, v_rows, y_rows):
    send_both(scal, v_ref, y_ref, sel_ref, v_rows, y_rows, inner_ref, outer_ref)


def fill_table(v_ref, y_ref, sel_ref, a_ref, b_ref, c_ref, table):
    for dim in range(3):
        layers = dot(v_ref[...].reshape(SLOTS * C, CELLS), sel_ref[2 * dim])
        layers += dot(y_ref[...].reshape(SLOTS * C, CELLS), sel_ref[2 * dim + 1])
        layers = layers.astype(BF)
        for high in range(2):
            face = 2 * dim + high
            table[face * SLOTS : (face + 1) * SLOTS] = layers[
                :, high * 128 : high * 128 + 128
            ].reshape(SLOTS, C, 128)
    table[BASE_A:BASE_B] = a_ref[...]
    table[BASE_B:BASE_C] = b_ref[...]
    table[BASE_C:ROWS] = c_ref[...]


def block_taps(start, idx, tag, v_ref, y_ref, spread_ref, table, picked, ta, tb):
    masks = [inside(face, C) for face in range(6)]
    for p in range(PB):
        ta[p, 0:C] = v_ref[start + p]
        tb[p, 0:C] = y_ref[start + p]
    for dim in range(3):
        spreads = []
        for face in (2 * dim, 2 * dim + 1):
            for p in range(PB):
                picked[p] = table[idx[(start + p) * 6 + face]]
            spreads.append(dot(picked[...].reshape(PB * C, 128), spread_ref[face]))
        low, high = 2 * dim, 2 * dim + 1
        for p in range(PB):
            field = v_ref[start + p]
            other = y_ref[start + p]
            rows = slice(p * C, (p + 1) * C)
            t_low = tag[(start + p) * 6 + low].astype(F32)
            t_high = tag[(start + p) * 6 + high].astype(F32)
            z_low = spreads[0][rows, CELLS:]
            z_high = spreads[1][rows, CELLS:]
            for k, face in enumerate((low, high)):
                ta[p, C * (face + 1) : C * (face + 2)] = (
                    toward(field, face) * masks[face] + spreads[k][rows, :CELLS].astype(BF)
                )
            tb[p, C * (high + 1) : C * (high + 2)] = toward(other, low) * masks[low] + (
                z_low * (1.0 - t_low) + z_high * t_high
            ).astype(BF)
            tb[p, C * (low + 1) : C * (low + 2)] = toward(other, high) * masks[high] + (
                z_high * (1.0 - t_high) + z_low * t_low
            ).astype(BF)


def fine_kernel(
    scal, idx, tag, dst, lead_dst, trail_dst,
    x_ref, z_ref, a_ref, b_ref, c_ref, wa_ref, wb_ref, sel_ref, spread_ref, rest_ref,
    ta_ref, tb_ref, hidden_ref, slope_ref, gm_ref, par_ref, inner_ref, outer_ref,
    xs, zs, table, picked, par, lead, trail,
):
    step = pl.program_id(0)

    @pl.when(step == 0)
    def _():
        for p in range(SLOTS):
            live = (p < scal[0]).astype(F32)
            xs[p] = (x_ref[p].astype(F32) * live).astype(BF)
            zs[p] = (z_ref[p].astype(F32) * live).astype(BF)
        fill_table(xs, zs, sel_ref, a_ref, b_ref, c_ref, table)
        par[...] = jnp.zeros_like(par)
        lead[...] = jnp.zeros_like(lead)
        trail[...] = jnp.zeros_like(trail)

    start = step * PB
    block_taps(start, idx, tag, xs, zs, spread_ref, table, picked, ta_ref, tb_ref)
    for p in range(PB):
        pre = dot(wa_ref[...], ta_ref[p])
        sigma = 1.0 / (1.0 + jnp.exp(-pre))
        hidden_ref[p] = (pre * sigma).astype(BF)
        slope_ref[p] = (sigma * (1.0 + pre * (1.0 - sigma))).astype(BF)
        gm_ref[p] = dot(wb_ref[...], tb_ref[p]).astype(BF)
    child = dot(hidden_ref[...].reshape(PB * C, CELLS), rest_ref[0])
    child += dot(gm_ref[...].reshape(PB * C, CELLS), rest_ref[1])
    child = child.astype(BF)
    for p in range(PB):
        row = child[p * C : (p + 1) * C]
        par[dst[start + p]] = row
        lead[lead_dst[start + p]] = row
        trail[trail_dst[start + p]] = row

    @pl.when(step == STEPS - 1)
    def _():
        par_ref[...] = par[: NPAR * 8]

        @pl.when(scal[1] == 0)
        def _():
            inner_ref[...] = trail[:8]
            outer_ref[...] = lead[:8]

        @pl.when(scal[1] == 1)
        def _():
            inner_ref[...] = lead[:8]
            outer_ref[...] = trail[:8]


def coarse_level(scal, par_ref, inner_ref, outer_ref, wa, wb, place_ref, unplace_ref, par, taps, up_rows, dw_ref):
    par[: NPAR * 8] = par_ref[...]
    par[NPAR * 8 :] = jnp.zeros((8, C, 128), BF)
    last = scal[2] * 8
    first_in = 1 - scal[1]

    def merge(start, got_ref):
        for o in range(8):
            par[start + o] = par[start + o] + got_ref[o]

    @pl.when(scal[1] == 0)
    def _():
        merge(0, outer_ref)
        merge(last, inner_ref)

    @pl.when(scal[1] == 1)
    def _():
        merge(0, inner_ref)
        merge(last, outer_ref)

    masks = [inside(face, C) for face in range(6)]
    shifts = [(o // 4) * 256 + (o // 2 % 2) * 32 + (o % 2) * 4 for o in range(8)]
    dw = jnp.zeros((C, 7 * C), F32)
    for q in range(NPAR):
        field = jnp.zeros((C, CELLS), F32)
        cotan = jnp.zeros((C, CELLS), F32)
        for o in range(8):
            put = dot(par[q * 8 + o], place_ref[...])
            one, two = put[:, :CELLS], put[:, CELLS:]
            if shifts[o]:
                one = pltpu.roll(one, shifts[o], 1)
                two = pltpu.roll(two, shifts[o], 1)
            field += one
            cotan += two
        field = field.astype(BF)
        taps[0:C] = field
        for face in range(6):
            taps[C * (face + 1) : C * (face + 2)] = toward(field, face) * masks[face] + field * (
                1 - masks[face]
            )
        pre = dot(wa, taps[...])
        sigma = 1.0 / (1.0 + jnp.exp(-pre))
        act = (pre * sigma).astype(BF)
        grad = (cotan * (sigma * (1.0 + pre * (1.0 - sigma)))).astype(BF)
        part = dot_nt(grad, taps[...])
        if q == 0:
            part = part * scal[3].astype(F32)
        dw += part
        taps[0:C] = grad
        for face in range(6):
            back = face ^ 1
            taps[C * (face + 1) : C * (face + 2)] = toward(grad, back) * masks[back] + grad * (
                1 - masks[face]
            )
        down = dot(wb, taps[...]).astype(BF)
        for o in range(8):
            one, two = act, down
            if shifts[o]:
                one = pltpu.roll(act, CELLS - shifts[o], 1)
                two = pltpu.roll(down, CELLS - shifts[o], 1)
            rows = dot(one, unplace_ref[:CELLS]) + dot(two, unplace_ref[CELLS:])
            up_rows[q * 8 + o] = rows.astype(BF)
    up_rows[NPAR * 8] = jnp.zeros((C, 128), BF)
    dw_ref[2 * C : 3 * C, 0 : 7 * C] = dw


def merge_kernel(
    scal, urow,
    ta_ref, tb_ref, hidden_ref, slope_ref, gm_ref, par_ref, pin_ref, pout_ref,
    wa_ref, wb_ref, place_ref, unplace_ref, up_ref, sel_ref,
    merged_ref, gpa_ref, dw_ref, inner_ref, outer_ref,
    par, taps, up_rows, picked, v_rows, y_rows,
):
    step = pl.program_id(0)

    @pl.when(step == 0)
    def _():
        dw_ref[...] = jnp.zeros_like(dw_ref)
        coarse_level(
            scal, par_ref, pin_ref, pout_ref, wa_ref[...], wb_ref[...],
            place_ref, unplace_ref, par, taps, up_rows, dw_ref,
        )

    start = step * PB
    for p in range(PB):
        picked[p] = up_rows[urow[start + p]]
    spread = dot(picked[...].reshape(PB * C, 128), up_ref[...])
    dw_in = jnp.zeros((C, 7 * C), F32)
    dw_out = jnp.zeros((C, 7 * C), F32)
    for p in range(PB):
        rows = slice(p * C, (p + 1) * C)
        merged = (hidden_ref[p].astype(F32) + spread[rows, :CELLS]).astype(BF)
        grad = gm_ref[p].astype(F32) + spread[rows, CELLS:] * 0.125
        gpa = (grad * slope_ref[p].astype(F32)).astype(BF)
        merged_ref[start + p] = merged
        gpa_ref[start + p] = gpa
        dw_in += dot_nt(gpa, ta_ref[p])
        dw_out += dot_nt(merged, tb_ref[p])
    dw_ref[0:C, 0 : 7 * C] += dw_in
    dw_ref[C : 2 * C, 0 : 7 * C] += dw_out

    @pl.when(step == STEPS - 1)
    def _():
        send_both(scal, merged_ref, gpa_ref, sel_ref, v_rows, y_rows, inner_ref, outer_ref)


def final_kernel(
    scal, idx, tag,
    v_ref, y_ref, x_ref, z_ref, a_ref, b_ref, c_ref, wa_ref, wb_ref, sel_ref, spread_ref,
    out_ref, gs_ref,
    table, picked, ta, tb,
):
    step = pl.program_id(0)

    @pl.when(step == 0)
    def _():
        fill_table(v_ref, y_ref, sel_ref, a_ref, b_ref, c_ref, table)

    start = step * PB
    block_taps(start, idx, tag, v_ref, y_ref, spread_ref, table, picked, ta, tb)
    for p in range(PB):
        live = (start + p < scal[0]).astype(F32)
        out_ref[p] = (x_ref[p].astype(F32) * live + dot(wa_ref[...], ta[p])).astype(BF)
        gs_ref[p] = (z_ref[p].astype(F32) * live + dot(wb_ref[...], tb[p])).astype(BF)


SMEM = functools.partial(pl.BlockSpec, memory_space=pltpu.SMEM)


def whole(shape):
    zeros = (0,) * len(shape)
    return pl.BlockSpec(shape, lambda i: zeros)


def blocked(shape):
    rest = (0,) * (len(shape) - 1)
    return pl.BlockSpec((PB,) + tuple(shape[1:]), lambda i: (i,) + rest)


def params():
    return pltpu.CompilerParams(
        dimension_semantics=("arbitrary",), vmem_limit_bytes=VMEM_LIMIT
    )


def shape_of(shape, dtype=BF):
    return jax.ShapeDtypeStruct(shape, dtype)


def pairs(kind, devices):
    if kind == "inner":
        links = [(2 * c, 2 * c + 1) for c in range(devices // 2)]
    else:
        links = [(2 * c + 1, 2 * c + 2) for c in range(devices // 2 - 1)]
    return links + [(b, a) for a, b in links]


def trade(block, kind):
    return lax.ppermute(block, "patch", pairs(kind, lax.axis_size("patch")))


def relay(inner, outer):
    got_a = trade(inner, "inner")
    got_b = trade(jnp.concatenate([outer, got_a[:FAR]], axis=0), "outer")
    got_c = trade(got_b[:FAR], "inner")
    return got_a, got_b, got_c


def sum_over_devices(block):
    devices = lax.axis_size("patch")
    for mask in (1, 2, 6, 8, 24, 32, 96):
        block = block + lax.ppermute(block, "patch", [(i, i ^ mask) for i in range(devices)])
    return block


def on_device(
    fine_state, weight_in, weight_out, weight_coarse, cotangent,
    owner_count, neighbour, level_tag, octant,
):
    rank = lax.axis_index("patch")
    devices = lax.axis_size("patch")
    sel, spread, rest, up, place, unplace = [jnp.asarray(item) for item in constants()]

    odd = rank % 2
    ranks = jnp.arange(devices)
    first = jnp.sum(jnp.where(ranks < rank, owner_count, 0))
    count = jnp.sum(jnp.where(ranks == rank, owner_count, 0))
    count_1 = jnp.sum(jnp.where(ranks == rank - 1, owner_count, 0))
    count_2 = jnp.sum(jnp.where(ranks == rank - 2, owner_count, 0))
    stop = first + count
    last = jnp.where(stop % 8 != 0, stop // 8 - first // 8, NPAR)
    scal = jnp.stack([count, odd, last, jnp.where(first % 8 == 0, 1, 0)]).astype(jnp.int32)

    slots = jnp.arange(SLOTS)
    live = slots < count
    dst = jnp.where(live, (first % 8 + slots) // 8 * 8 + octant, NPAR * 8)
    lead = live & (slots < (-first) % 8)
    trail = live & (slots >= count - stop % 8)
    lead_dst = jnp.where(lead, octant, 8)
    trail_dst = jnp.where(trail, octant, 8)

    face = jnp.arange(6)[None, :]
    dim = face // 2
    depth = jnp.where(dim == 0, MORTON[0], jnp.where(dim == 1, MORTON[1], MORTON[2]))
    row0 = jnp.where(dim == 0, ROW0[0], jnp.where(dim == 1, ROW0[1], ROW0[2]))
    away = neighbour // SLOTS - rank
    slot = neighbour % SLOTS
    opposite = face + 1 - 2 * (face % 2)
    here = opposite * SLOTS + slot
    from_left = slot - (count_1 - depth)
    near_left = jnp.where(dim == 2, (from_left + 8) % 16, row0 + from_left)
    far_left = slot - (count_2 - 8)
    near_right = row0 + slot
    far_right = slot
    inner_is_left = odd == 1
    near_base_left = jnp.where(inner_is_left, BASE_A, BASE_B)
    near_base_right = jnp.where(inner_is_left, BASE_B, BASE_A)
    far_base_left = jnp.where(inner_is_left, BASE_C, BASE_B + NEAR)
    far_base_right = jnp.where(inner_is_left, BASE_B + NEAR, BASE_C)
    index = jnp.where(away == 0, here, 0)
    index = jnp.where(away == -1, near_base_left + near_left, index)
    index = jnp.where(away == -2, far_base_left + far_left, index)
    index = jnp.where(away == 1, near_base_right + near_right, index)
    index = jnp.where(away == 2, far_base_right + far_right, index)
    index = jnp.where(level_tag == 1, face * SLOTS + slots[:, None], index)
    index = jnp.clip(index, 0, ROWS - 1).astype(jnp.int32).reshape(-1)
    tags = level_tag.reshape(-1)

    def forward_matrix(weight):
        return weight.transpose(2, 0, 1).reshape(C, 7 * C)

    def backward_matrix(weight):
        return weight.transpose(1, 0, 2).reshape(C, 7 * C)

    field = (SLOTS, C, CELLS)
    stack = (SLOTS, 7 * C, CELLS)
    near = (NEAR, C, 128)
    near_far = (NEAR + FAR, C, 128)
    far = (FAR, C, 128)
    mat = (C, 7 * C)
    rows_scratch = pltpu.VMEM((16, C, CELLS), BF)

    inner, outer = pl.pallas_call(
        layers_kernel,
        grid=(1,),
        in_specs=[SMEM(), whole(field), whole(field), whole(sel.shape)],
        out_specs=[whole(near), whole(near)],
        out_shape=[shape_of(near), shape_of(near)],
        scratch_shapes=[rows_scratch, rows_scratch],
        compiler_params=params(),
        name="face_rows",
    )(scal, fine_state, cotangent, sel)
    got_a, got_b, got_c = relay(inner, outer)

    taps_a, taps_b, hidden, slope, grad_merged, par, pin, pout = pl.pallas_call(
        fine_kernel,
        grid=(STEPS,),
        in_specs=[SMEM()] * 6
        + [whole(field), whole(field), whole(near), whole(near_far), whole(far)]
        + [whole(mat), whole(mat), whole(sel.shape), whole(spread.shape), whole(rest.shape)],
        out_specs=[blocked(stack), blocked(stack), blocked(field), blocked(field), blocked(field)]
        + [whole((NPAR * 8, C, 128)), whole(far), whole(far)],
        out_shape=[shape_of(stack), shape_of(stack), shape_of(field), shape_of(field)]
        + [shape_of(field), shape_of((NPAR * 8, C, 128)), shape_of(far), shape_of(far)],
        scratch_shapes=[
            pltpu.VMEM(field, BF),
            pltpu.VMEM(field, BF),
            pltpu.VMEM((ROWS, C, 128), BF),
            pltpu.VMEM((PB, C, 128), BF),
            pltpu.VMEM((NPAR * 8 + 8, C, 128), BF),
            pltpu.VMEM((16, C, 128), BF),
            pltpu.VMEM((16, C, 128), BF),
        ],
        compiler_params=params(),
        name="fine_level",
    )(
        scal, index, tags, dst.astype(jnp.int32), lead_dst.astype(jnp.int32),
        trail_dst.astype(jnp.int32), fine_state, cotangent, got_a, got_b, got_c,
        forward_matrix(weight_in), backward_matrix(weight_out), sel, spread, rest,
    )
    child_out = trade(pout, "outer")
    child_in = trade(pin, "inner")

    dw_shape = (3 * C, 256)
    merged, grad_pre, dw, inner, outer = pl.pallas_call(
        merge_kernel,
        grid=(STEPS,),
        in_specs=[SMEM()] * 2
        + [blocked(stack), blocked(stack), blocked(field), blocked(field), blocked(field)]
        + [whole((NPAR * 8, C, 128)), whole(far), whole(far), whole(mat), whole(mat)]
        + [whole(place.shape), whole(unplace.shape), whole(up.shape), whole(sel.shape)],
        out_specs=[whole(field), whole(field), whole(dw_shape), whole(near), whole(near)],
        out_shape=[shape_of(field), shape_of(field), shape_of(dw_shape, F32)]
        + [shape_of(near), shape_of(near)],
        scratch_shapes=[
            pltpu.VMEM((NPAR * 8 + 8, C, 128), BF),
            pltpu.VMEM((7 * C, CELLS), BF),
            pltpu.VMEM((NPAR * 8 + 8, C, 128), BF),
            pltpu.VMEM((PB, C, 128), BF),
            rows_scratch,
            rows_scratch,
        ],
        compiler_params=params(),
        name="coarse_and_merge",
    )(
        scal, dst.astype(jnp.int32), taps_a, taps_b, hidden, slope, grad_merged, par,
        child_in, child_out, forward_matrix(weight_coarse), backward_matrix(weight_coarse),
        place, unplace, up, sel,
    )
    got_a, got_b, got_c = relay(inner, outer)
    total = sum_over_devices(dw)

    output, grad_state = pl.pallas_call(
        final_kernel,
        grid=(STEPS,),
        in_specs=[SMEM()] * 3
        + [whole(field), whole(field), blocked(field), blocked(field)]
        + [whole(near), whole(near_far), whole(far), whole(mat), whole(mat)]
        + [whole(sel.shape), whole(spread.shape)],
        out_specs=[blocked(field), blocked(field)],
        out_shape=[shape_of(field), shape_of(field)],
        scratch_shapes=[
            pltpu.VMEM((ROWS, C, 128), BF),
            pltpu.VMEM((PB, C, 128), BF),
            pltpu.VMEM((PB, 7 * C, CELLS), BF),
            pltpu.VMEM((PB, 7 * C, CELLS), BF),
        ],
        compiler_params=params(),
        name="last_level",
    )(
        scal, index, tags, merged, grad_pre, fine_state, cotangent, got_a, got_b, got_c,
        forward_matrix(weight_out), backward_matrix(weight_in), sel, spread,
    )

    scale = 1.0 / math.sqrt(float(devices * SLOTS * CELLS))
    total = total[:, : 7 * C].reshape(3, C, 7, C) * scale
    return (
        output,
        grad_state,
        total[0].transpose(1, 2, 0),
        total[1].transpose(1, 0, 2),
        total[2].transpose(1, 2, 0),
    )


def solution(mesh):
    in_specs = (
        P("patch", None, None),
        P(),
        P(),
        P(),
        P("patch", None, None),
        P(),
        P("patch", None),
        P("patch", None),
        P("patch"),
    )
    out_specs = (P("patch", None, None), P("patch", None, None), P(), P(), P())
    return jax.shard_map(
        on_device, mesh=mesh, in_specs=in_specs, out_specs=out_specs, check_vma=False
    )
```

```python
import functools
import math

import numpy as np
import jax
import jax.numpy as jnp
from jax import lax
from jax.experimental import pallas as pl
from jax.experimental.pallas import tpu as pltpu
from jax.sharding import PartitionSpec as P

BF = jnp.bfloat16
F32 = jnp.float32
EDGE = 8
CELLS = 512
SLOTS = 32
C = 32
PB = 8
STEPS = SLOTS // PB
NPAR = 5
STRIDES = (64, 8, 1)
MORTON = (3, 8, 16)
ROW0 = (24, 16, 0)
NEAR = 27
FAR = 8
BASE_A = 6 * SLOTS
BASE_B = BASE_A + NEAR
BASE_C = BASE_B + NEAR + FAR
ROWS = BASE_C + FAR
VMEM_LIMIT = 56 * 1024 * 1024
IDX, TAG, DST, LEAD, TRAIL, SCAL = 0, 192, 384, 416, 448, 480
N_COUNT, N_ODD, N_LAST, N_OWNED = SCAL, SCAL + 1, SCAL + 2, SCAL + 3
META = 512
IN_F, OUT_B, OUT_F, IN_B, CO_F, CO_B = range(6)


def cell_coords():
    ids = np.arange(CELLS)
    return [ids // 64, ids // 8 % 8, ids % 8]


def face_cells(face):
    coords = cell_coords()
    keep = coords[face // 2] == (EDGE - 1 if face % 2 else 0)
    return np.nonzero(keep)[0]


def constants():
    sel = np.zeros((3, 2, CELLS, 256), np.float32)
    spread = np.zeros((2, 256, 2 * CELLS), np.float32)
    for face in range(6):
        for j, cell in enumerate(face_cells(face)):
            for kind in range(2):
                col = (face % 2) * 128 + kind * 64 + j
                sel[face // 2, kind, cell, col] = 1
                if face >= 2:
                    spread[face // 2 - 1, col, kind * CELLS + cell] = 1
    c0, c1, c2 = cell_coords()
    group = (c0 // 2) * 16 + (c1 // 2) * 4 + c2 // 2
    rest = np.zeros((2, CELLS, 128), np.float32)
    up = np.zeros((128, 2 * CELLS), np.float32)
    for cell in range(CELLS):
        rest[0, cell, group[cell]] = 0.125
        rest[1, cell, 64 + group[cell]] = 1
        up[group[cell], cell] = 1
        up[64 + group[cell], CELLS + cell] = 1
    place = np.zeros((256, 2 * CELLS), np.float32)
    for o2 in range(2):
        for a in range(64):
            cell = (a // 16) * 64 + (a // 4 % 4) * 8 + a % 4 + 4 * o2
            place[128 * o2 + a, cell] = 1
            place[128 * o2 + 64 + a, CELLS + cell] = 1
    as_bf = lambda item: np.asarray(item, jnp.bfloat16)
    return (
        as_bf(sel.reshape(6, CELLS, 256)),
        as_bf(spread),
        as_bf(rest),
        as_bf(up),
        as_bf(place),
    )


def dot(a, b):
    return jnp.dot(a, b, preferred_element_type=F32)


def dot_nt(a, b):
    return lax.dot_general(a, b, (((1,), (1,)), ((), ())), preferred_element_type=F32)


def coord_of(dim):
    lane = lax.broadcasted_iota(jnp.int32, (16, CELLS), 1)
    return (lane // STRIDES[dim]) % EDGE


def on_face(face):
    edge = EDGE - 1 if face % 2 else 0
    return jnp.where(coord_of(face // 2) == edge, 1.0, 0.0)


def halves(field):
    return field.reshape(field.shape[0] // 16, 16, CELLS)


def times(field, mask):
    return (halves(field) * mask[None]).reshape(field.shape)


def toward(field, face):
    stride = STRIDES[face // 2]
    shift = CELLS - stride if face % 2 else stride
    return pltpu.roll(field, shift, 1)


def send_rows(count, odd, v_ref, y_ref, sel_ref, v_rows, y_rows, sides, inner_ref, outer_ref):
    for side in range(2):
        for dim in (2, 1, 0):
            depth = MORTON[dim]
            for i in range(depth):
                slot = jnp.clip(count - depth + i, 0, SLOTS - 1) if side else i
                v_rows[i] = v_ref[slot]
                y_rows[i] = y_ref[slot]
            cols = slice(side * 128, side * 128 + 128)
            layers = dot(v_rows[:depth].reshape(depth * C, CELLS), sel_ref[2 * dim, :, cols])
            layers += dot(y_rows[:depth].reshape(depth * C, CELLS), sel_ref[2 * dim + 1, :, cols])
            layers = layers.astype(BF).reshape(depth, C, 128)
            if dim == 2 and side:
                sides[side, 0:8] = layers[8:16]
                sides[side, 8:16] = layers[0:8]
            else:
                sides[side, ROW0[dim] : ROW0[dim] + depth] = layers
    inner_ref[...] = sides[1 - odd]
    outer_ref[...] = sides[odd]


def layers_kernel(counts, v_ref, y_ref, sel_ref, inner_ref, outer_ref, v_rows, y_rows, sides):
    rank = lax.axis_index("patch")
    send_rows(
        counts[rank], rank % 2, v_ref, y_ref, sel_ref, v_rows, y_rows, sides, inner_ref, outer_ref
    )


def fill_table(v_ref, y_ref, sel_ref, table):
    for dim in range(3):
        layers = dot(v_ref[...].reshape(SLOTS * C, CELLS), sel_ref[2 * dim])
        layers += dot(y_ref[...].reshape(SLOTS * C, CELLS), sel_ref[2 * dim + 1])
        layers = layers.astype(BF)
        for high in range(2):
            face = 2 * dim + high
            table[face * SLOTS : (face + 1) * SLOTS] = layers[
                :, high * 128 : high * 128 + 128
            ].reshape(SLOTS, C, 128)


def prepare_kernel(
    counts, neighbour, level_tag, octant,
    got_ref, x_ref, z_ref, sel_ref, w_in, w_out, w_co,
    meta, xs, zs, mats, table,
):
    rank = lax.axis_index("patch")
    odd = rank % 2

    def count_at(device):
        here = counts[jnp.clip(device, 0, counts.shape[0] - 1)]
        return jnp.where(device < 0, 0, here)

    first = lax.fori_loop(0, rank, lambda d, s: s + counts[d], jnp.int32(0))
    count = count_at(rank)
    count_1 = count_at(rank - 1)
    count_2 = count_at(rank - 2)
    stop = first + count
    meta[N_COUNT] = count
    meta[N_ODD] = odd
    meta[N_LAST] = jnp.where(stop % 8 != 0, stop // 8 - first // 8, NPAR)
    meta[N_OWNED] = jnp.where(first % 8 == 0, 1, 0)
    near_left = jnp.where(odd == 1, BASE_A, BASE_B)
    near_right = jnp.where(odd == 1, BASE_B, BASE_A)
    far_left = jnp.where(odd == 1, BASE_C, BASE_B + NEAR)
    far_right = jnp.where(odd == 1, BASE_B + NEAR, BASE_C)
    lead_count = (8 - first % 8) % 8

    def per_slot(p, carry):
        live = p < count
        parent = (first % 8 + p) // 8
        o = jnp.clip(octant[p], 0, 7)
        meta[DST + p] = jnp.where(live, parent * 8 + o, NPAR * 8)
        meta[LEAD + p] = jnp.where(live & (p < lead_count), o, 8)
        meta[TRAIL + p] = jnp.where(live & (p >= count - stop % 8), o, 8)
        for face in range(6):
            dim = face // 2
            depth = MORTON[dim]
            other = neighbour[face, p]
            tag = level_tag[face, p]
            away = other // SLOTS - rank
            slot = other % SLOTS
            if face % 2:
                near = near_right + ROW0[dim] + slot
                far = far_right + slot
            else:
                back = slot - (count_1 - depth)
                near = near_left + ((back + 8) % 16 if dim == 2 else ROW0[dim] + back)
                far = far_left + slot - (count_2 - 8)
            row = jnp.where(away == 0, (face ^ 1) * SLOTS + slot, near)
            row = jnp.where(jnp.abs(away) == 2, far, row)
            row = jnp.where(tag == 1, face * SLOTS + p, row)
            meta[IDX + face * SLOTS + p] = jnp.clip(row, 0, ROWS - 1)
            meta[TAG + face * SLOTS + p] = tag
        return carry

    lax.fori_loop(0, SLOTS, per_slot, 0)
    for k, (weight, turned) in enumerate(
        ((w_in, True), (w_out, False), (w_out, True), (w_in, False), (w_co, True), (w_co, False))
    ):
        for f in range(7):
            one = weight[f].astype(F32)
            mats[k, :, f * C : (f + 1) * C] = (one.T if turned else one).astype(BF)
    for p in range(SLOTS):
        live = (p < count).astype(F32)
        xs[p] = (x_ref[p].astype(F32) * live).astype(BF)
        zs[p] = (z_ref[p].astype(F32) * live).astype(BF)
    fill_table(xs, zs, sel_ref, table)
    table[BASE_A:BASE_B] = got_ref[...]


def table_kernel(v_ref, y_ref, sel_ref, table):
    fill_table(v_ref, y_ref, sel_ref, table)


def join_table(parts, coef, table):
    start = 0
    for part in parts:
        size = part.shape[0]
        table[start : start + size] = part[...]
        start += size
    for dim in range(3):
        low, high = on_face(2 * dim), on_face(2 * dim + 1)
        for t_low in range(2):
            for t_high in range(2):
                row = dim * 4 + t_low * 2 + t_high
                coef[row, 0] = (low * (1 - t_low) + high * t_high).astype(BF)
                coef[row, 1] = (high * (1 - t_high) + low * t_low).astype(BF)


def block_taps(start, meta, v_ref, y_ref, spread_ref, table, coef, picked, ta, tb):
    for dim in range(3):
        low, high = 2 * dim, 2 * dim + 1
        edges = [on_face(low), on_face(high)]
        inside = [(1.0 - edge).astype(BF) for edge in edges]
        edges = [edge.astype(BF) for edge in edges]
        if dim:
            for p in range(PB):
                picked[p, :, 0:128] = table[meta[IDX + low * SLOTS + start + p]]
                picked[p, :, 128:256] = table[meta[IDX + high * SLOTS + start + p]]
            spread = dot(picked[...].reshape(PB * C, 256), spread_ref[dim - 1]).astype(BF)
        for p in range(PB):
            if dim:
                rows = slice(p * C, (p + 1) * C)
                v_edge = spread[rows, :CELLS]
                y_edge = spread[rows, CELLS:]
            else:
                r_low = table[meta[IDX + low * SLOTS + start + p]]
                r_high = table[meta[IDX + high * SLOTS + start + p]]
                blank = jnp.zeros((C, 256), BF)
                v_edge = jnp.concatenate([r_low, blank, pltpu.roll(r_high, 64, 1)], axis=1)
                y_edge = jnp.concatenate([pltpu.roll(r_low, 64, 1), blank, r_high], axis=1)
            field = v_ref[p]
            other = y_ref[p]
            if dim == 0:
                ta[p, 0:C] = field
                tb[p, 0:C] = other
            row = (
                dim * 4
                + meta[TAG + low * SLOTS + start + p] * 2
                + meta[TAG + high * SLOTS + start + p]
            )
            for k, face in enumerate((low, high)):
                ta[p, C * (face + 1) : C * (face + 2)] = times(
                    toward(field, face), inside[k]
                ) + times(v_edge, edges[k])
                back = face ^ 1
                tb[p, C * (back + 1) : C * (back + 2)] = times(
                    toward(other, face), inside[k]
                ) + times(y_edge, coef[row, k])


def silu_pair(pre):
    sigma = 1.0 / (1.0 + jnp.exp(-pre))
    return pre * sigma, sigma * (1.0 + pre * (1.0 - sigma))


def fine_kernel(
    meta, xs, zs, t_ref, b_ref, c_ref, mats, spread_ref, rest_ref,
    ta_ref, tb_ref, hidden_ref, slope_ref, gm_ref, par_ref, inner_ref, outer_ref,
    table, coef, picked, par, ends,
):
    step = pl.program_id(0)

    @pl.when(step == 0)
    def _():
        join_table((t_ref, b_ref, c_ref), coef, table)
        par[...] = jnp.zeros_like(par)
        ends[...] = jnp.zeros_like(ends)

    start = step * PB
    block_taps(start, meta, xs, zs, spread_ref, table, coef, picked, ta_ref, tb_ref)
    for p in range(PB):
        hidden, slope = silu_pair(dot(mats[IN_F], ta_ref[p]))
        hidden_ref[p] = hidden.astype(BF)
        slope_ref[p] = slope.astype(BF)
        gm_ref[p] = dot(mats[OUT_B], tb_ref[p]).astype(BF)
    child = dot(hidden_ref[...].reshape(PB * C, CELLS), rest_ref[0])
    child += dot(gm_ref[...].reshape(PB * C, CELLS), rest_ref[1])
    child = child.astype(BF)
    for p in range(PB):
        row = child[p * C : (p + 1) * C]
        par[meta[DST + start + p]] = row
        ends[0, meta[LEAD + start + p]] = row
        ends[1, meta[TRAIL + start + p]] = row

    @pl.when(step == STEPS - 1)
    def _():
        par_ref[...] = par[: NPAR * 8]
        odd = meta[N_ODD]
        inner_ref[...] = ends[1 - odd, 0:8]
        outer_ref[...] = ends[odd, 0:8]


def coarse_level(meta, par_ref, inner_ref, outer_ref, wa, wb, place_ref, par, taps, up_rows, dw_ref):
    par[: NPAR * 8] = par_ref[...]
    par[NPAR * 8 :] = jnp.zeros((8, C, 128), BF)
    last = meta[N_LAST] * 8
    odd = meta[N_ODD]
    inner_at = jnp.where(odd == 1, 0, last)
    outer_at = jnp.where(odd == 1, last, 0)
    for o in range(8):
        par[inner_at + o] = par[inner_at + o] + inner_ref[o]
    for o in range(8):
        par[outer_at + o] = par[outer_at + o] + outer_ref[o]

    rows = NPAR * C
    both = jnp.zeros((rows, 2 * CELLS), BF)
    for o in range(0, 8, 2):
        lhs = jnp.concatenate(
            [
                jnp.concatenate([par[q * 8 + o], par[q * 8 + o + 1]], axis=1)
                for q in range(NPAR)
            ],
            axis=0,
        )
        put = dot(lhs, place_ref[...]).astype(BF)
        shift = (o // 4) * 256 + (o // 2 % 2) * 32
        if shift:
            put = jnp.concatenate(
                [
                    pltpu.roll(put[:, :CELLS], shift, 1),
                    pltpu.roll(put[:, CELLS:], shift, 1),
                ],
                axis=1,
            )
        both += put
    field = both[:, :CELLS]
    cotan = both[:, CELLS:].astype(F32)
    edges = [on_face(face).astype(BF) for face in range(6)]
    inside = [(1.0 - on_face(face)).astype(BF) for face in range(6)]

    def store(face, value):
        taps[:, C * face : C * (face + 1)] = value.reshape(NPAR, C, CELLS)

    store(0, field)
    for face in range(6):
        store(face + 1, times(toward(field, face), inside[face]) + times(field, edges[face]))
    pre = jnp.concatenate([dot(wa, taps[q]) for q in range(NPAR)], axis=0)
    act, slope = silu_pair(pre)
    act = act.astype(BF)
    grad = (cotan * slope).astype(BF)
    dw = jnp.zeros((7 * C, C), F32)
    for q in range(NPAR):
        part = dot_nt(taps[q], grad[q * C : (q + 1) * C])
        if q == 0:
            part = part * meta[N_OWNED].astype(F32)
        dw += part
    store(0, grad)
    for face in range(6):
        back = face ^ 1
        store(face + 1, times(toward(grad, back), inside[back]) + times(grad, edges[face]))
    down = jnp.concatenate([dot(wb, taps[q]) for q in range(NPAR)], axis=0).astype(BF)
    for o in range(0, 8, 2):
        one, two = act, down
        shift = (o // 4) * 256 + (o // 2 % 2) * 32
        if shift:
            one = pltpu.roll(act, CELLS - shift, 1)
            two = pltpu.roll(down, CELLS - shift, 1)
        got = dot_nt(one, place_ref[:, :CELLS]) + dot_nt(two, place_ref[:, CELLS:])
        got = got.astype(BF)
        for q in range(NPAR):
            up_rows[q * 8 + o] = got[q * C : (q + 1) * C, :128]
            up_rows[q * 8 + o + 1] = got[q * C : (q + 1) * C, 128:]
    up_rows[NPAR * 8] = jnp.zeros((C, 128), BF)
    dw_ref[:, 2 * C : 3 * C] = dw


def merge_kernel(
    meta,
    ta_ref, tb_ref, hidden_ref, slope_ref, gm_ref, par_ref, pin_ref, pout_ref,
    mats, place_ref, up_ref, sel_ref,
    merged_ref, gpa_ref, dw_ref, inner_ref, outer_ref,
    par, taps, up_rows, picked, v_rows, y_rows, sides,
):
    step = pl.program_id(0)

    @pl.when(step == 0)
    def _():
        dw_ref[...] = jnp.zeros_like(dw_ref)
        coarse_level(
            meta, par_ref, pin_ref, pout_ref, mats[CO_F], mats[CO_B],
            place_ref, par, taps, up_rows, dw_ref,
        )

    start = step * PB
    for p in range(PB):
        picked[p] = up_rows[meta[DST + start + p]]
    spread = dot(picked[...].reshape(PB * C, 128), up_ref[...])
    dw_in = jnp.zeros((7 * C, C), F32)
    dw_out = jnp.zeros((7 * C, C), F32)
    for p in range(PB):
        rows = slice(p * C, (p + 1) * C)
        merged = (hidden_ref[p].astype(F32) + spread[rows, :CELLS]).astype(BF)
        grad = gm_ref[p].astype(F32) + spread[rows, CELLS:] * 0.125
        gpa = (grad * slope_ref[p].astype(F32)).astype(BF)
        merged_ref[start + p] = merged
        gpa_ref[start + p] = gpa
        dw_in += dot_nt(ta_ref[p], gpa)
        dw_out += dot_nt(tb_ref[p], merged)
    dw_ref[:, 0:C] += dw_in
    dw_ref[:, C : 2 * C] += dw_out

    @pl.when(step == STEPS - 1)
    def _():
        send_rows(
            meta[N_COUNT], meta[N_ODD], merged_ref, gpa_ref, sel_ref,
            v_rows, y_rows, sides, inner_ref, outer_ref,
        )


def final_kernel(
    meta, v_ref, y_ref, xs, zs, t_ref, a_ref, b_ref, c_ref, mats, spread_ref,
    out_ref, gs_ref,
    table, coef, picked, ta, tb,
):
    step = pl.program_id(0)

    @pl.when(step == 0)
    def _():
        join_table((t_ref, a_ref, b_ref, c_ref), coef, table)

    start = step * PB
    block_taps(start, meta, v_ref, y_ref, spread_ref, table, coef, picked, ta, tb)
    for p in range(PB):
        out_ref[p] = (xs[p].astype(F32) + dot(mats[OUT_F], ta[p])).astype(BF)
        gs_ref[p] = (zs[p].astype(F32) + dot(mats[IN_B], tb[p])).astype(BF)


def weights_kernel(scale, parts_ref, in_ref, out_ref, co_ref):
    total = parts_ref[...] * scale
    for f in range(7):
        rows = slice(f * C, (f + 1) * C)
        in_ref[f] = total[rows, 0:C]
        out_ref[f] = total[rows, C : 2 * C].T
        co_ref[f] = total[rows, 2 * C : 3 * C]


SMEM = functools.partial(pl.BlockSpec, memory_space=pltpu.SMEM)


def whole(shape):
    zeros = (0,) * len(shape)
    return pl.BlockSpec(shape, lambda i: zeros)


def blocked(shape):
    rest = (0,) * (len(shape) - 1)
    return pl.BlockSpec((PB,) + tuple(shape[1:]), lambda i: (i,) + rest)


def params():
    return pltpu.CompilerParams(
        dimension_semantics=("arbitrary",), vmem_limit_bytes=VMEM_LIMIT
    )


def shape_of(shape, dtype=BF):
    return jax.ShapeDtypeStruct(shape, dtype)


def cost(micros):
    return pl.CostEstimate(
        flops=int(micros * 1e6), bytes_accessed=int(micros * 3.0e6), transcendentals=0
    )


def pairs(kind, devices):
    if kind == "inner":
        links = [(2 * c, 2 * c + 1) for c in range(devices // 2)]
    else:
        links = [(2 * c + 1, 2 * c + 2) for c in range(devices // 2 - 1)]
    return links + [(b, a) for a, b in links]


def trade(block, kind):
    return lax.ppermute(block, "patch", pairs(kind, lax.axis_size("patch")))


def relay_out(outer, got_a):
    return trade(jnp.concatenate([outer, got_a[:FAR]], axis=0), "outer")


def relay_in(got_b, first):
    got_b, first = lax.optimization_barrier((got_b, first))
    return trade(got_b[:FAR], "inner"), first


def sum_over_devices(block):
    devices = lax.axis_size("patch")
    for mask in (1, 2, 6, 8, 24, 32, 96):
        block = block + lax.ppermute(block, "patch", [(i, i ^ mask) for i in range(devices)])
    return block


def on_device(
    fine_state, weight_in, weight_out, weight_coarse, cotangent,
    owner_count, neighbour, level_tag, octant,
):
    devices = lax.axis_size("patch")
    sel, spread, rest, up, place = [jnp.asarray(item) for item in constants()]

    field = (SLOTS, C, CELLS)
    stack = (SLOTS, 7 * C, CELLS)
    near = (NEAR, C, 128)
    near_far = (NEAR + FAR, C, 128)
    far = (FAR, C, 128)
    mats_shape = (6, C, 7 * C)
    first_part = (BASE_B, C, 128)
    local_part = (BASE_A, C, 128)
    rows_scratch = [pltpu.VMEM((16, C, CELLS), BF)] * 2 + [pltpu.VMEM((2, NEAR, C, 128), BF)]
    tap_scratch = [
        pltpu.VMEM((ROWS, C, 128), BF),
        pltpu.VMEM((12, 2, 16, CELLS), BF),
        pltpu.VMEM((PB, C, 256), BF),
    ]

    inner, outer = pl.pallas_call(
        layers_kernel,
        grid=(1,),
        in_specs=[SMEM(), whole(field), whole(field), whole(sel.shape)],
        out_specs=[whole(near), whole(near)],
        out_shape=[shape_of(near), shape_of(near)],
        scratch_shapes=rows_scratch,
        compiler_params=params(),
        cost_estimate=cost(4),
        name="face_rows",
    )(owner_count, fine_state, cotangent, sel)
    got_a = trade(inner, "inner")
    got_b = relay_out(outer, got_a)

    meta, xs, zs, mats, table = pl.pallas_call(
        prepare_kernel,
        grid=(1,),
        in_specs=[SMEM()] * 4
        + [whole(near), whole(field), whole(field), whole(sel.shape)]
        + [whole(weight_in.shape)] * 3,
        out_specs=[SMEM(), whole(field), whole(field), whole(mats_shape), whole(first_part)],
        out_shape=[shape_of((META,), jnp.int32), shape_of(field), shape_of(field)]
        + [shape_of(mats_shape), shape_of(first_part)],
        compiler_params=params(),
        cost_estimate=cost(6),
        name="prepare",
    )(
        owner_count, neighbour.T, level_tag.T, octant, got_a, fine_state, cotangent, sel,
        weight_in, weight_out, weight_coarse,
    )
    got_c, meta = relay_in(got_b, meta)

    taps_a, taps_b, hidden, slope, grad_merged, par, pin, pout = pl.pallas_call(
        fine_kernel,
        grid=(STEPS,),
        in_specs=[SMEM(), blocked(field), blocked(field)]
        + [whole(first_part), whole(near_far), whole(far), whole(mats_shape)]
        + [whole(spread.shape), whole(rest.shape)],
        out_specs=[blocked(stack), blocked(stack), blocked(field), blocked(field), blocked(field)]
        + [whole((NPAR * 8, C, 128)), whole(far), whole(far)],
        out_shape=[shape_of(stack), shape_of(stack), shape_of(field), shape_of(field)]
        + [shape_of(field), shape_of((NPAR * 8, C, 128)), shape_of(far), shape_of(far)],
        scratch_shapes=tap_scratch
        + [pltpu.VMEM((NPAR * 8 + 8, C, 128), BF), pltpu.VMEM((2, 16, C, 128), BF)],
        compiler_params=params(),
        cost_estimate=cost(12),
        name="fine_level",
    )(meta, xs, zs, table, got_b, got_c, mats, spread, rest)
    child_out = trade(pout, "outer")
    child_in = trade(pin, "inner")

    dw_shape = (7 * C, 128)
    merged, grad_pre, dw, inner, outer = pl.pallas_call(
        merge_kernel,
        grid=(STEPS,),
        in_specs=[SMEM()]
        + [blocked(stack), blocked(stack), blocked(field), blocked(field), blocked(field)]
        + [whole((NPAR * 8, C, 128)), whole(far), whole(far), whole(mats_shape)]
        + [whole(place.shape), whole(up.shape), whole(sel.shape)],
        out_specs=[whole(field), whole(field), whole(dw_shape), whole(near), whole(near)],
        out_shape=[shape_of(field), shape_of(field), shape_of(dw_shape, F32)]
        + [shape_of(near), shape_of(near)],
        scratch_shapes=[
            pltpu.VMEM((NPAR * 8 + 8, C, 128), BF),
            pltpu.VMEM((NPAR, 7 * C, CELLS), BF),
            pltpu.VMEM((NPAR * 8 + 8, C, 128), BF),
            pltpu.VMEM((PB, C, 128), BF),
        ]
        + rows_scratch,
        compiler_params=params(),
        cost_estimate=cost(14),
        name="coarse_and_merge",
    )(
        meta, taps_a, taps_b, hidden, slope, grad_merged, par, child_in, child_out, mats,
        place, up, sel,
    )
    parts = sum_over_devices(dw)
    got_a = trade(inner, "inner")
    got_b = relay_out(outer, got_a)

    table = pl.pallas_call(
        table_kernel,
        grid=(1,),
        in_specs=[whole(field), whole(field), whole(sel.shape)],
        out_specs=whole(local_part),
        out_shape=shape_of(local_part),
        compiler_params=params(),
        cost_estimate=cost(3),
        name="face_table",
    )(merged, grad_pre, sel)
    got_c, table = relay_in(got_b, table)

    output, grad_state = pl.pallas_call(
        final_kernel,
        grid=(STEPS,),
        in_specs=[SMEM()]
        + [blocked(field)] * 4
        + [whole(local_part), whole(near), whole(near_far), whole(far), whole(mats_shape)]
        + [whole(spread.shape)],
        out_specs=[blocked(field), blocked(field)],
        out_shape=[shape_of(field), shape_of(field)],
        scratch_shapes=tap_scratch
        + [pltpu.VMEM((PB, 7 * C, CELLS), BF), pltpu.VMEM((PB, 7 * C, CELLS), BF)],
        compiler_params=params(),
        cost_estimate=cost(10),
        name="last_level",
    )(meta, merged, grad_pre, xs, zs, table, got_a, got_b, got_c, mats, spread)

    scale = 1.0 / math.sqrt(float(devices * SLOTS * CELLS))
    mat = shape_of((7, C, C), F32)
    grads = pl.pallas_call(
        functools.partial(weights_kernel, scale),
        out_shape=[mat, mat, mat],
        cost_estimate=cost(2),
        name="weight_sums",
    )(parts)
    return (output, grad_state, *grads)


def solution(mesh):
    in_specs = (
        P("patch", None, None),
        P(),
        P(),
        P(),
        P("patch", None, None),
        P(),
        P("patch", None),
        P("patch", None),
        P("patch"),
    )
    out_specs = (P("patch", None, None), P("patch", None, None), P(), P(), P())
    return jax.shard_map(
        on_device, mesh=mesh, in_specs=in_specs, out_specs=out_specs, check_vma=False
    )
```

```python
import functools
import math

import numpy as np
import jax
import jax.numpy as jnp
from jax import lax
from jax.experimental import pallas as pl
from jax.experimental.pallas import tpu as pltpu
from jax.sharding import PartitionSpec as P

BF = jnp.bfloat16
F32 = jnp.float32
EDGE = 8
CELLS = 512
SLOTS = 32
C = 32
PB = 8
STEPS = SLOTS // PB
NPAR = 5
STRIDES = (64, 8, 1)
MORTON = (3, 8, 16)
ROW0 = (24, 16, 0)
NEAR = 27
FAR = 8
BASE_A = 6 * SLOTS
BASE_B = BASE_A + NEAR
BASE_C = BASE_B + NEAR + FAR
ROWS = BASE_C + FAR
VMEM_LIMIT = 14 * 1024 * 1024
IDX, TAG, DST, LEAD, TRAIL, SCAL = 0, 192, 384, 416, 448, 480
N_COUNT, N_ODD, N_LAST, N_OWNED = SCAL, SCAL + 1, SCAL + 2, SCAL + 3
META = 512
IN_F, OUT_B, OUT_F, IN_B, CO_F, CO_B = range(6)


def cell_coords():
    ids = np.arange(CELLS)
    return [ids // 64, ids // 8 % 8, ids % 8]


def face_cells(face):
    coords = cell_coords()
    keep = coords[face // 2] == (EDGE - 1 if face % 2 else 0)
    return np.nonzero(keep)[0]


def constants():
    sel = np.zeros((3, 2, CELLS, 256), np.float32)
    spread = np.zeros((2, 256, 2 * CELLS), np.float32)
    for face in range(6):
        for j, cell in enumerate(face_cells(face)):
            for kind in range(2):
                col = (face % 2) * 128 + kind * 64 + j
                sel[face // 2, kind, cell, col] = 1
                if face >= 2:
                    spread[face // 2 - 1, col, kind * CELLS + cell] = 1
    c0, c1, c2 = cell_coords()
    group = (c0 // 2) * 16 + (c1 // 2) * 4 + c2 // 2
    rest = np.zeros((2, CELLS, 128), np.float32)
    up = np.zeros((128, 2 * CELLS), np.float32)
    for cell in range(CELLS):
        rest[0, cell, group[cell]] = 0.125
        rest[1, cell, 64 + group[cell]] = 1
        up[group[cell], cell] = 1
        up[64 + group[cell], CELLS + cell] = 1
    place = np.zeros((256, 2 * CELLS), np.float32)
    for o2 in range(2):
        for a in range(64):
            cell = (a // 16) * 64 + (a // 4 % 4) * 8 + a % 4 + 4 * o2
            place[128 * o2 + a, cell] = 1
            place[128 * o2 + 64 + a, CELLS + cell] = 1
    as_bf = lambda item: np.asarray(item, jnp.bfloat16)
    return (
        as_bf(sel.reshape(6, CELLS, 256)),
        as_bf(spread),
        as_bf(rest),
        as_bf(up),
        as_bf(place),
    )


def dot(a, b):
    return jnp.dot(a, b, preferred_element_type=F32)


def dot_nt(a, b):
    return lax.dot_general(a, b, (((1,), (1,)), ((), ())), preferred_element_type=F32)


def coord_of(dim):
    lane = lax.broadcasted_iota(jnp.int32, (16, CELLS), 1)
    return (lane // STRIDES[dim]) % EDGE


def on_face(face):
    edge = EDGE - 1 if face % 2 else 0
    return jnp.where(coord_of(face // 2) == edge, 1.0, 0.0)


def halves(field):
    return field.reshape(field.shape[0] // 16, 16, CELLS)


def times(field, mask):
    return (halves(field) * mask[None]).reshape(field.shape)


def toward(field, face):
    stride = STRIDES[face // 2]
    shift = CELLS - stride if face % 2 else stride
    return pltpu.roll(field, shift, 1)


def send_rows(count, odd, v_ref, y_ref, sel_ref, v_rows, y_rows, sides, inner_ref, outer_ref):
    for side in range(2):
        for dim in (2, 1, 0):
            depth = MORTON[dim]
            for i in range(depth):
                slot = jnp.clip(count - depth + i, 0, SLOTS - 1) if side else i
                v_rows[i] = v_ref[slot]
                y_rows[i] = y_ref[slot]
            cols = slice(side * 128, side * 128 + 128)
            layers = dot(v_rows[:depth].reshape(depth * C, CELLS), sel_ref[2 * dim, :, cols])
            layers += dot(y_rows[:depth].reshape(depth * C, CELLS), sel_ref[2 * dim + 1, :, cols])
            layers = layers.astype(BF).reshape(depth, C, 128)
            if dim == 2 and side:
                sides[side, 0:8] = layers[8:16]
                sides[side, 8:16] = layers[0:8]
            else:
                sides[side, ROW0[dim] : ROW0[dim] + depth] = layers
    inner_ref[...] = sides[1 - odd]
    outer_ref[...] = sides[odd]


def layers_kernel(counts, v_ref, y_ref, sel_ref, inner_ref, outer_ref, v_rows, y_rows, sides):
    rank = lax.axis_index("patch")
    send_rows(
        counts[rank], rank % 2, v_ref, y_ref, sel_ref, v_rows, y_rows, sides, inner_ref, outer_ref
    )


def fill_table(v_ref, y_ref, sel_ref, table):
    for dim in range(3):
        layers = dot(v_ref[...].reshape(SLOTS * C, CELLS), sel_ref[2 * dim])
        layers += dot(y_ref[...].reshape(SLOTS * C, CELLS), sel_ref[2 * dim + 1])
        layers = layers.astype(BF)
        for high in range(2):
            face = 2 * dim + high
            table[face * SLOTS : (face + 1) * SLOTS] = layers[
                :, high * 128 : high * 128 + 128
            ].reshape(SLOTS, C, 128)


def prepare_kernel(
    counts, neighbour, level_tag, octant,
    got_ref, x_ref, z_ref, sel_ref, w_in, w_out, w_co,
    meta, xs, zs, mats, table,
):
    rank = lax.axis_index("patch")
    odd = rank % 2

    def count_at(device):
        here = counts[jnp.clip(device, 0, counts.shape[0] - 1)]
        return jnp.where(device < 0, 0, here)

    first = lax.fori_loop(0, rank, lambda d, s: s + counts[d], jnp.int32(0))
    count = count_at(rank)
    count_1 = count_at(rank - 1)
    count_2 = count_at(rank - 2)
    stop = first + count
    meta[N_COUNT] = count
    meta[N_ODD] = odd
    meta[N_LAST] = jnp.where(stop % 8 != 0, stop // 8 - first // 8, NPAR)
    meta[N_OWNED] = jnp.where(first % 8 == 0, 1, 0)
    near_left = jnp.where(odd == 1, BASE_A, BASE_B)
    near_right = jnp.where(odd == 1, BASE_B, BASE_A)
    far_left = jnp.where(odd == 1, BASE_C, BASE_B + NEAR)
    far_right = jnp.where(odd == 1, BASE_B + NEAR, BASE_C)
    lead_count = (8 - first % 8) % 8

    def per_slot(p, carry):
        live = p < count
        parent = (first % 8 + p) // 8
        o = jnp.clip(octant[p], 0, 7)
        meta[DST + p] = jnp.where(live, parent * 8 + o, NPAR * 8)
        meta[LEAD + p] = jnp.where(live & (p < lead_count), o, 8)
        meta[TRAIL + p] = jnp.where(live & (p >= count - stop % 8), o, 8)
        for face in range(6):
            dim = face // 2
            depth = MORTON[dim]
            other = neighbour[face, p]
            tag = level_tag[face, p]
            away = other // SLOTS - rank
            slot = other % SLOTS
            if face % 2:
                near = near_right + ROW0[dim] + slot
                far = far_right + slot
            else:
                back = slot - (count_1 - depth)
                near = near_left + ((back + 8) % 16 if dim == 2 else ROW0[dim] + back)
                far = far_left + slot - (count_2 - 8)
            row = jnp.where(away == 0, (face ^ 1) * SLOTS + slot, near)
            row = jnp.where(jnp.abs(away) == 2, far, row)
            row = jnp.where(tag == 1, face * SLOTS + p, row)
            meta[IDX + face * SLOTS + p] = jnp.clip(row, 0, ROWS - 1)
            meta[TAG + face * SLOTS + p] = tag
        return carry

    lax.fori_loop(0, SLOTS, per_slot, 0)
    for k, (weight, turned) in enumerate(
        ((w_in, True), (w_out, False), (w_out, True), (w_in, False), (w_co, True), (w_co, False))
    ):
        for f in range(7):
            one = weight[f].astype(F32)
            mats[k, :, f * C : (f + 1) * C] = (one.T if turned else one).astype(BF)
    for p in range(SLOTS):
        live = (p < count).astype(F32)
        xs[p] = (x_ref[p].astype(F32) * live).astype(BF)
        zs[p] = (z_ref[p].astype(F32) * live).astype(BF)
    fill_table(xs, zs, sel_ref, table)
    table[BASE_A:BASE_B] = got_ref[...]


def table_kernel(v_ref, y_ref, sel_ref, table):
    fill_table(v_ref, y_ref, sel_ref, table)


def join_table(parts, coef, table):
    start = 0
    for part in parts:
        size = part.shape[0]
        table[start : start + size] = part[...]
        start += size
    for dim in range(3):
        low, high = on_face(2 * dim), on_face(2 * dim + 1)
        for t_low in range(2):
            for t_high in range(2):
                row = dim * 4 + t_low * 2 + t_high
                coef[row, 0] = (low * (1 - t_low) + high * t_high).astype(BF)
                coef[row, 1] = (high * (1 - t_high) + low * t_low).astype(BF)


def block_taps(start, meta, v_ref, y_ref, spread_ref, table, coef, picked, ta, tb):
    for dim in range(3):
        low, high = 2 * dim, 2 * dim + 1
        edges = [on_face(low), on_face(high)]
        inside = [(1.0 - edge).astype(BF) for edge in edges]
        edges = [edge.astype(BF) for edge in edges]
        if dim:
            for p in range(PB):
                picked[p, :, 0:128] = table[meta[IDX + low * SLOTS + start + p]]
                picked[p, :, 128:256] = table[meta[IDX + high * SLOTS + start + p]]
            spread = dot(picked[...].reshape(PB * C, 256), spread_ref[dim - 1]).astype(BF)
        for p in range(PB):
            if dim:
                rows = slice(p * C, (p + 1) * C)
                v_edge = spread[rows, :CELLS]
                y_edge = spread[rows, CELLS:]
            else:
                r_low = table[meta[IDX + low * SLOTS + start + p]]
                r_high = table[meta[IDX + high * SLOTS + start + p]]
                blank = jnp.zeros((C, 256), BF)
                v_edge = jnp.concatenate([r_low, blank, pltpu.roll(r_high, 64, 1)], axis=1)
                y_edge = jnp.concatenate([pltpu.roll(r_low, 64, 1), blank, r_high], axis=1)
            field = v_ref[p]
            other = y_ref[p]
            if dim == 0:
                ta[p, 0:C] = field
                tb[p, 0:C] = other
            row = (
                dim * 4
                + meta[TAG + low * SLOTS + start + p] * 2
                + meta[TAG + high * SLOTS + start + p]
            )
            for k, face in enumerate((low, high)):
                ta[p, C * (face + 1) : C * (face + 2)] = times(
                    toward(field, face), inside[k]
                ) + times(v_edge, edges[k])
                back = face ^ 1
                tb[p, C * (back + 1) : C * (back + 2)] = times(
                    toward(other, face), inside[k]
                ) + times(y_edge, coef[row, k])


def silu_pair(pre):
    sigma = 1.0 / (1.0 + jnp.exp(-pre))
    return pre * sigma, sigma * (1.0 + pre * (1.0 - sigma))


def fine_kernel(
    meta, xs, zs, t_ref, b_ref, c_ref, mats, spread_ref, rest_ref,
    ta_ref, tb_ref, hidden_ref, slope_ref, gm_ref, par_ref, inner_ref, outer_ref,
    table, coef, picked, par, ends,
):
    join_table((t_ref, b_ref, c_ref), coef, table)
    par[...] = jnp.zeros_like(par)
    ends[...] = jnp.zeros_like(ends)

    @pl.loop(0, STEPS)
    def _(step):
        start = step * PB
        x_at, z_at, ta, tb, hidden_at, slope_at, gm_at = [
            item.at[pl.ds(start, PB)]
            for item in (xs, zs, ta_ref, tb_ref, hidden_ref, slope_ref, gm_ref)
        ]
        block_taps(start, meta, x_at, z_at, spread_ref, table, coef, picked, ta, tb)
        for p in range(PB):
            hidden, slope = silu_pair(dot(mats[IN_F], ta[p]))
            hidden_at[p] = hidden.astype(BF)
            slope_at[p] = slope.astype(BF)
            gm_at[p] = dot(mats[OUT_B], tb[p]).astype(BF)
        child = dot(hidden_at[...].reshape(PB * C, CELLS), rest_ref[0])
        child += dot(gm_at[...].reshape(PB * C, CELLS), rest_ref[1])
        child = child.astype(BF)
        for p in range(PB):
            row = child[p * C : (p + 1) * C]
            par[meta[DST + start + p]] = row
            ends[0, meta[LEAD + start + p]] = row
            ends[1, meta[TRAIL + start + p]] = row

    par_ref[...] = par[: NPAR * 8]
    odd = meta[N_ODD]
    inner_ref[...] = ends[1 - odd, 0:8]
    outer_ref[...] = ends[odd, 0:8]


def coarse_level(meta, par_ref, inner_ref, outer_ref, wa, wb, place_ref, par, taps, up_rows, dw_ref):
    par[: NPAR * 8] = par_ref[...]
    par[NPAR * 8 :] = jnp.zeros((8, C, 128), BF)
    last = meta[N_LAST] * 8
    odd = meta[N_ODD]
    inner_at = jnp.where(odd == 1, 0, last)
    outer_at = jnp.where(odd == 1, last, 0)
    for o in range(8):
        par[inner_at + o] = par[inner_at + o] + inner_ref[o]
    for o in range(8):
        par[outer_at + o] = par[outer_at + o] + outer_ref[o]

    rows = NPAR * C
    both = jnp.zeros((rows, 2 * CELLS), BF)
    for o in range(0, 8, 2):
        lhs = jnp.concatenate(
            [
                jnp.concatenate([par[q * 8 + o], par[q * 8 + o + 1]], axis=1)
                for q in range(NPAR)
            ],
            axis=0,
        )
        put = dot(lhs, place_ref[...]).astype(BF)
        shift = (o // 4) * 256 + (o // 2 % 2) * 32
        if shift:
            put = jnp.concatenate(
                [
                    pltpu.roll(put[:, :CELLS], shift, 1),
                    pltpu.roll(put[:, CELLS:], shift, 1),
                ],
                axis=1,
            )
        both += put
    field = both[:, :CELLS]
    cotan = both[:, CELLS:].astype(F32)
    edges = [on_face(face).astype(BF) for face in range(6)]
    inside = [(1.0 - on_face(face)).astype(BF) for face in range(6)]

    def store(face, value):
        taps[:, C * face : C * (face + 1)] = value.reshape(NPAR, C, CELLS)

    store(0, field)
    for face in range(6):
        store(face + 1, times(toward(field, face), inside[face]) + times(field, edges[face]))
    pre = jnp.concatenate([dot(wa, taps[q]) for q in range(NPAR)], axis=0)
    act, slope = silu_pair(pre)
    act = act.astype(BF)
    grad = (cotan * slope).astype(BF)
    dw = jnp.zeros((7 * C, C), F32)
    for q in range(NPAR):
        part = dot_nt(taps[q], grad[q * C : (q + 1) * C])
        if q == 0:
            part = part * meta[N_OWNED].astype(F32)
        dw += part
    store(0, grad)
    for face in range(6):
        back = face ^ 1
        store(face + 1, times(toward(grad, back), inside[back]) + times(grad, edges[face]))
    down = jnp.concatenate([dot(wb, taps[q]) for q in range(NPAR)], axis=0).astype(BF)
    for o in range(0, 8, 2):
        one, two = act, down
        shift = (o // 4) * 256 + (o // 2 % 2) * 32
        if shift:
            one = pltpu.roll(act, CELLS - shift, 1)
            two = pltpu.roll(down, CELLS - shift, 1)
        got = dot_nt(one, place_ref[:, :CELLS]) + dot_nt(two, place_ref[:, CELLS:])
        got = got.astype(BF)
        for q in range(NPAR):
            up_rows[q * 8 + o] = got[q * C : (q + 1) * C, :128]
            up_rows[q * 8 + o + 1] = got[q * C : (q + 1) * C, 128:]
    up_rows[NPAR * 8] = jnp.zeros((C, 128), BF)
    dw_ref[:, 2 * C : 3 * C] = dw


def merge_kernel(
    meta,
    ta_ref, tb_ref, hidden_ref, slope_ref, gm_ref, par_ref, pin_ref, pout_ref,
    mats, place_ref, up_ref, sel_ref,
    merged_ref, gpa_ref, dw_ref, inner_ref, outer_ref,
    par, taps, up_rows, picked, v_rows, y_rows, sides,
):
    dw_ref[...] = jnp.zeros_like(dw_ref)
    coarse_level(
        meta, par_ref, pin_ref, pout_ref, mats[CO_F], mats[CO_B],
        place_ref, par, taps, up_rows, dw_ref,
    )

    @pl.loop(0, STEPS)
    def _(step):
        start = step * PB
        for p in range(PB):
            picked[p] = up_rows[meta[DST + start + p]]
        spread = dot(picked[...].reshape(PB * C, 128), up_ref[...])
        dw_in = jnp.zeros((7 * C, C), F32)
        dw_out = jnp.zeros((7 * C, C), F32)
        for p in range(PB):
            rows = slice(p * C, (p + 1) * C)
            here = start + p
            merged = (hidden_ref[here].astype(F32) + spread[rows, :CELLS]).astype(BF)
            grad = gm_ref[here].astype(F32) + spread[rows, CELLS:] * 0.125
            gpa = (grad * slope_ref[here].astype(F32)).astype(BF)
            merged_ref[here] = merged
            gpa_ref[here] = gpa
            dw_in += dot_nt(ta_ref[here], gpa)
            dw_out += dot_nt(tb_ref[here], merged)
        dw_ref[:, 0:C] += dw_in
        dw_ref[:, C : 2 * C] += dw_out

    send_rows(
        meta[N_COUNT], meta[N_ODD], merged_ref, gpa_ref, sel_ref,
        v_rows, y_rows, sides, inner_ref, outer_ref,
    )


def final_kernel(
    meta, v_ref, y_ref, xs, zs, t_ref, a_ref, b_ref, c_ref, mats, spread_ref,
    out_ref, gs_ref,
    table, coef, picked, ta, tb,
):
    join_table((t_ref, a_ref, b_ref, c_ref), coef, table)

    @pl.loop(0, STEPS)
    def _(step):
        start = step * PB
        v_at, y_at = v_ref.at[pl.ds(start, PB)], y_ref.at[pl.ds(start, PB)]
        block_taps(start, meta, v_at, y_at, spread_ref, table, coef, picked, ta, tb)
        for p in range(PB):
            here = start + p
            out_ref[here] = (xs[here].astype(F32) + dot(mats[OUT_F], ta[p])).astype(BF)
            gs_ref[here] = (zs[here].astype(F32) + dot(mats[IN_B], tb[p])).astype(BF)


def weights_kernel(scale, parts_ref, in_ref, out_ref, co_ref):
    total = parts_ref[...] * scale
    for f in range(7):
        rows = slice(f * C, (f + 1) * C)
        in_ref[f] = total[rows, 0:C]
        out_ref[f] = total[rows, C : 2 * C].T
        co_ref[f] = total[rows, 2 * C : 3 * C]


SMEM = functools.partial(pl.BlockSpec, memory_space=pltpu.SMEM)


VMEM = functools.partial(pl.BlockSpec, memory_space=pltpu.VMEM)


def params():
    return pltpu.CompilerParams(vmem_limit_bytes=VMEM_LIMIT)


def shape_of(shape, dtype=BF):
    return jax.ShapeDtypeStruct(shape, dtype)


def cost(micros):
    return pl.CostEstimate(
        flops=int(micros * 1e6), bytes_accessed=int(micros * 3.0e6), transcendentals=0
    )


def pairs(kind, devices):
    if kind == "inner":
        links = [(2 * c, 2 * c + 1) for c in range(devices // 2)]
    else:
        links = [(2 * c + 1, 2 * c + 2) for c in range(devices // 2 - 1)]
    return links + [(b, a) for a, b in links]


def trade(block, kind):
    return lax.ppermute(block, "patch", pairs(kind, lax.axis_size("patch")))


def relay_out(outer, got_a):
    return trade(jnp.concatenate([outer, got_a[:FAR]], axis=0), "outer")


def relay_in(got_b, first):
    got_b, first = lax.optimization_barrier((got_b, first))
    return trade(got_b[:FAR], "inner"), first


def sum_over_devices(block):
    devices = lax.axis_size("patch")
    for mask in (1, 2, 6, 8, 24, 32, 96):
        block = block + lax.ppermute(block, "patch", [(i, i ^ mask) for i in range(devices)])
    return block


def on_device(
    fine_state, weight_in, weight_out, weight_coarse, cotangent,
    owner_count, neighbour, level_tag, octant,
):
    devices = lax.axis_size("patch")
    sel, spread, rest, up, place = [jnp.asarray(item) for item in constants()]

    field = (SLOTS, C, CELLS)
    stack = (SLOTS, 7 * C, CELLS)
    near = (NEAR, C, 128)
    near_far = (NEAR + FAR, C, 128)
    far = (FAR, C, 128)
    mats_shape = (6, C, 7 * C)
    first_part = (BASE_B, C, 128)
    local_part = (BASE_A, C, 128)
    rows_scratch = [pltpu.VMEM((16, C, CELLS), BF)] * 2 + [pltpu.VMEM((2, NEAR, C, 128), BF)]
    tap_scratch = [
        pltpu.VMEM((ROWS, C, 128), BF),
        pltpu.VMEM((12, 2, 16, CELLS), BF),
        pltpu.VMEM((PB, C, 256), BF),
    ]

    inner, outer = pl.pallas_call(
        layers_kernel,
        in_specs=[SMEM(), VMEM(), VMEM(), VMEM()],
        out_specs=[VMEM(), VMEM()],
        out_shape=[shape_of(near), shape_of(near)],
        scratch_shapes=rows_scratch,
        compiler_params=params(),
        cost_estimate=cost(4),
        name="face_rows",
    )(owner_count, fine_state, cotangent, sel)
    got_a = trade(inner, "inner")
    got_b = relay_out(outer, got_a)

    meta, xs, zs, mats, table = pl.pallas_call(
        prepare_kernel,
        in_specs=[SMEM()] * 4
        + [VMEM(), VMEM(), VMEM(), VMEM()]
        + [VMEM()] * 3,
        out_specs=[SMEM(), VMEM(), VMEM(), VMEM(), VMEM()],
        out_shape=[shape_of((META,), jnp.int32), shape_of(field), shape_of(field)]
        + [shape_of(mats_shape), shape_of(first_part)],
        compiler_params=params(),
        cost_estimate=cost(6),
        name="prepare",
    )(
        owner_count, neighbour.T, level_tag.T, octant, got_a, fine_state, cotangent, sel,
        weight_in, weight_out, weight_coarse,
    )
    got_c, meta = relay_in(got_b, meta)

    taps_a, taps_b, hidden, slope, grad_merged, par, pin, pout = pl.pallas_call(
        fine_kernel,
        in_specs=[SMEM(), VMEM(), VMEM()]
        + [VMEM(), VMEM(), VMEM(), VMEM()]
        + [VMEM(), VMEM()],
        out_specs=[VMEM(), VMEM(), VMEM(), VMEM(), VMEM()]
        + [VMEM(), VMEM(), VMEM()],
        out_shape=[shape_of(stack), shape_of(stack), shape_of(field), shape_of(field)]
        + [shape_of(field), shape_of((NPAR * 8, C, 128)), shape_of(far), shape_of(far)],
        scratch_shapes=tap_scratch
        + [pltpu.VMEM((NPAR * 8 + 8, C, 128), BF), pltpu.VMEM((2, 16, C, 128), BF)],
        compiler_params=params(),
        cost_estimate=cost(12),
        name="fine_level",
    )(meta, xs, zs, table, got_b, got_c, mats, spread, rest)
    child_out = trade(pout, "outer")
    child_in = trade(pin, "inner")

    dw_shape = (7 * C, 128)
    merged, grad_pre, dw, inner, outer = pl.pallas_call(
        merge_kernel,
        in_specs=[SMEM()]
        + [VMEM(), VMEM(), VMEM(), VMEM(), VMEM()]
        + [VMEM(), VMEM(), VMEM(), VMEM()]
        + [VMEM(), VMEM(), VMEM()],
        out_specs=[VMEM(), VMEM(), VMEM(), VMEM(), VMEM()],
        out_shape=[shape_of(field), shape_of(field), shape_of(dw_shape, F32)]
        + [shape_of(near), shape_of(near)],
        scratch_shapes=[
            pltpu.VMEM((NPAR * 8 + 8, C, 128), BF),
            pltpu.VMEM((NPAR, 7 * C, CELLS), BF),
            pltpu.VMEM((NPAR * 8 + 8, C, 128), BF),
            pltpu.VMEM((PB, C, 128), BF),
        ]
        + rows_scratch,
        compiler_params=params(),
        cost_estimate=cost(14),
        name="coarse_and_merge",
    )(
        meta, taps_a, taps_b, hidden, slope, grad_merged, par, child_in, child_out, mats,
        place, up, sel,
    )
    parts = sum_over_devices(dw)
    got_a = trade(inner, "inner")
    got_b = relay_out(outer, got_a)

    table = pl.pallas_call(
        table_kernel,
        in_specs=[VMEM(), VMEM(), VMEM()],
        out_specs=VMEM(),
        out_shape=shape_of(local_part),
        compiler_params=params(),
        cost_estimate=cost(3),
        name="face_table",
    )(merged, grad_pre, sel)
    got_c, table = relay_in(got_b, table)

    output, grad_state = pl.pallas_call(
        final_kernel,
        in_specs=[SMEM()]
        + [VMEM()] * 4
        + [VMEM(), VMEM(), VMEM(), VMEM(), VMEM()]
        + [VMEM()],
        out_specs=[VMEM(), VMEM()],
        out_shape=[shape_of(field), shape_of(field)],
        scratch_shapes=tap_scratch
        + [pltpu.VMEM((PB, 7 * C, CELLS), BF), pltpu.VMEM((PB, 7 * C, CELLS), BF)],
        compiler_params=params(),
        cost_estimate=cost(10),
        name="last_level",
    )(meta, merged, grad_pre, xs, zs, table, got_a, got_b, got_c, mats, spread)

    scale = 1.0 / math.sqrt(float(devices * SLOTS * CELLS))
    mat = shape_of((7, C, C), F32)
    grads = pl.pallas_call(
        functools.partial(weights_kernel, scale),
        in_specs=[VMEM()],
        out_specs=[VMEM()] * 3,
        compiler_params=params(),
        out_shape=[mat, mat, mat],
        cost_estimate=cost(2),
        name="weight_sums",
    )(parts)
    return (output, grad_state, *grads)


def solution(mesh):
    in_specs = (
        P("patch", None, None),
        P(),
        P(),
        P(),
        P("patch", None, None),
        P(),
        P("patch", None),
        P("patch", None),
        P("patch"),
    )
    out_specs = (P("patch", None, None), P("patch", None, None), P(), P(), P())
    return jax.shard_map(
        on_device, mesh=mesh, in_specs=in_specs, out_specs=out_specs, check_vma=False
    )
```

```python
import functools
import math

import numpy as np
import jax
import jax.numpy as jnp
from jax import lax
from jax.experimental import pallas as pl
from jax.experimental.pallas import tpu as pltpu
from jax.sharding import PartitionSpec as P

BF = jnp.bfloat16
F32 = jnp.float32
EDGE = 8
CELLS = 512
SLOTS = 32
C = 32
PB = 8
STEPS = SLOTS // PB
NPAR = 5
STRIDES = (64, 8, 1)
MORTON = (3, 8, 16)
ROW0 = (24, 16, 0)
NEAR = 27
FAR = 8
BASE_A = 6 * SLOTS
BASE_B = BASE_A + NEAR
BASE_C = BASE_B + NEAR + FAR
ROWS = BASE_C + FAR
VMEM_LIMIT = 14 * 1024 * 1024
FULL_LIMIT = 60 * 1024 * 1024
DST, LEAD, TRAIL, SCAL = 0, 32, 64, 96
N_COUNT, N_ODD, N_LAST, N_OWNED = SCAL, SCAL + 1, SCAL + 2, SCAL + 3
META = 128
IN_F, OUT_B = range(2)
OUT_F, IN_B, CO_F, CO_B = range(4)
CHUNKS = 8
DWR = 7


def cell_coords():
    ids = np.arange(CELLS)
    return [ids // 64, ids // 8 % 8, ids % 8]


def face_cells(face):
    coords = cell_coords()
    keep = coords[face // 2] == (EDGE - 1 if face % 2 else 0)
    return np.nonzero(keep)[0]


def constants():
    sel = np.zeros((3, 2, CELLS, 256), np.float32)
    spread = np.zeros((2, 256, 2 * CELLS), np.float32)
    for face in range(6):
        for j, cell in enumerate(face_cells(face)):
            for kind in range(2):
                col = (face % 2) * 128 + kind * 64 + j
                sel[face // 2, kind, cell, col] = 1
                if face >= 2:
                    spread[face // 2 - 1, col, kind * CELLS + cell] = 1
    c0, c1, c2 = cell_coords()
    group = (c0 // 2) * 16 + (c1 // 2) * 4 + c2 // 2
    rest = np.zeros((2, CELLS, 128), np.float32)
    up = np.zeros((128, 2 * CELLS), np.float32)
    for cell in range(CELLS):
        rest[0, cell, group[cell]] = 0.125
        rest[1, cell, 64 + group[cell]] = 1
        up[group[cell], cell] = 1
        up[64 + group[cell], CELLS + cell] = 1
    place = np.zeros((256, 2 * CELLS), np.float32)
    for o2 in range(2):
        for a in range(64):
            cell = (a // 16) * 64 + (a // 4 % 4) * 8 + a % 4 + 4 * o2
            place[128 * o2 + a, cell] = 1
            place[128 * o2 + 64 + a, CELLS + cell] = 1
    as_bf = lambda item: np.asarray(item, jnp.bfloat16)
    return (
        as_bf(sel.reshape(6, CELLS, 256)),
        as_bf(spread),
        as_bf(rest),
        as_bf(up),
        as_bf(place),
    )


def dot(a, b):
    return jnp.dot(a, b, preferred_element_type=F32)


def dot_nt(a, b):
    return lax.dot_general(a, b, (((1,), (1,)), ((), ())), preferred_element_type=F32)


def coord_of(dim):
    lane = lax.broadcasted_iota(jnp.int32, (16, CELLS), 1)
    return (lane // STRIDES[dim]) % EDGE


def on_face(face):
    edge = EDGE - 1 if face % 2 else 0
    return jnp.where(coord_of(face // 2) == edge, 1.0, 0.0)


def halves(field):
    return field.reshape(field.shape[0] // 16, 16, CELLS)


def times(field, mask):
    return (halves(field) * mask[None]).reshape(field.shape)


def toward(field, face):
    stride = STRIDES[face // 2]
    shift = CELLS - stride if face % 2 else stride
    return pltpu.roll(field, shift, 1)


def send_rows(count, odd, v_ref, y_ref, sel_ref, v_rows, y_rows, sides, inner_ref, outer_ref):
    for side in range(2):
        for dim in (2, 1, 0):
            depth = MORTON[dim]
            for i in range(depth):
                slot = jnp.clip(count - depth + i, 0, SLOTS - 1) if side else i
                v_rows[i] = v_ref[slot]
                y_rows[i] = y_ref[slot]
            cols = slice(side * 128, side * 128 + 128)
            layers = dot(v_rows[:depth].reshape(depth * C, CELLS), sel_ref[2 * dim, :, cols])
            layers += dot(y_rows[:depth].reshape(depth * C, CELLS), sel_ref[2 * dim + 1, :, cols])
            layers = layers.astype(BF).reshape(depth, C, 128)
            if dim == 2 and side:
                sides[side, 0:8] = layers[8:16]
                sides[side, 8:16] = layers[0:8]
            else:
                sides[side, ROW0[dim] : ROW0[dim] + depth] = layers
    inner_ref[...] = sides[1 - odd]
    outer_ref[...] = sides[odd]


def make_selection(sel_ref):
    cell = lax.broadcasted_iota(jnp.int32, (CELLS, 256), 0)
    lane = lax.broadcasted_iota(jnp.int32, (CELLS, 256), 1)
    at = lane % 64
    edge = jnp.where(lane < 128, 0, EDGE - 1)
    first_half = lane % 128 < 64
    for dim in range(3):
        if dim == 0:
            want = edge * 64 + at
        elif dim == 1:
            want = at // 8 * 64 + edge * 8 + at % 8
        else:
            want = at * 8 + edge
        hit = cell == want
        sel_ref[2 * dim] = jnp.where(hit & first_half, 1.0, 0.0).astype(BF)
        sel_ref[2 * dim + 1] = jnp.where(hit & ~first_half, 1.0, 0.0).astype(BF)


def layers_kernel(
    counts_hbm, x_hbm, z_hbm, inner_ref, outer_ref,
    v_rows, y_rows, sides, x_ref, z_ref, sel_ref, counts, sems, counts_sem,
):
    rank = lax.axis_index("patch")
    size = SLOTS // CHUNKS
    copies = [pltpu.make_async_copy(counts_hbm, counts, counts_sem)]
    for k in range(CHUNKS):
        part = pl.ds(k * size, size)
        copies.append(pltpu.make_async_copy(x_hbm.at[part], x_ref.at[part], sems.at[0, k]))
        copies.append(pltpu.make_async_copy(z_hbm.at[part], z_ref.at[part], sems.at[1, k]))
    for copy in copies:
        copy.start()
    make_selection(sel_ref)
    for copy in copies:
        copy.wait()
    send_rows(
        counts[rank], rank % 2, x_ref, z_ref, sel_ref, v_rows, y_rows, sides, inner_ref, outer_ref
    )


def fill_table(v_ref, y_ref, sel_ref, table):
    for dim in range(3):
        layers = dot(v_ref[...].reshape(SLOTS * C, CELLS), sel_ref[2 * dim])
        layers += dot(y_ref[...].reshape(SLOTS * C, CELLS), sel_ref[2 * dim + 1])
        layers = layers.astype(BF)
        for high in range(2):
            face = 2 * dim + high
            table[face * SLOTS : (face + 1) * SLOTS] = layers[
                :, high * 128 : high * 128 + 128
            ].reshape(SLOTS, C, 128)


def fill_mats(mats, weights):
    for k, (weight, turned) in enumerate(weights):
        for f in range(7):
            one = weight[f].astype(F32)
            mats[k, :, f * C : (f + 1) * C] = (one.T if turned else one).astype(BF)


def prepare_kernel(
    counts, octant, neighbour, level_tag,
    got_ref, x_ref, z_ref, sel_ref, w_in, w_out,
    meta, index, xs, zs, mats, table,
):
    rank = lax.axis_index("patch")
    odd = rank % 2

    def count_at(device):
        here = counts[jnp.clip(device, 0, counts.shape[0] - 1)]
        return jnp.where(device < 0, 0, here)

    first = lax.fori_loop(0, rank, lambda d, s: s + counts[d], jnp.int32(0))
    count = count_at(rank)
    count_1 = count_at(rank - 1)
    count_2 = count_at(rank - 2)
    stop = first + count
    meta[N_COUNT] = count
    meta[N_ODD] = odd
    meta[N_LAST] = jnp.where(stop % 8 != 0, stop // 8 - first // 8, NPAR)
    meta[N_OWNED] = jnp.where(first % 8 == 0, 1, 0)
    lead_count = (8 - first % 8) % 8
    for p in range(SLOTS):
        live = p < count
        parent = (first % 8 + p) // 8
        o = jnp.clip(octant[p], 0, 7)
        meta[DST + p] = jnp.where(live, parent * 8 + o, NPAR * 8)
        meta[LEAD + p] = jnp.where(live & (p < lead_count), o, 8)
        meta[TRAIL + p] = jnp.where(live & (p >= count - stop % 8), o, 8)

    near_left = jnp.where(odd == 1, BASE_A, BASE_B)
    near_right = jnp.where(odd == 1, BASE_B, BASE_A)
    far_left = jnp.where(odd == 1, BASE_C, BASE_B + NEAR)
    far_right = jnp.where(odd == 1, BASE_B + NEAR, BASE_C)
    face = lax.broadcasted_iota(jnp.int32, (6, SLOTS), 0)
    own = lax.broadcasted_iota(jnp.int32, (6, SLOTS), 1)
    depth = jnp.where(face < 2, MORTON[0], jnp.where(face < 4, MORTON[1], MORTON[2]))
    row0 = jnp.where(face < 2, ROW0[0], jnp.where(face < 4, ROW0[1], ROW0[2]))
    high = (face & 1) == 1
    other = neighbour[...]
    away = (other >> 5) - rank
    slot = other & 31
    back = slot - (count_1 - depth)
    left = jnp.where(face >= 4, (back + 8) & 15, row0 + back) + near_left
    near = jnp.where(high, near_right + row0 + slot, left)
    far = jnp.where(high, far_right + slot, far_left + slot - (count_2 - 8))
    row = jnp.where(away == 0, (face ^ 1) * SLOTS + slot, near)
    row = jnp.where((away == 2) | (away == -2), far, row)
    row = jnp.where(level_tag[...] == 1, face * SLOTS + own, row)
    index[0:6] = jnp.clip(row, 0, ROWS - 1)
    index[6:12] = level_tag[...]

    fill_mats(mats, ((w_in, True), (w_out, False)))
    for p in range(SLOTS):
        live = (p < count).astype(F32)
        xs[p] = (x_ref[p].astype(F32) * live).astype(BF)
        zs[p] = (z_ref[p].astype(F32) * live).astype(BF)
    fill_table(xs, zs, sel_ref, table)
    table[BASE_A:BASE_B] = got_ref[...]


def window_kernel(hidden_ref, tb_ref, rest_ref, w_in, w_out, w_co, mats, dw_ref, means_ref):
    fill_mats(mats, ((w_out, True), (w_in, False), (w_co, True), (w_co, False)))
    dw_ref[...] = jnp.zeros_like(dw_ref)

    @pl.loop(0, STEPS)
    def _(step):
        dw = jnp.zeros((7 * C, C), F32)
        for p in range(PB):
            here = step * PB + p
            dw += dot_nt(tb_ref[here], hidden_ref[here])
            means_ref[here] = dot(tb_ref[here], rest_ref[0]).astype(BF)
        dw_ref[...] += dw


def table_kernel(v_ref, y_ref, sel_ref, table):
    fill_table(v_ref, y_ref, sel_ref, table)


def join_table(parts, coef, table):
    start = 0
    for part in parts:
        size = part.shape[0]
        table[start : start + size] = part[...]
        start += size
    for dim in range(3):
        low, high = on_face(2 * dim), on_face(2 * dim + 1)
        for t_low in range(2):
            for t_high in range(2):
                row = dim * 4 + t_low * 2 + t_high
                coef[row, 0] = (low * (1 - t_low) + high * t_high).astype(BF)
                coef[row, 1] = (high * (1 - t_high) + low * t_low).astype(BF)


def block_taps(start, index, v_ref, y_ref, spread_ref, table, coef, picked, ta, tb):
    for dim in range(3):
        low, high = 2 * dim, 2 * dim + 1
        edges = [on_face(low), on_face(high)]
        inside = [(1.0 - edge).astype(BF) for edge in edges]
        edges = [edge.astype(BF) for edge in edges]
        if dim:
            for p in range(PB):
                picked[p, :, 0:128] = table[index[low, start + p]]
                picked[p, :, 128:256] = table[index[high, start + p]]
            spread = dot(picked[...].reshape(PB * C, 256), spread_ref[dim - 1]).astype(BF)
        for p in range(PB):
            if dim:
                rows = slice(p * C, (p + 1) * C)
                v_edge = spread[rows, :CELLS]
                y_edge = spread[rows, CELLS:]
            else:
                r_low = table[index[low, start + p]]
                r_high = table[index[high, start + p]]
                blank = jnp.zeros((C, 256), BF)
                v_edge = jnp.concatenate([r_low, blank, pltpu.roll(r_high, 64, 1)], axis=1)
                y_edge = jnp.concatenate([pltpu.roll(r_low, 64, 1), blank, r_high], axis=1)
            field = v_ref[p]
            other = y_ref[p]
            if dim == 0:
                ta[p, 0:C] = field
                tb[p, 0:C] = other
            row = (
                dim * 4
                + index[6 + low, start + p] * 2
                + index[6 + high, start + p]
            )
            for k, face in enumerate((low, high)):
                ta[p, C * (face + 1) : C * (face + 2)] = times(
                    toward(field, face), inside[k]
                ) + times(v_edge, edges[k])
                back = face ^ 1
                tb[p, C * (back + 1) : C * (back + 2)] = times(
                    toward(other, face), inside[k]
                ) + times(y_edge, coef[row, k])


def silu_pair(pre):
    sigma = 1.0 / (1.0 + jnp.exp(-pre))
    return pre * sigma, sigma * (1.0 + pre * (1.0 - sigma))


def fine_kernel(
    meta, index, xs, zs, t_ref, b_ref, c_ref, mats, spread_ref, rest_ref,
    ta_ref, tb_ref, hidden_ref, slope_ref, gm_ref, par_ref, inner_ref, outer_ref,
    table, coef, picked, par, ends,
):
    join_table((t_ref, b_ref, c_ref), coef, table)
    par[...] = jnp.zeros_like(par)
    ends[...] = jnp.zeros_like(ends)

    @pl.loop(0, STEPS)
    def _(step):
        start = step * PB
        x_at, z_at, ta, tb, hidden_at, slope_at, gm_at = [
            item.at[pl.ds(start, PB)]
            for item in (xs, zs, ta_ref, tb_ref, hidden_ref, slope_ref, gm_ref)
        ]
        block_taps(start, index, x_at, z_at, spread_ref, table, coef, picked, ta, tb)
        for p in range(PB):
            hidden, slope = silu_pair(dot(mats[IN_F], ta[p]))
            hidden_at[p] = hidden.astype(BF)
            slope_at[p] = slope.astype(BF)
            gm_at[p] = dot(mats[OUT_B], tb[p]).astype(BF)
        child = dot(hidden_at[...].reshape(PB * C, CELLS), rest_ref[0])
        child += dot(gm_at[...].reshape(PB * C, CELLS), rest_ref[1])
        child = child.astype(BF)
        for p in range(PB):
            row = child[p * C : (p + 1) * C]
            par[meta[DST + start + p]] = row
            ends[0, meta[LEAD + start + p]] = row
            ends[1, meta[TRAIL + start + p]] = row

    par_ref[...] = par[: NPAR * 8]
    odd = meta[N_ODD]
    inner_ref[...] = ends[1 - odd, 0:8]
    outer_ref[...] = ends[odd, 0:8]


def coarse_level(meta, par_ref, inner_ref, outer_ref, wa, wb, place_ref, par, taps, up_rows, dw_ref):
    par[: NPAR * 8] = par_ref[...]
    par[NPAR * 8 :] = jnp.zeros((8, C, 128), BF)
    last = meta[N_LAST] * 8
    odd = meta[N_ODD]
    inner_at = jnp.where(odd == 1, 0, last)
    outer_at = jnp.where(odd == 1, last, 0)
    for o in range(8):
        par[inner_at + o] = par[inner_at + o] + inner_ref[o]
    for o in range(8):
        par[outer_at + o] = par[outer_at + o] + outer_ref[o]

    rows = NPAR * C
    both = jnp.zeros((rows, 2 * CELLS), BF)
    for o in range(0, 8, 2):
        lhs = jnp.concatenate(
            [
                jnp.concatenate([par[q * 8 + o], par[q * 8 + o + 1]], axis=1)
                for q in range(NPAR)
            ],
            axis=0,
        )
        put = dot(lhs, place_ref[...]).astype(BF)
        shift = (o // 4) * 256 + (o // 2 % 2) * 32
        if shift:
            put = jnp.concatenate(
                [
                    pltpu.roll(put[:, :CELLS], shift, 1),
                    pltpu.roll(put[:, CELLS:], shift, 1),
                ],
                axis=1,
            )
        both += put
    field = both[:, :CELLS]
    cotan = both[:, CELLS:].astype(F32)
    edges = [on_face(face).astype(BF) for face in range(6)]
    inside = [(1.0 - on_face(face)).astype(BF) for face in range(6)]

    def store(face, value):
        taps[:, C * face : C * (face + 1)] = value.reshape(NPAR, C, CELLS)

    store(0, field)
    for face in range(6):
        store(face + 1, times(toward(field, face), inside[face]) + times(field, edges[face]))
    pre = jnp.concatenate([dot(wa, taps[q]) for q in range(NPAR)], axis=0)
    act, slope = silu_pair(pre)
    act = act.astype(BF)
    grad = (cotan * slope).astype(BF)
    dw = jnp.zeros((7 * C, C), F32)
    for q in range(NPAR):
        part = dot_nt(taps[q], grad[q * C : (q + 1) * C])
        if q == 0:
            part = part * meta[N_OWNED].astype(F32)
        dw += part
    store(0, grad)
    for face in range(6):
        back = face ^ 1
        store(face + 1, times(toward(grad, back), inside[back]) + times(grad, edges[face]))
    down = jnp.concatenate([dot(wb, taps[q]) for q in range(NPAR)], axis=0).astype(BF)
    for o in range(0, 8, 2):
        one, two = act, down
        shift = (o // 4) * 256 + (o // 2 % 2) * 32
        if shift:
            one = pltpu.roll(act, CELLS - shift, 1)
            two = pltpu.roll(down, CELLS - shift, 1)
        got = dot_nt(one, place_ref[:, :CELLS]) + dot_nt(two, place_ref[:, CELLS:])
        got = got.astype(BF)
        for q in range(NPAR):
            up_rows[q * 8 + o] = got[q * C : (q + 1) * C, :128]
            up_rows[q * 8 + o + 1] = got[q * C : (q + 1) * C, 128:]
    up_rows[NPAR * 8] = jnp.zeros((C, 128), BF)
    dw_ref[:, 2 * C : 3 * C] = dw


def merge_kernel(
    meta,
    ta_ref, means_ref, dw0_ref, hidden_ref, slope_ref, gm_ref, par_ref, pin_ref, pout_ref,
    mats, place_ref, up_ref, sel_ref,
    merged_ref, gpa_ref, sum_ref, inner_ref, outer_ref,
    par, taps, up_rows, picked, v_rows, y_rows, sides, dw_ref,
):
    dw_ref[...] = jnp.zeros_like(dw_ref)
    dw_ref[:, C : 2 * C] = dw0_ref[...]
    coarse_level(
        meta, par_ref, pin_ref, pout_ref, mats[CO_F], mats[CO_B],
        place_ref, par, taps, up_rows, dw_ref,
    )

    @pl.loop(0, STEPS)
    def _(step):
        start = step * PB
        for p in range(PB):
            picked[p] = up_rows[meta[DST + start + p]]
        spread = dot(picked[...].reshape(PB * C, 128), up_ref[...])
        dw_in = jnp.zeros((7 * C, C), F32)
        dw_out = jnp.zeros((7 * C, C), F32)
        for p in range(PB):
            rows = slice(p * C, (p + 1) * C)
            here = start + p
            merged = (hidden_ref[here].astype(F32) + spread[rows, :CELLS]).astype(BF)
            grad = gm_ref[here].astype(F32) + spread[rows, CELLS:] * 0.125
            gpa = (grad * slope_ref[here].astype(F32)).astype(BF)
            merged_ref[here] = merged
            gpa_ref[here] = gpa
            dw_in += dot_nt(ta_ref[here], gpa)
            dw_out += dot_nt(means_ref[here], picked[p])
        dw_ref[:, 0:C] += dw_in
        dw_ref[:, C : 2 * C] += dw_out * 8.0

    send_rows(
        meta[N_COUNT], meta[N_ODD], merged_ref, gpa_ref, sel_ref,
        v_rows, y_rows, sides, inner_ref.at[0:NEAR], outer_ref,
    )
    rounded = dw_ref[...].astype(BF).reshape(DWR, C, 128)
    sum_ref[...] = rounded
    inner_ref[NEAR : NEAR + DWR] = rounded


def second_table_kernel(v_ref, y_ref, sel_ref, got_ref, table):
    fill_table(v_ref, y_ref, sel_ref, table)
    table[BASE_A:BASE_B] = got_ref[0:NEAR]


def final_body(step, index, v_ref, y_ref, xs, zs, mats, spread_ref, table, coef, out_hbm, gs_hbm,
               picked, ta, tb, out_ref, gs_ref, sems):
    start = step * PB
    part = pl.ds(start, PB)
    block_taps(
        start, index, v_ref.at[part], y_ref.at[part], spread_ref, table, coef, picked, ta, tb
    )
    for p in range(PB):
        out_ref[p] = (xs[start + p].astype(F32) + dot(mats[OUT_F], ta[p])).astype(BF)
        gs_ref[p] = (zs[start + p].astype(F32) + dot(mats[IN_B], tb[p])).astype(BF)
    copies = [
        pltpu.make_async_copy(out_ref, out_hbm.at[part], sems.at[0]),
        pltpu.make_async_copy(gs_ref, gs_hbm.at[part], sems.at[1]),
    ]
    for copy in copies:
        copy.start()
    for copy in copies:
        copy.wait()


def first_final_kernel(
    index, v_ref, y_ref, xs, zs, mats, spread_ref, t_ref, b_ref, c_ref,
    table, coef, out_hbm, gs_hbm, *scratch,
):
    join_table((t_ref, b_ref, c_ref), coef, table)
    final_body(0, index, v_ref, y_ref, xs, zs, mats, spread_ref, table, coef, out_hbm, gs_hbm,
               *scratch)


def next_final_kernel(
    step, index, v_ref, y_ref, xs, zs, mats, spread_ref, table, coef, out_in, gs_in,
    out_hbm, gs_hbm, *scratch,
):
    final_body(step, index, v_ref, y_ref, xs, zs, mats, spread_ref, table, coef, out_hbm, gs_hbm,
               *scratch)


def weights_kernel(scale, one_ref, two_ref, in_ref, out_ref, co_ref):
    for f in range(7):
        total = (one_ref[f].astype(F32) + two_ref[f].astype(F32)) * scale
        in_ref[f] = total[:, 0:C]
        out_ref[f] = total[:, C : 2 * C].T
        co_ref[f] = total[:, 2 * C : 3 * C]


SMEM = functools.partial(pl.BlockSpec, memory_space=pltpu.SMEM)


VMEM = functools.partial(pl.BlockSpec, memory_space=pltpu.VMEM)
HBM = functools.partial(pl.BlockSpec, memory_space=pltpu.HBM)


def params(limit=VMEM_LIMIT):
    return pltpu.CompilerParams(vmem_limit_bytes=limit)


def shape_of(shape, dtype=BF):
    return jax.ShapeDtypeStruct(shape, dtype)


def cost(micros):
    return pl.CostEstimate(
        flops=int(micros * 1e6), bytes_accessed=int(micros * 3.0e6), transcendentals=0
    )


def pairs(kind, devices):
    if kind == "inner":
        links = [(2 * c, 2 * c + 1) for c in range(devices // 2)]
    else:
        links = [(2 * c + 1, 2 * c + 2) for c in range(devices // 2 - 1)]
    return links + [(b, a) for a, b in links]


def trade(block, kind):
    return lax.ppermute(block, "patch", pairs(kind, lax.axis_size("patch")))


def relay_out(outer, got_a):
    return trade(jnp.concatenate([outer, got_a[:FAR]], axis=0), "outer")


def relay_in(got_b, first):
    got_b, first = lax.optimization_barrier((got_b, first))
    return trade(got_b[:FAR], "inner"), first


def add(one, two):
    return (one.astype(F32) + two.astype(F32)).astype(BF)


def swap(block, mask):
    devices = lax.axis_size("patch")
    return lax.ppermute(block, "patch", [(i, i ^ mask) for i in range(devices)])


def on_device(
    fine_state, weight_in, weight_out, weight_coarse, cotangent,
    owner_count, neighbour, level_tag, octant,
):
    devices = lax.axis_size("patch")
    sel, spread, rest, up, place = [jnp.asarray(item) for item in constants()]

    field = (SLOTS, C, CELLS)
    stack = (SLOTS, 7 * C, CELLS)
    near = (NEAR, C, 128)
    far = (FAR, C, 128)
    par_rows = (NPAR * 8, C, 128)
    sel_shape = (6, CELLS, 256)
    rows_scratch = [pltpu.VMEM((16, C, CELLS), BF)] * 2 + [pltpu.VMEM((2, NEAR, C, 128), BF)]
    table_shape = (ROWS, C, 128)
    coef_shape = (12, 2, 16, CELLS)
    picked_scratch = pltpu.VMEM((PB, C, 256), BF)

    inner, outer = pl.pallas_call(
        layers_kernel,
        in_specs=[HBM()] * 3,
        out_specs=[VMEM()] * 2,
        out_shape=[shape_of(near), shape_of(near)],
        scratch_shapes=rows_scratch
        + [pltpu.VMEM(field, BF), pltpu.VMEM(field, BF), pltpu.VMEM(sel_shape, BF)]
        + [pltpu.SMEM(owner_count.shape, jnp.int32)]
        + [pltpu.SemaphoreType.DMA((2, CHUNKS)), pltpu.SemaphoreType.DMA],
        compiler_params=params(),
        cost_estimate=cost(4),
        name="face_rows",
    )(
        pltpu.with_memory_space_constraint(owner_count, pltpu.HBM),
        pltpu.with_memory_space_constraint(fine_state, pltpu.HBM),
        pltpu.with_memory_space_constraint(cotangent, pltpu.HBM),
    )
    got_a = trade(inner, "inner")
    got_b = relay_out(outer, got_a)

    meta, index, xs, zs, mats, table = pl.pallas_call(
        prepare_kernel,
        in_specs=[SMEM()] * 2 + [VMEM()] * 8,
        out_specs=[SMEM()] + [VMEM()] * 5,
        out_shape=[shape_of((META,), jnp.int32), shape_of((12, SLOTS), jnp.int32)]
        + [shape_of(field), shape_of(field), shape_of((2, C, 7 * C)), shape_of((BASE_B, C, 128))],
        compiler_params=params(),
        cost_estimate=cost(4),
        name="prepare",
    )(
        owner_count, octant, neighbour.T, level_tag.T, got_a, fine_state, cotangent, sel,
        weight_in, weight_out,
    )
    got_c, meta = relay_in(got_b, meta)

    taps_a, taps_b, hidden, slope, grad_merged, par, pin, pout = pl.pallas_call(
        fine_kernel,
        in_specs=[SMEM()] * 2 + [VMEM()] * 8,
        out_specs=[VMEM()] * 8,
        out_shape=[shape_of(stack), shape_of(stack), shape_of(field), shape_of(field)]
        + [shape_of(field), shape_of(par_rows), shape_of(far), shape_of(far)],
        scratch_shapes=[
            pltpu.VMEM(table_shape, BF),
            pltpu.VMEM(coef_shape, BF),
            picked_scratch,
            pltpu.VMEM((NPAR * 8 + 8, C, 128), BF),
            pltpu.VMEM((2, 16, C, 128), BF),
        ],
        compiler_params=params(),
        cost_estimate=cost(8),
        name="fine_level",
    )(meta, index, xs, zs, table, got_b, got_c, mats, spread, rest)
    child_out = trade(pout, "outer")
    child_in = trade(pin, "inner")

    mats, dw_part, means = pl.pallas_call(
        window_kernel,
        in_specs=[VMEM()] * 6,
        out_specs=[VMEM()] * 3,
        out_shape=[shape_of((4, C, 7 * C)), shape_of((7 * C, C), F32)]
        + [shape_of((SLOTS, 7 * C, 128))],
        compiler_params=params(),
        cost_estimate=cost(3),
        name="window",
    )(hidden, taps_b, rest, weight_in, weight_out, weight_coarse)

    merged, grad_pre, sums, inner, outer = pl.pallas_call(
        merge_kernel,
        in_specs=[SMEM()] + [VMEM()] * 13,
        out_specs=[VMEM()] * 5,
        out_shape=[shape_of(field), shape_of(field), shape_of((DWR, C, 128))]
        + [shape_of((NEAR + DWR, C, 128)), shape_of(near)],
        scratch_shapes=[
            pltpu.VMEM((NPAR * 8 + 8, C, 128), BF),
            pltpu.VMEM((NPAR, 7 * C, CELLS), BF),
            pltpu.VMEM((NPAR * 8 + 8, C, 128), BF),
            pltpu.VMEM((PB, C, 128), BF),
        ]
        + rows_scratch
        + [pltpu.VMEM((7 * C, 128), F32)],
        compiler_params=params(),
        cost_estimate=cost(9),
        name="coarse_and_merge",
    )(
        meta, taps_a, means, dw_part, hidden, slope, grad_merged, par, child_in, child_out, mats,
        place, up, sel,
    )
    got_a = trade(inner, "inner")
    got_b = relay_out(outer, got_a)
    sums = add(sums, got_a[NEAR:])
    sums = add(sums, swap(sums, 2))

    table = pl.pallas_call(
        second_table_kernel,
        in_specs=[VMEM()] * 4,
        out_specs=VMEM(),
        out_shape=shape_of((BASE_B, C, 128)),
        compiler_params=params(),
        cost_estimate=cost(2),
        name="face_table",
    )(merged, grad_pre, sel, got_a)
    got_c, table = relay_in(got_b, table)

    last_scratch = [
        picked_scratch,
        pltpu.VMEM((PB, 7 * C, CELLS), BF),
        pltpu.VMEM((PB, 7 * C, CELLS), BF),
        pltpu.VMEM((PB, C, CELLS), BF),
        pltpu.VMEM((PB, C, CELLS), BF),
        pltpu.SemaphoreType.DMA((2,)),
    ]
    fixed = (index, merged, grad_pre, xs, zs, mats, spread)
    partner = swap(sums, 6)
    table, coef, output, grad_state = pl.pallas_call(
        first_final_kernel,
        in_specs=[SMEM()] + [VMEM()] * 9,
        out_specs=[VMEM(), VMEM(), HBM(), HBM()],
        out_shape=[shape_of(table_shape), shape_of(coef_shape), shape_of(field), shape_of(field)],
        scratch_shapes=last_scratch,
        compiler_params=params(),
        cost_estimate=cost(2),
        name="last_level",
    )(*fixed, table, got_b, got_c)
    sums = add(sums, partner)
    for step, mask in ((1, 8), (2, 24), (3, 32)):
        sums, coef = lax.optimization_barrier((sums, coef))
        partner = swap(sums, mask)
        output, grad_state = pl.pallas_call(
            functools.partial(next_final_kernel, step),
            in_specs=[SMEM()] + [VMEM()] * 8 + [HBM(), HBM()],
            out_specs=[HBM(), HBM()],
            out_shape=[shape_of(field), shape_of(field)],
            input_output_aliases={9: 0, 10: 1},
            scratch_shapes=last_scratch,
            compiler_params=params(),
            cost_estimate=cost(2),
            name="last_level",
        )(*fixed, table, coef, output, grad_state)
        sums = add(sums, partner)
        sums, output = lax.optimization_barrier((sums, output))
    partner = swap(sums, 96)

    scale = 1.0 / math.sqrt(float(devices * SLOTS * CELLS))
    mat = shape_of((7, C, C), F32)
    grads = pl.pallas_call(
        functools.partial(weights_kernel, scale),
        in_specs=[VMEM()] * 2,
        out_specs=[VMEM()] * 3,
        compiler_params=params(),
        out_shape=[mat, mat, mat],
        cost_estimate=cost(1),
        name="weight_sums",
    )(sums, partner)
    return (output, grad_state, *grads)


def solution(mesh):
    in_specs = (
        P("patch", None, None),
        P(),
        P(),
        P(),
        P("patch", None, None),
        P(),
        P("patch", None),
        P("patch", None),
        P("patch"),
    )
    out_specs = (P("patch", None, None), P("patch", None, None), P(), P(), P())
    return jax.shard_map(
        on_device, mesh=mesh, in_specs=in_specs, out_specs=out_specs, check_vma=False
    )
```

```python
import functools
import math

import numpy as np
import jax
import jax.numpy as jnp
from jax import lax
from jax.experimental import pallas as pl
from jax.experimental.pallas import tpu as pltpu
from jax.sharding import PartitionSpec as P

BF = jnp.bfloat16
F32 = jnp.float32
EDGE = 8
CELLS = 512
SLOTS = 32
C = 32
PB = 8
STEPS = SLOTS // PB
NPAR = 5
STRIDES = (64, 8, 1)
MORTON = (3, 8, 16)
ROW0 = (24, 16, 0)
NEAR = 27
FAR = 8
BASE_A = 6 * SLOTS
BASE_B = BASE_A + NEAR
BASE_C = BASE_B + NEAR + FAR
ROWS = BASE_C + FAR
VMEM_LIMIT = 14 * 1024 * 1024
FULL_LIMIT = 60 * 1024 * 1024
DST, LEAD, TRAIL, SCAL = 0, 32, 64, 96
N_COUNT, N_ODD, N_LAST, N_OWNED = SCAL, SCAL + 1, SCAL + 2, SCAL + 3
META = 128
IN_F, OUT_B = range(2)
OUT_F, IN_B, CO_F, CO_B = range(4)
CHUNKS = 8
DWR = 7


def cell_coords():
    ids = np.arange(CELLS)
    return [ids // 64, ids // 8 % 8, ids % 8]


def face_cells(face):
    coords = cell_coords()
    keep = coords[face // 2] == (EDGE - 1 if face % 2 else 0)
    return np.nonzero(keep)[0]


def constants():
    sel = np.zeros((3, 2, CELLS, 256), np.float32)
    spread = np.zeros((2, 256, 2 * CELLS), np.float32)
    for face in range(6):
        for j, cell in enumerate(face_cells(face)):
            for kind in range(2):
                col = (face % 2) * 128 + kind * 64 + j
                sel[face // 2, kind, cell, col] = 1
                if face >= 2:
                    spread[face // 2 - 1, col, kind * CELLS + cell] = 1
    c0, c1, c2 = cell_coords()
    group = (c0 // 2) * 16 + (c1 // 2) * 4 + c2 // 2
    rest = np.zeros((2, CELLS, 128), np.float32)
    up = np.zeros((128, 2 * CELLS), np.float32)
    for cell in range(CELLS):
        rest[0, cell, group[cell]] = 0.125
        rest[1, cell, 64 + group[cell]] = 1
        up[group[cell], cell] = 1
        up[64 + group[cell], CELLS + cell] = 1
    place = np.zeros((256, 2 * CELLS), np.float32)
    for o2 in range(2):
        for a in range(64):
            cell = (a // 16) * 64 + (a // 4 % 4) * 8 + a % 4 + 4 * o2
            place[128 * o2 + a, cell] = 1
            place[128 * o2 + 64 + a, CELLS + cell] = 1
    as_bf = lambda item: np.asarray(item, jnp.bfloat16)
    return (
        as_bf(sel.reshape(6, CELLS, 256)),
        as_bf(spread),
        as_bf(rest),
        as_bf(up),
        as_bf(place),
    )


def dot(a, b):
    return jnp.dot(a, b, preferred_element_type=F32)


def dot_nt(a, b):
    return lax.dot_general(a, b, (((1,), (1,)), ((), ())), preferred_element_type=F32)


def coord_of(dim):
    lane = lax.broadcasted_iota(jnp.int32, (16, CELLS), 1)
    return (lane // STRIDES[dim]) % EDGE


def on_face(face):
    edge = EDGE - 1 if face % 2 else 0
    return jnp.where(coord_of(face // 2) == edge, 1.0, 0.0)


def halves(field):
    return field.reshape(field.shape[0] // 16, 16, CELLS)


def times(field, mask):
    return (halves(field) * mask[None]).reshape(field.shape)


def toward(field, face):
    stride = STRIDES[face // 2]
    shift = CELLS - stride if face % 2 else stride
    return pltpu.roll(field, shift, 1)


def send_rows(count, odd, v_ref, y_ref, sel_ref, v_rows, y_rows, sides, inner_ref, outer_ref):
    for side in range(2):
        for dim in (2, 1, 0):
            depth = MORTON[dim]
            for i in range(depth):
                slot = jnp.clip(count - depth + i, 0, SLOTS - 1) if side else i
                v_rows[i] = v_ref[slot]
                y_rows[i] = y_ref[slot]
            cols = slice(side * 128, side * 128 + 128)
            layers = dot(v_rows[:depth].reshape(depth * C, CELLS), sel_ref[2 * dim, :, cols])
            layers += dot(y_rows[:depth].reshape(depth * C, CELLS), sel_ref[2 * dim + 1, :, cols])
            layers = layers.astype(BF).reshape(depth, C, 128)
            if dim == 2 and side:
                sides[side, 0:8] = layers[8:16]
                sides[side, 8:16] = layers[0:8]
            else:
                sides[side, ROW0[dim] : ROW0[dim] + depth] = layers
    inner_ref[...] = sides[1 - odd]
    outer_ref[...] = sides[odd]


def make_selection(sel_ref):
    cell = lax.broadcasted_iota(jnp.int32, (CELLS, 256), 0)
    lane = lax.broadcasted_iota(jnp.int32, (CELLS, 256), 1)
    at = lane % 64
    edge = jnp.where(lane < 128, 0, EDGE - 1)
    first_half = lane % 128 < 64
    for dim in range(3):
        if dim == 0:
            want = edge * 64 + at
        elif dim == 1:
            want = at // 8 * 64 + edge * 8 + at % 8
        else:
            want = at * 8 + edge
        hit = cell == want
        sel_ref[2 * dim] = jnp.where(hit & first_half, 1.0, 0.0).astype(BF)
        sel_ref[2 * dim + 1] = jnp.where(hit & ~first_half, 1.0, 0.0).astype(BF)


def layers_kernel(
    counts_hbm, x_hbm, z_hbm, inner_ref, outer_ref,
    v_rows, y_rows, sides, x_ref, z_ref, sel_ref, counts, sems, counts_sem,
):
    rank = lax.axis_index("patch")
    size = SLOTS // CHUNKS
    copies = [pltpu.make_async_copy(counts_hbm, counts, counts_sem)]
    for k in range(CHUNKS):
        part = pl.ds(k * size, size)
        copies.append(pltpu.make_async_copy(x_hbm.at[part], x_ref.at[part], sems.at[0, k]))
        copies.append(pltpu.make_async_copy(z_hbm.at[part], z_ref.at[part], sems.at[1, k]))
    for copy in copies:
        copy.start()
    make_selection(sel_ref)
    for copy in copies:
        copy.wait()
    send_rows(
        counts[rank], rank % 2, x_ref, z_ref, sel_ref, v_rows, y_rows, sides, inner_ref, outer_ref
    )


def fill_table(v_ref, y_ref, sel_ref, table):
    for dim in range(3):
        layers = dot(v_ref[...].reshape(SLOTS * C, CELLS), sel_ref[2 * dim])
        layers += dot(y_ref[...].reshape(SLOTS * C, CELLS), sel_ref[2 * dim + 1])
        layers = layers.astype(BF)
        for high in range(2):
            face = 2 * dim + high
            table[face * SLOTS : (face + 1) * SLOTS] = layers[
                :, high * 128 : high * 128 + 128
            ].reshape(SLOTS, C, 128)


def fill_mats(mats, weights):
    for k, (weight, turned) in enumerate(weights):
        for f in range(7):
            one = weight[f].astype(F32)
            mats[k, :, f * C : (f + 1) * C] = (one.T if turned else one).astype(BF)


def prepare_kernel(
    counts, octant, neighbour, level_tag,
    got_ref, x_ref, z_ref, sel_ref, w_in, w_out,
    meta, index, xs, zs, mats, table,
):
    rank = lax.axis_index("patch")
    odd = rank % 2

    def count_at(device):
        here = counts[jnp.clip(device, 0, counts.shape[0] - 1)]
        return jnp.where(device < 0, 0, here)

    first = lax.fori_loop(0, rank, lambda d, s: s + counts[d], jnp.int32(0))
    count = count_at(rank)
    count_1 = count_at(rank - 1)
    count_2 = count_at(rank - 2)
    stop = first + count
    meta[N_COUNT] = count
    meta[N_ODD] = odd
    meta[N_LAST] = jnp.where(stop % 8 != 0, stop // 8 - first // 8, NPAR)
    meta[N_OWNED] = jnp.where(first % 8 == 0, 1, 0)
    lead_count = (8 - first % 8) % 8
    for p in range(SLOTS):
        live = p < count
        parent = (first % 8 + p) // 8
        o = jnp.clip(octant[p], 0, 7)
        meta[DST + p] = jnp.where(live, parent * 8 + o, NPAR * 8)
        meta[LEAD + p] = jnp.where(live & (p < lead_count), o, 8)
        meta[TRAIL + p] = jnp.where(live & (p >= count - stop % 8), o, 8)

    near_left = jnp.where(odd == 1, BASE_A, BASE_B)
    near_right = jnp.where(odd == 1, BASE_B, BASE_A)
    far_left = jnp.where(odd == 1, BASE_C, BASE_B + NEAR)
    far_right = jnp.where(odd == 1, BASE_B + NEAR, BASE_C)
    face = lax.broadcasted_iota(jnp.int32, (6, SLOTS), 0)
    own = lax.broadcasted_iota(jnp.int32, (6, SLOTS), 1)
    depth = jnp.where(face < 2, MORTON[0], jnp.where(face < 4, MORTON[1], MORTON[2]))
    row0 = jnp.where(face < 2, ROW0[0], jnp.where(face < 4, ROW0[1], ROW0[2]))
    high = (face & 1) == 1
    other = neighbour[...]
    away = (other >> 5) - rank
    slot = other & 31
    back = slot - (count_1 - depth)
    left = jnp.where(face >= 4, (back + 8) & 15, row0 + back) + near_left
    near = jnp.where(high, near_right + row0 + slot, left)
    far = jnp.where(high, far_right + slot, far_left + slot - (count_2 - 8))
    row = jnp.where(away == 0, (face ^ 1) * SLOTS + slot, near)
    row = jnp.where((away == 2) | (away == -2), far, row)
    row = jnp.where(level_tag[...] == 1, face * SLOTS + own, row)
    index[0:6] = jnp.clip(row, 0, ROWS - 1)
    index[6:12] = level_tag[...]

    fill_mats(mats, ((w_in, True), (w_out, False)))
    for p in range(SLOTS):
        live = (p < count).astype(F32)
        xs[p] = (x_ref[p].astype(F32) * live).astype(BF)
        zs[p] = (z_ref[p].astype(F32) * live).astype(BF)
    fill_table(xs, zs, sel_ref, table)
    table[BASE_A:BASE_B] = got_ref[...]


def window_kernel(hidden_ref, tb_ref, rest_ref, w_in, w_out, w_co, mats, dw_ref, means_ref):
    fill_mats(mats, ((w_out, True), (w_in, False), (w_co, True), (w_co, False)))
    dw_ref[...] = jnp.zeros_like(dw_ref)

    @pl.loop(0, STEPS)
    def _(step):
        dw = jnp.zeros((7 * C, C), F32)
        for p in range(PB):
            here = step * PB + p
            dw += dot_nt(tb_ref[here], hidden_ref[here])
            means_ref[here] = dot(tb_ref[here], rest_ref[0]).astype(BF)
        dw_ref[...] += dw


def table_kernel(v_ref, y_ref, sel_ref, table):
    fill_table(v_ref, y_ref, sel_ref, table)


def join_table(parts, coef, table):
    start = 0
    for part in parts:
        size = part.shape[0]
        table[start : start + size] = part[...]
        start += size
    for dim in range(3):
        low, high = on_face(2 * dim), on_face(2 * dim + 1)
        for t_low in range(2):
            for t_high in range(2):
                row = dim * 4 + t_low * 2 + t_high
                coef[row, 0] = (low * (1 - t_low) + high * t_high).astype(BF)
                coef[row, 1] = (high * (1 - t_high) + low * t_low).astype(BF)


def block_taps(start, index, v_ref, y_ref, spread_ref, table, coef, picked, ta, tb):
    for dim in range(3):
        low, high = 2 * dim, 2 * dim + 1
        edges = [on_face(low), on_face(high)]
        inside = [(1.0 - edge).astype(BF) for edge in edges]
        edges = [edge.astype(BF) for edge in edges]
        if dim:
            for p in range(PB):
                picked[p, :, 0:128] = table[index[low, start + p]]
                picked[p, :, 128:256] = table[index[high, start + p]]
            spread = dot(picked[...].reshape(PB * C, 256), spread_ref[dim - 1]).astype(BF)
        for p in range(PB):
            if dim:
                rows = slice(p * C, (p + 1) * C)
                v_edge = spread[rows, :CELLS]
                y_edge = spread[rows, CELLS:]
            else:
                r_low = table[index[low, start + p]]
                r_high = table[index[high, start + p]]
                blank = jnp.zeros((C, 256), BF)
                v_edge = jnp.concatenate([r_low, blank, pltpu.roll(r_high, 64, 1)], axis=1)
                y_edge = jnp.concatenate([pltpu.roll(r_low, 64, 1), blank, r_high], axis=1)
            field = v_ref[p]
            other = y_ref[p]
            if dim == 0:
                ta[p, 0:C] = field
                tb[p, 0:C] = other
            row = (
                dim * 4
                + index[6 + low, start + p] * 2
                + index[6 + high, start + p]
            )
            for k, face in enumerate((low, high)):
                ta[p, C * (face + 1) : C * (face + 2)] = jnp.where(
                    edges[k][None] > 0, halves(v_edge), halves(toward(field, face))
                ).reshape(C, CELLS)
                back = face ^ 1
                tb[p, C * (back + 1) : C * (back + 2)] = times(
                    toward(other, face), inside[k]
                ) + times(y_edge, coef[row, k])


def silu_pair(pre):
    sigma = 1.0 / (1.0 + jnp.exp(-pre))
    return pre * sigma, sigma * (1.0 + pre * (1.0 - sigma))


def fine_kernel(
    meta, index, xs, zs, t_ref, b_ref, c_ref, mats, spread_ref, rest_ref,
    ta_ref, tb_ref, hidden_ref, slope_ref, gm_ref, par_ref, inner_ref, outer_ref,
    table, coef, picked, par, ends,
):
    join_table((t_ref, b_ref, c_ref), coef, table)
    par[...] = jnp.zeros_like(par)
    ends[...] = jnp.zeros_like(ends)

    @pl.loop(0, STEPS)
    def _(step):
        start = step * PB
        x_at, z_at, ta, tb, hidden_at, slope_at, gm_at = [
            item.at[pl.ds(start, PB)]
            for item in (xs, zs, ta_ref, tb_ref, hidden_ref, slope_ref, gm_ref)
        ]
        block_taps(start, index, x_at, z_at, spread_ref, table, coef, picked, ta, tb)
        for p in range(PB):
            hidden, slope = silu_pair(dot(mats[IN_F], ta[p]))
            hidden_at[p] = hidden.astype(BF)
            slope_at[p] = slope.astype(BF)
            gm_at[p] = dot(mats[OUT_B], tb[p]).astype(BF)
        child = dot(hidden_at[...].reshape(PB * C, CELLS), rest_ref[0])
        child += dot(gm_at[...].reshape(PB * C, CELLS), rest_ref[1])
        child = child.astype(BF)
        for p in range(PB):
            row = child[p * C : (p + 1) * C]
            par[meta[DST + start + p]] = row
            ends[0, meta[LEAD + start + p]] = row
            ends[1, meta[TRAIL + start + p]] = row

    par_ref[...] = par[: NPAR * 8]
    odd = meta[N_ODD]
    inner_ref[...] = ends[1 - odd, 0:8]
    outer_ref[...] = ends[odd, 0:8]


def coarse_level(meta, par_ref, inner_ref, outer_ref, wa, wb, place_ref, par, taps, up_rows, dw_ref):
    par[: NPAR * 8] = par_ref[...]
    par[NPAR * 8 :] = jnp.zeros((8, C, 128), BF)
    last = meta[N_LAST] * 8
    odd = meta[N_ODD]
    inner_at = jnp.where(odd == 1, 0, last)
    outer_at = jnp.where(odd == 1, last, 0)
    for o in range(8):
        par[inner_at + o] = par[inner_at + o] + inner_ref[o]
    for o in range(8):
        par[outer_at + o] = par[outer_at + o] + outer_ref[o]

    rows = NPAR * C
    both = jnp.zeros((rows, 2 * CELLS), BF)
    for o in range(0, 8, 2):
        lhs = jnp.concatenate(
            [
                jnp.concatenate([par[q * 8 + o], par[q * 8 + o + 1]], axis=1)
                for q in range(NPAR)
            ],
            axis=0,
        )
        put = dot(lhs, place_ref[...]).astype(BF)
        shift = (o // 4) * 256 + (o // 2 % 2) * 32
        if shift:
            put = jnp.concatenate(
                [
                    pltpu.roll(put[:, :CELLS], shift, 1),
                    pltpu.roll(put[:, CELLS:], shift, 1),
                ],
                axis=1,
            )
        both += put
    field = both[:, :CELLS]
    cotan = both[:, CELLS:].astype(F32)
    edges = [on_face(face).astype(BF) for face in range(6)]
    inside = [(1.0 - on_face(face)).astype(BF) for face in range(6)]

    def store(face, value):
        taps[:, C * face : C * (face + 1)] = value.reshape(NPAR, C, CELLS)

    store(0, field)
    for face in range(6):
        store(face + 1, times(toward(field, face), inside[face]) + times(field, edges[face]))
    pre = jnp.concatenate([dot(wa, taps[q]) for q in range(NPAR)], axis=0)
    act, slope = silu_pair(pre)
    act = act.astype(BF)
    grad = (cotan * slope).astype(BF)
    dw = jnp.zeros((7 * C, C), F32)
    for q in range(NPAR):
        part = dot_nt(taps[q], grad[q * C : (q + 1) * C])
        if q == 0:
            part = part * meta[N_OWNED].astype(F32)
        dw += part
    store(0, grad)
    for face in range(6):
        back = face ^ 1
        store(face + 1, times(toward(grad, back), inside[back]) + times(grad, edges[face]))
    down = jnp.concatenate([dot(wb, taps[q]) for q in range(NPAR)], axis=0).astype(BF)
    for o in range(0, 8, 2):
        one, two = act, down
        shift = (o // 4) * 256 + (o // 2 % 2) * 32
        if shift:
            one = pltpu.roll(act, CELLS - shift, 1)
            two = pltpu.roll(down, CELLS - shift, 1)
        got = dot_nt(one, place_ref[:, :CELLS]) + dot_nt(two, place_ref[:, CELLS:])
        got = got.astype(BF)
        for q in range(NPAR):
            up_rows[q * 8 + o] = got[q * C : (q + 1) * C, :128]
            up_rows[q * 8 + o + 1] = got[q * C : (q + 1) * C, 128:]
    up_rows[NPAR * 8] = jnp.zeros((C, 128), BF)
    dw_ref[:, 2 * C : 3 * C] = dw


def merge_kernel(
    meta,
    ta_ref, means_ref, dw0_ref, hidden_ref, slope_ref, gm_ref, par_ref, pin_ref, pout_ref,
    mats, place_ref, up_ref, sel_ref,
    merged_ref, gpa_ref, sum_ref, inner_ref, outer_ref,
    par, taps, up_rows, picked, v_rows, y_rows, sides, dw_ref,
):
    dw_ref[...] = jnp.zeros_like(dw_ref)
    dw_ref[:, C : 2 * C] = dw0_ref[...]
    coarse_level(
        meta, par_ref, pin_ref, pout_ref, mats[CO_F], mats[CO_B],
        place_ref, par, taps, up_rows, dw_ref,
    )

    @pl.loop(0, STEPS)
    def _(step):
        start = step * PB
        for p in range(PB):
            picked[p] = up_rows[meta[DST + start + p]]
        spread = dot(picked[...].reshape(PB * C, 128), up_ref[...])
        dw_in = jnp.zeros((7 * C, C), F32)
        dw_out = jnp.zeros((7 * C, C), F32)
        for p in range(PB):
            rows = slice(p * C, (p + 1) * C)
            here = start + p
            merged = (hidden_ref[here].astype(F32) + spread[rows, :CELLS]).astype(BF)
            grad = gm_ref[here].astype(F32) + spread[rows, CELLS:] * 0.125
            gpa = (grad * slope_ref[here].astype(F32)).astype(BF)
            merged_ref[here] = merged
            gpa_ref[here] = gpa
            dw_in += dot_nt(ta_ref[here], gpa)
            dw_out += dot_nt(means_ref[here], picked[p])
        dw_ref[:, 0:C] += dw_in
        dw_ref[:, C : 2 * C] += dw_out * 8.0

    send_rows(
        meta[N_COUNT], meta[N_ODD], merged_ref, gpa_ref, sel_ref,
        v_rows, y_rows, sides, inner_ref.at[0:NEAR], outer_ref,
    )
    rounded = dw_ref[...].astype(BF).reshape(DWR, C, 128)
    sum_ref[...] = rounded
    inner_ref[NEAR : NEAR + DWR] = rounded


def second_table_kernel(v_ref, y_ref, sel_ref, got_ref, table):
    fill_table(v_ref, y_ref, sel_ref, table)
    table[BASE_A:BASE_B] = got_ref[0:NEAR]


def final_body(step, index, v_ref, y_ref, xs, zs, mats, spread_ref, table, coef, out_hbm, gs_hbm,
               picked, ta, tb, out_ref, gs_ref, sems):
    start = step * PB
    part = pl.ds(start, PB)
    block_taps(
        start, index, v_ref.at[part], y_ref.at[part], spread_ref, table, coef, picked, ta, tb
    )
    for p in range(PB):
        out_ref[p] = (xs[start + p].astype(F32) + dot(mats[OUT_F], ta[p])).astype(BF)
        gs_ref[p] = (zs[start + p].astype(F32) + dot(mats[IN_B], tb[p])).astype(BF)
    copies = [
        pltpu.make_async_copy(out_ref, out_hbm.at[part], sems.at[0]),
        pltpu.make_async_copy(gs_ref, gs_hbm.at[part], sems.at[1]),
    ]
    for copy in copies:
        copy.start()
    for copy in copies:
        copy.wait()


def first_final_kernel(
    index, v_ref, y_ref, xs, zs, mats, spread_ref, t_ref, b_ref, c_ref,
    table, coef, out_hbm, gs_hbm, *scratch,
):
    join_table((t_ref, b_ref, c_ref), coef, table)
    final_body(0, index, v_ref, y_ref, xs, zs, mats, spread_ref, table, coef, out_hbm, gs_hbm,
               *scratch)


def next_final_kernel(
    step, index, v_ref, y_ref, xs, zs, mats, spread_ref, table, coef, out_in, gs_in,
    out_hbm, gs_hbm, *scratch,
):
    final_body(step, index, v_ref, y_ref, xs, zs, mats, spread_ref, table, coef, out_hbm, gs_hbm,
               *scratch)


def weights_kernel(scale, one_ref, two_ref, in_ref, out_ref, co_ref):
    for f in range(7):
        total = (one_ref[f].astype(F32) + two_ref[f].astype(F32)) * scale
        in_ref[f] = total[:, 0:C]
        out_ref[f] = total[:, C : 2 * C].T
        co_ref[f] = total[:, 2 * C : 3 * C]


SMEM = functools.partial(pl.BlockSpec, memory_space=pltpu.SMEM)


VMEM = functools.partial(pl.BlockSpec, memory_space=pltpu.VMEM)
HBM = functools.partial(pl.BlockSpec, memory_space=pltpu.HBM)


def params(limit=VMEM_LIMIT):
    return pltpu.CompilerParams(vmem_limit_bytes=limit)


def shape_of(shape, dtype=BF):
    return jax.ShapeDtypeStruct(shape, dtype)


def cost(micros):
    return pl.CostEstimate(
        flops=int(micros * 1e6), bytes_accessed=int(micros * 3.0e6), transcendentals=0
    )


def pairs(kind, devices):
    if kind == "inner":
        links = [(2 * c, 2 * c + 1) for c in range(devices // 2)]
    else:
        links = [(2 * c + 1, 2 * c + 2) for c in range(devices // 2 - 1)]
    return links + [(b, a) for a, b in links]


def trade(block, kind):
    return lax.ppermute(block, "patch", pairs(kind, lax.axis_size("patch")))


def relay_out(outer, got_a):
    return trade(jnp.concatenate([outer, got_a[:FAR]], axis=0), "outer")


def relay_in(got_b, first):
    got_b, first = lax.optimization_barrier((got_b, first))
    return trade(got_b[:FAR], "inner"), first


def add(one, two):
    return (one.astype(F32) + two.astype(F32)).astype(BF)


def swap(block, mask):
    devices = lax.axis_size("patch")
    return lax.ppermute(block, "patch", [(i, i ^ mask) for i in range(devices)])


def on_device(
    fine_state, weight_in, weight_out, weight_coarse, cotangent,
    owner_count, neighbour, level_tag, octant,
):
    devices = lax.axis_size("patch")
    sel, spread, rest, up, place = [jnp.asarray(item) for item in constants()]

    field = (SLOTS, C, CELLS)
    stack = (SLOTS, 7 * C, CELLS)
    near = (NEAR, C, 128)
    far = (FAR, C, 128)
    par_rows = (NPAR * 8, C, 128)
    sel_shape = (6, CELLS, 256)
    rows_scratch = [pltpu.VMEM((16, C, CELLS), BF)] * 2 + [pltpu.VMEM((2, NEAR, C, 128), BF)]
    table_shape = (ROWS, C, 128)
    coef_shape = (12, 2, 16, CELLS)
    picked_scratch = pltpu.VMEM((PB, C, 256), BF)

    inner, outer = pl.pallas_call(
        layers_kernel,
        in_specs=[HBM()] * 3,
        out_specs=[VMEM()] * 2,
        out_shape=[shape_of(near), shape_of(near)],
        scratch_shapes=rows_scratch
        + [pltpu.VMEM(field, BF), pltpu.VMEM(field, BF), pltpu.VMEM(sel_shape, BF)]
        + [pltpu.SMEM(owner_count.shape, jnp.int32)]
        + [pltpu.SemaphoreType.DMA((2, CHUNKS)), pltpu.SemaphoreType.DMA],
        compiler_params=params(),
        cost_estimate=cost(4),
        name="face_rows",
    )(
        pltpu.with_memory_space_constraint(owner_count, pltpu.HBM),
        pltpu.with_memory_space_constraint(fine_state, pltpu.HBM),
        pltpu.with_memory_space_constraint(cotangent, pltpu.HBM),
    )
    got_a = trade(inner, "inner")
    got_b = relay_out(outer, got_a)

    meta, index, xs, zs, mats, table = pl.pallas_call(
        prepare_kernel,
        in_specs=[SMEM()] * 2 + [VMEM()] * 8,
        out_specs=[SMEM()] + [VMEM()] * 5,
        out_shape=[shape_of((META,), jnp.int32), shape_of((12, SLOTS), jnp.int32)]
        + [shape_of(field), shape_of(field), shape_of((2, C, 7 * C)), shape_of((BASE_B, C, 128))],
        compiler_params=params(),
        cost_estimate=cost(4),
        name="prepare",
    )(
        owner_count, octant, neighbour.T, level_tag.T, got_a, fine_state, cotangent, sel,
        weight_in, weight_out,
    )
    got_c, meta = relay_in(got_b, meta)

    taps_a, taps_b, hidden, slope, grad_merged, par, pin, pout = pl.pallas_call(
        fine_kernel,
        in_specs=[SMEM()] * 2 + [VMEM()] * 8,
        out_specs=[VMEM()] * 8,
        out_shape=[shape_of(stack), shape_of(stack), shape_of(field), shape_of(field)]
        + [shape_of(field), shape_of(par_rows), shape_of(far), shape_of(far)],
        scratch_shapes=[
            pltpu.VMEM(table_shape, BF),
            pltpu.VMEM(coef_shape, BF),
            picked_scratch,
            pltpu.VMEM((NPAR * 8 + 8, C, 128), BF),
            pltpu.VMEM((2, 16, C, 128), BF),
        ],
        compiler_params=params(),
        cost_estimate=cost(8),
        name="fine_level",
    )(meta, index, xs, zs, table, got_b, got_c, mats, spread, rest)
    child_out = trade(pout, "outer")
    child_in = trade(pin, "inner")

    mats, dw_part, means = pl.pallas_call(
        window_kernel,
        in_specs=[VMEM()] * 6,
        out_specs=[VMEM()] * 3,
        out_shape=[shape_of((4, C, 7 * C)), shape_of((7 * C, C), F32)]
        + [shape_of((SLOTS, 7 * C, 128))],
        compiler_params=params(),
        cost_estimate=cost(3),
        name="window",
    )(hidden, taps_b, rest, weight_in, weight_out, weight_coarse)

    merged, grad_pre, sums, inner, outer = pl.pallas_call(
        merge_kernel,
        in_specs=[SMEM()] + [VMEM()] * 13,
        out_specs=[VMEM()] * 5,
        out_shape=[shape_of(field), shape_of(field), shape_of((DWR, C, 128))]
        + [shape_of((NEAR + DWR, C, 128)), shape_of(near)],
        scratch_shapes=[
            pltpu.VMEM((NPAR * 8 + 8, C, 128), BF),
            pltpu.VMEM((NPAR, 7 * C, CELLS), BF),
            pltpu.VMEM((NPAR * 8 + 8, C, 128), BF),
            pltpu.VMEM((PB, C, 128), BF),
        ]
        + rows_scratch
        + [pltpu.VMEM((7 * C, 128), F32)],
        compiler_params=params(),
        cost_estimate=cost(9),
        name="coarse_and_merge",
    )(
        meta, taps_a, means, dw_part, hidden, slope, grad_merged, par, child_in, child_out, mats,
        place, up, sel,
    )
    got_a = trade(inner, "inner")
    got_b = relay_out(outer, got_a)
    sums = add(sums, got_a[NEAR:])
    sums = add(sums, swap(sums, 2))

    table = pl.pallas_call(
        second_table_kernel,
        in_specs=[VMEM()] * 4,
        out_specs=VMEM(),
        out_shape=shape_of((BASE_B, C, 128)),
        compiler_params=params(),
        cost_estimate=cost(2),
        name="face_table",
    )(merged, grad_pre, sel, got_a)
    got_c, table = relay_in(got_b, table)

    last_scratch = [
        picked_scratch,
        pltpu.VMEM((PB, 7 * C, CELLS), BF),
        pltpu.VMEM((PB, 7 * C, CELLS), BF),
        pltpu.VMEM((PB, C, CELLS), BF),
        pltpu.VMEM((PB, C, CELLS), BF),
        pltpu.SemaphoreType.DMA((2,)),
    ]
    fixed = (index, merged, grad_pre, xs, zs, mats, spread)
    sums, got_c = lax.optimization_barrier((add(sums, swap(sums, 6)), got_c))
    partner = swap(sums, 8)
    table, coef, output, grad_state = pl.pallas_call(
        first_final_kernel,
        in_specs=[SMEM()] + [VMEM()] * 9,
        out_specs=[VMEM(), VMEM(), HBM(), HBM()],
        out_shape=[shape_of(table_shape), shape_of(coef_shape), shape_of(field), shape_of(field)],
        scratch_shapes=last_scratch,
        compiler_params=params(),
        cost_estimate=cost(2),
        name="last_level",
    )(*fixed, table, got_b, got_c)
    for step, mask in ((1, 24), (2, 32), (3, 96)):
        sums, coef, output = lax.optimization_barrier((add(sums, partner), coef, output))
        partner = swap(sums, mask)
        output, grad_state = pl.pallas_call(
            functools.partial(next_final_kernel, step),
            in_specs=[SMEM()] + [VMEM()] * 8 + [HBM(), HBM()],
            out_specs=[HBM(), HBM()],
            out_shape=[shape_of(field), shape_of(field)],
            input_output_aliases={9: 0, 10: 1},
            scratch_shapes=last_scratch,
            compiler_params=params(),
            cost_estimate=cost(2),
            name="last_level",
        )(*fixed, table, coef, output, grad_state)

    scale = 1.0 / math.sqrt(float(devices * SLOTS * CELLS))
    mat = shape_of((7, C, C), F32)
    grads = pl.pallas_call(
        functools.partial(weights_kernel, scale),
        in_specs=[VMEM()] * 2,
        out_specs=[VMEM()] * 3,
        compiler_params=params(),
        out_shape=[mat, mat, mat],
        cost_estimate=cost(1),
        name="weight_sums",
    )(sums, partner)
    return (output, grad_state, *grads)


def solution(mesh):
    in_specs = (
        P("patch", None, None),
        P(),
        P(),
        P(),
        P("patch", None, None),
        P(),
        P("patch", None),
        P("patch", None),
        P("patch"),
    )
    out_specs = (P("patch", None, None), P("patch", None, None), P(), P(), P())
    return jax.shard_map(
        on_device, mesh=mesh, in_specs=in_specs, out_specs=out_specs, check_vma=False
    )
```

```python
import functools
import math

import numpy as np
import jax
import jax.numpy as jnp
from jax import lax
from jax.experimental import pallas as pl
from jax.experimental.pallas import tpu as pltpu
from jax.sharding import PartitionSpec as P

BF = jnp.bfloat16
F32 = jnp.float32
EDGE = 8
CELLS = 512
SLOTS = 32
C = 32
PB = 8
STEPS = SLOTS // PB
BIG = 32
BIG_STEPS = SLOTS // BIG
NPAR = 5
STRIDES = (64, 8, 1)
MORTON = (3, 8, 16)
ROW0 = (24, 16, 0)
NEAR = 27
FAR = 8
BASE_A = 6 * SLOTS
BASE_B = BASE_A + NEAR
BASE_C = BASE_B + NEAR + FAR
ROWS = BASE_C + FAR
VMEM_LIMIT = 14 * 1024 * 1024
DST, LEAD, TRAIL, SCAL = 0, 32, 64, 96
N_COUNT, N_ODD, N_LAST, N_OWNED = SCAL, SCAL + 1, SCAL + 2, SCAL + 3
META = 128
IN_F, OUT_B = range(2)
OUT_F, IN_B, CO_F, CO_B = range(4)
CHUNKS = 8
DWR = 7


def cell_coords():
    ids = np.arange(CELLS)
    return [ids // 64, ids // 8 % 8, ids % 8]


def face_cells(face):
    coords = cell_coords()
    keep = coords[face // 2] == (EDGE - 1 if face % 2 else 0)
    return np.nonzero(keep)[0]


def constants():
    spread = np.zeros((2, 256, 2 * CELLS), np.float32)
    for face in range(6):
        for j, cell in enumerate(face_cells(face)):
            for kind in range(2):
                col = (face % 2) * 128 + kind * 64 + j
                if face >= 2:
                    spread[face // 2 - 1, col, kind * CELLS + cell] = 1
    c0, c1, c2 = cell_coords()
    group = (c0 // 2) * 16 + (c1 // 2) * 4 + c2 // 2
    rest = np.zeros((2, CELLS, 128), np.float32)
    up = np.zeros((128, 2 * CELLS), np.float32)
    for cell in range(CELLS):
        rest[0, cell, group[cell]] = 0.125
        rest[1, cell, 64 + group[cell]] = 1
        up[group[cell], cell] = 1
        up[64 + group[cell], CELLS + cell] = 1
    place = np.zeros((256, 2 * CELLS), np.float32)
    for o2 in range(2):
        for a in range(64):
            cell = (a // 16) * 64 + (a // 4 % 4) * 8 + a % 4 + 4 * o2
            place[128 * o2 + a, cell] = 1
            place[128 * o2 + 64 + a, CELLS + cell] = 1
    as_bf = lambda item: np.asarray(item, jnp.bfloat16)
    return (
        as_bf(spread),
        as_bf(rest),
        as_bf(up),
        as_bf(place),
    )


def dot(a, b):
    return jnp.dot(a, b, preferred_element_type=F32)


def dot_nt(a, b):
    return lax.dot_general(a, b, (((1,), (1,)), ((), ())), preferred_element_type=F32)


def coord_of(dim):
    lane = lax.broadcasted_iota(jnp.int32, (16, CELLS), 1)
    return (lane // STRIDES[dim]) % EDGE


def on_face(face):
    edge = EDGE - 1 if face % 2 else 0
    return jnp.where(coord_of(face // 2) == edge, 1.0, 0.0)


def halves(field):
    return field.reshape(field.shape[0] // 16, 16, CELLS)


def times(field, mask):
    return (halves(field) * mask[None]).reshape(field.shape)


def toward(field, face):
    stride = STRIDES[face // 2]
    shift = CELLS - stride if face % 2 else stride
    return pltpu.roll(field, shift, 1)


def send_rows(
    count, odd, v_ref, y_ref, sel_ref, v_rows, y_rows, sides, inner_ref, outer_ref, waits=((), ())
):
    for side in range(2):
        for copy in waits[side]:
            copy.wait()
        for dim in (2, 1, 0):
            depth = MORTON[dim]
            for i in range(depth):
                slot = jnp.clip(count - depth + i, 0, SLOTS - 1) if side else i
                v_rows[i] = v_ref[slot]
                y_rows[i] = y_ref[slot]
            cols = slice(side * 128, side * 128 + 128)
            layers = dot(v_rows[:depth].reshape(depth * C, CELLS), sel_ref[2 * dim, :, cols])
            layers += dot(y_rows[:depth].reshape(depth * C, CELLS), sel_ref[2 * dim + 1, :, cols])
            layers = layers.astype(BF).reshape(depth, C, 128)
            if dim == 2 and side:
                sides[side, 0:8] = layers[8:16]
                sides[side, 8:16] = layers[0:8]
            else:
                sides[side, ROW0[dim] : ROW0[dim] + depth] = layers
    inner_ref[...] = sides[1 - odd]
    outer_ref[...] = sides[odd]


def make_selection(sel_ref):
    cell = lax.broadcasted_iota(jnp.int32, (CELLS, 256), 0)
    lane = lax.broadcasted_iota(jnp.int32, (CELLS, 256), 1)
    at = lane % 64
    edge = jnp.where(lane < 128, 0, EDGE - 1)
    first_half = lane % 128 < 64
    for dim in range(3):
        if dim == 0:
            want = edge * 64 + at
        elif dim == 1:
            want = at // 8 * 64 + edge * 8 + at % 8
        else:
            want = at * 8 + edge
        hit = cell == want
        sel_ref[2 * dim] = jnp.where(hit & first_half, 1.0, 0.0).astype(BF)
        sel_ref[2 * dim + 1] = jnp.where(hit & ~first_half, 1.0, 0.0).astype(BF)


def layers_kernel(
    counts_hbm, x_hbm, z_hbm, inner_ref, outer_ref, sel_ref,
    v_rows, y_rows, sides, x_ref, z_ref, counts, sems, counts_sem,
):
    rank = lax.axis_index("patch")
    size = SLOTS // CHUNKS
    count_copy = pltpu.make_async_copy(counts_hbm, counts, counts_sem)
    count_copy.start()
    copies = []
    for k in range(CHUNKS):
        part = pl.ds(k * size, size)
        copies.append(pltpu.make_async_copy(x_hbm.at[part], x_ref.at[part], sems.at[0, k]))
        copies.append(pltpu.make_async_copy(z_hbm.at[part], z_ref.at[part], sems.at[1, k]))
    for copy in copies:
        copy.start()
    make_selection(sel_ref)
    count_copy.wait()
    send_rows(
        counts[rank], rank % 2, x_ref, z_ref, sel_ref, v_rows, y_rows, sides, inner_ref, outer_ref,
        waits=(copies[:CHUNKS], copies[CHUNKS:]),
    )


def fill_table(v_ref, y_ref, sel_ref, table):
    for dim in range(3):
        layers = dot(v_ref[...].reshape(SLOTS * C, CELLS), sel_ref[2 * dim])
        layers += dot(y_ref[...].reshape(SLOTS * C, CELLS), sel_ref[2 * dim + 1])
        layers = layers.astype(BF)
        for high in range(2):
            face = 2 * dim + high
            table[face * SLOTS : (face + 1) * SLOTS] = layers[
                :, high * 128 : high * 128 + 128
            ].reshape(SLOTS, C, 128)


def fill_mats(mats, weights):
    for k, (weight, turned) in enumerate(weights):
        for f in range(7):
            one = weight[f].astype(F32)
            mats[k, :, f * C : (f + 1) * C] = (one.T if turned else one).astype(BF)


def prepare_kernel(
    counts, octant, neighbour, level_tag,
    got_ref, x_ref, z_ref, sel_ref, w_in, w_out,
    meta, index, xs, zs, mats, table,
):
    rank = lax.axis_index("patch")
    odd = rank % 2

    def count_at(device):
        here = counts[jnp.clip(device, 0, counts.shape[0] - 1)]
        return jnp.where(device < 0, 0, here)

    first = lax.fori_loop(0, rank, lambda d, s: s + counts[d], jnp.int32(0))
    count = count_at(rank)
    count_1 = count_at(rank - 1)
    count_2 = count_at(rank - 2)
    stop = first + count
    meta[N_COUNT] = count
    meta[N_ODD] = odd
    meta[N_LAST] = jnp.where(stop % 8 != 0, stop // 8 - first // 8, NPAR)
    meta[N_OWNED] = jnp.where(first % 8 == 0, 1, 0)
    lead_count = (8 - first % 8) % 8
    for p in range(SLOTS):
        live = p < count
        parent = (first % 8 + p) // 8
        o = jnp.clip(octant[p], 0, 7)
        meta[DST + p] = jnp.where(live, parent * 8 + o, NPAR * 8)
        meta[LEAD + p] = jnp.where(live & (p < lead_count), o, 8)
        meta[TRAIL + p] = jnp.where(live & (p >= count - stop % 8), o, 8)

    near_left = jnp.where(odd == 1, BASE_A, BASE_B)
    near_right = jnp.where(odd == 1, BASE_B, BASE_A)
    far_left = jnp.where(odd == 1, BASE_C, BASE_B + NEAR)
    far_right = jnp.where(odd == 1, BASE_B + NEAR, BASE_C)
    face = lax.broadcasted_iota(jnp.int32, (6, SLOTS), 0)
    own = lax.broadcasted_iota(jnp.int32, (6, SLOTS), 1)
    depth = jnp.where(face < 2, MORTON[0], jnp.where(face < 4, MORTON[1], MORTON[2]))
    row0 = jnp.where(face < 2, ROW0[0], jnp.where(face < 4, ROW0[1], ROW0[2]))
    high = (face & 1) == 1
    other = neighbour[...]
    away = (other >> 5) - rank
    slot = other & 31
    back = slot - (count_1 - depth)
    left = jnp.where(face >= 4, (back + 8) & 15, row0 + back) + near_left
    near = jnp.where(high, near_right + row0 + slot, left)
    far = jnp.where(high, far_right + slot, far_left + slot - (count_2 - 8))
    row = jnp.where(away == 0, (face ^ 1) * SLOTS + slot, near)
    row = jnp.where((away == 2) | (away == -2), far, row)
    row = jnp.where(level_tag[...] == 1, face * SLOTS + own, row)
    index[0:6] = jnp.clip(row, 0, ROWS - 1)
    index[6:12] = level_tag[...]

    fill_mats(mats, ((w_in, True), (w_out, False)))
    for p in range(SLOTS):
        live = (p < count).astype(F32)
        xs[p] = (x_ref[p].astype(F32) * live).astype(BF)
        zs[p] = (z_ref[p].astype(F32) * live).astype(BF)
    fill_table(xs, zs, sel_ref, table)
    table[BASE_A:BASE_B] = got_ref[...]


def window_kernel(hidden_ref, tb_ref, rest_ref, w_in, w_out, w_co, mats, dw_ref, means_ref):
    fill_mats(mats, ((w_out, True), (w_in, False), (w_co, True), (w_co, False)))
    dw_ref[...] = jnp.zeros_like(dw_ref)

    @pl.loop(0, BIG_STEPS)
    def _(step):
        dw = jnp.zeros((7 * C, C), F32)
        for p in range(BIG):
            here = step * BIG + p
            dw += dot_nt(tb_ref[here], hidden_ref[here])
            means_ref[here] = dot(tb_ref[here], rest_ref[0]).astype(BF)
        dw_ref[...] += dw


def table_kernel(v_ref, y_ref, sel_ref, table):
    fill_table(v_ref, y_ref, sel_ref, table)


def join_table(parts, coef, table):
    start = 0
    for part in parts:
        size = part.shape[0]
        table[start : start + size] = part[...]
        start += size
    for dim in range(3):
        low, high = on_face(2 * dim), on_face(2 * dim + 1)
        for t_low in range(2):
            for t_high in range(2):
                row = dim * 4 + t_low * 2 + t_high
                coef[row, 0] = (low * (1 - t_low) + high * t_high).astype(BF)
                coef[row, 1] = (high * (1 - t_high) + low * t_low).astype(BF)


def block_taps(start, index, v_ref, y_ref, spread_ref, table, coef, picked, ta, tb):
    size = v_ref.shape[0]
    for dim in range(3):
        low, high = 2 * dim, 2 * dim + 1
        edges = [on_face(low), on_face(high)]
        edges = [edge.astype(BF) for edge in edges]
        if dim:
            for p in range(size):
                picked[p, :, 0:128] = table[index[low, start + p]]
                picked[p, :, 128:256] = table[index[high, start + p]]
            spread = dot(picked[...].reshape(size * C, 256), spread_ref[dim - 1]).astype(BF)
        for p in range(size):
            if dim:
                rows = slice(p * C, (p + 1) * C)
                v_edge = spread[rows, :CELLS]
                y_edge = spread[rows, CELLS:]
            else:
                r_low = table[index[low, start + p]]
                r_high = table[index[high, start + p]]
                blank = jnp.zeros((C, 256), BF)
                v_edge = jnp.concatenate([r_low, blank, pltpu.roll(r_high, 64, 1)], axis=1)
                y_edge = jnp.concatenate([pltpu.roll(r_low, 64, 1), blank, r_high], axis=1)
            field = v_ref[p]
            other = y_ref[p]
            if dim == 0:
                ta[p, 0:C] = field
                tb[p, 0:C] = other
            row = (
                dim * 4
                + index[6 + low, start + p] * 2
                + index[6 + high, start + p]
            )
            for k, face in enumerate((low, high)):
                ta[p, C * (face + 1) : C * (face + 2)] = jnp.where(
                    edges[k][None] > 0, halves(v_edge), halves(toward(field, face))
                ).reshape(C, CELLS)
                back = face ^ 1
                kept = jnp.where(edges[k][None] > 0, 0.0, halves(toward(other, face)))
                tb[p, C * (back + 1) : C * (back + 2)] = (
                    kept + halves(y_edge) * coef[row, k][None]
                ).reshape(C, CELLS)


def silu_pair(pre):
    sigma = 1.0 / (1.0 + jnp.exp(-pre))
    return pre * sigma, sigma * (1.0 + pre * (1.0 - sigma))


def fine_kernel(
    meta, index, xs, zs, t_ref, b_ref, c_ref, mats, spread_ref, rest_ref,
    ta_ref, tb_ref, hidden_ref, slope_ref, gm_ref, par_ref, inner_ref, outer_ref,
    table, coef, picked, par, ends,
):
    join_table((t_ref, b_ref, c_ref), coef, table)
    par[...] = jnp.zeros_like(par)
    ends[...] = jnp.zeros_like(ends)

    @pl.loop(0, BIG_STEPS)
    def _(step):
        start = step * BIG
        x_at, z_at, ta, tb, hidden_at, slope_at, gm_at = [
            item.at[pl.ds(start, BIG)]
            for item in (xs, zs, ta_ref, tb_ref, hidden_ref, slope_ref, gm_ref)
        ]
        block_taps(start, index, x_at, z_at, spread_ref, table, coef, picked, ta, tb)
        for p in range(BIG):
            hidden, slope = silu_pair(dot(mats[IN_F], ta[p]))
            hidden_at[p] = hidden.astype(BF)
            slope_at[p] = slope.astype(BF)
            gm_at[p] = dot(mats[OUT_B], tb[p]).astype(BF)
        child = dot(hidden_at[...].reshape(BIG * C, CELLS), rest_ref[0])
        child += dot(gm_at[...].reshape(BIG * C, CELLS), rest_ref[1])
        child = child.astype(BF)
        for p in range(BIG):
            row = child[p * C : (p + 1) * C]
            par[meta[DST + start + p]] = row
            ends[0, meta[LEAD + start + p]] = row
            ends[1, meta[TRAIL + start + p]] = row

    par_ref[...] = par[: NPAR * 8]
    odd = meta[N_ODD]
    inner_ref[...] = ends[1 - odd, 0:8]
    outer_ref[...] = ends[odd, 0:8]


def coarse_level(meta, par_ref, inner_ref, outer_ref, wa, wb, place_ref, par, taps, up_rows, dw_ref):
    par[: NPAR * 8] = par_ref[...]
    par[NPAR * 8 :] = jnp.zeros((8, C, 128), BF)
    last = meta[N_LAST] * 8
    odd = meta[N_ODD]
    inner_at = jnp.where(odd == 1, 0, last)
    outer_at = jnp.where(odd == 1, last, 0)
    for o in range(8):
        par[inner_at + o] = par[inner_at + o] + inner_ref[o]
    for o in range(8):
        par[outer_at + o] = par[outer_at + o] + outer_ref[o]

    rows = NPAR * C
    both = jnp.zeros((rows, 2 * CELLS), BF)
    for o in range(0, 8, 2):
        lhs = jnp.concatenate(
            [
                jnp.concatenate([par[q * 8 + o], par[q * 8 + o + 1]], axis=1)
                for q in range(NPAR)
            ],
            axis=0,
        )
        put = dot(lhs, place_ref[...]).astype(BF)
        shift = (o // 4) * 256 + (o // 2 % 2) * 32
        if shift:
            put = jnp.concatenate(
                [
                    pltpu.roll(put[:, :CELLS], shift, 1),
                    pltpu.roll(put[:, CELLS:], shift, 1),
                ],
                axis=1,
            )
        both += put
    field = both[:, :CELLS]
    cotan = both[:, CELLS:].astype(F32)
    edges = [on_face(face).astype(BF) for face in range(6)]
    inside = [(1.0 - on_face(face)).astype(BF) for face in range(6)]

    def store(face, value):
        taps[:, C * face : C * (face + 1)] = value.reshape(NPAR, C, CELLS)

    store(0, field)
    for face in range(6):
        store(face + 1, times(toward(field, face), inside[face]) + times(field, edges[face]))
    pre = jnp.concatenate([dot(wa, taps[q]) for q in range(NPAR)], axis=0)
    act, slope = silu_pair(pre)
    act = act.astype(BF)
    grad = (cotan * slope).astype(BF)
    dw = jnp.zeros((7 * C, C), F32)
    for q in range(NPAR):
        part = dot_nt(taps[q], grad[q * C : (q + 1) * C])
        if q == 0:
            part = part * meta[N_OWNED].astype(F32)
        dw += part
    store(0, grad)
    for face in range(6):
        back = face ^ 1
        store(face + 1, times(toward(grad, back), inside[back]) + times(grad, edges[face]))
    down = jnp.concatenate([dot(wb, taps[q]) for q in range(NPAR)], axis=0).astype(BF)
    for o in range(0, 8, 2):
        one, two = act, down
        shift = (o // 4) * 256 + (o // 2 % 2) * 32
        if shift:
            one = pltpu.roll(act, CELLS - shift, 1)
            two = pltpu.roll(down, CELLS - shift, 1)
        got = dot_nt(one, place_ref[:, :CELLS]) + dot_nt(two, place_ref[:, CELLS:])
        got = got.astype(BF)
        for q in range(NPAR):
            up_rows[q * 8 + o] = got[q * C : (q + 1) * C, :128]
            up_rows[q * 8 + o + 1] = got[q * C : (q + 1) * C, 128:]
    up_rows[NPAR * 8] = jnp.zeros((C, 128), BF)
    dw_ref[:, 2 * C : 3 * C] = dw


def merge_kernel(
    meta,
    ta_ref, means_ref, dw0_ref, hidden_ref, slope_ref, gm_ref, par_ref, pin_ref, pout_ref,
    mats, place_ref, up_ref, sel_ref,
    merged_ref, gpa_ref, sum_ref, inner_ref, outer_ref,
    par, taps, up_rows, picked, v_rows, y_rows, sides, dw_ref,
):
    dw_ref[...] = jnp.zeros_like(dw_ref)
    dw_ref[:, C : 2 * C] = dw0_ref[...]
    coarse_level(
        meta, par_ref, pin_ref, pout_ref, mats[CO_F], mats[CO_B],
        place_ref, par, taps, up_rows, dw_ref,
    )

    @pl.loop(0, BIG_STEPS)
    def _(step):
        start = step * BIG
        for p in range(BIG):
            picked[p] = up_rows[meta[DST + start + p]]
        spread = dot(picked[...].reshape(BIG * C, 128), up_ref[...])
        dw_in = jnp.zeros((7 * C, C), F32)
        dw_out = jnp.zeros((7 * C, C), F32)
        for p in range(BIG):
            rows = slice(p * C, (p + 1) * C)
            here = start + p
            merged = (hidden_ref[here].astype(F32) + spread[rows, :CELLS]).astype(BF)
            grad = gm_ref[here].astype(F32) + spread[rows, CELLS:] * 0.125
            gpa = (grad * slope_ref[here].astype(F32)).astype(BF)
            merged_ref[here] = merged
            gpa_ref[here] = gpa
            dw_in += dot_nt(ta_ref[here], gpa)
            dw_out += dot_nt(means_ref[here], picked[p])
        dw_ref[:, 0:C] += dw_in
        dw_ref[:, C : 2 * C] += dw_out * 8.0

    send_rows(
        meta[N_COUNT], meta[N_ODD], merged_ref, gpa_ref, sel_ref,
        v_rows, y_rows, sides, inner_ref.at[0:NEAR], outer_ref,
    )
    rounded = dw_ref[...].astype(BF).reshape(DWR, C, 128)
    sum_ref[...] = rounded
    inner_ref[NEAR : NEAR + DWR] = rounded


def second_table_kernel(v_ref, y_ref, sel_ref, got_ref, table):
    fill_table(v_ref, y_ref, sel_ref, table)
    table[BASE_A:BASE_B] = got_ref[0:NEAR]


def final_body(step, index, v_ref, y_ref, xs, zs, mats, spread_ref, table, coef, out_hbm, gs_hbm,
               picked, ta, tb, out_ref, gs_ref, sems):
    start = step * PB
    part = pl.ds(start, PB)
    block_taps(
        start, index, v_ref.at[part], y_ref.at[part], spread_ref, table, coef, picked, ta, tb
    )
    half = PB // 2
    copies = []
    for k in range(2):
        for p in range(k * half, (k + 1) * half):
            out_ref[p] = (xs[start + p].astype(F32) + dot(mats[OUT_F], ta[p])).astype(BF)
            gs_ref[p] = (zs[start + p].astype(F32) + dot(mats[IN_B], tb[p])).astype(BF)
        here, there = pl.ds(k * half, half), pl.ds(start + k * half, half)
        new = [
            pltpu.make_async_copy(out_ref.at[here], out_hbm.at[there], sems.at[k, 0]),
            pltpu.make_async_copy(gs_ref.at[here], gs_hbm.at[there], sems.at[k, 1]),
        ]
        for copy in new:
            copy.start()
        copies += new
    for copy in copies:
        copy.wait()


def first_final_kernel(
    index, v_ref, y_ref, xs, zs, mats, spread_ref, t_ref, b_ref, c_ref,
    table, coef, out_hbm, gs_hbm, *scratch,
):
    join_table((t_ref, b_ref, c_ref), coef, table)
    final_body(0, index, v_ref, y_ref, xs, zs, mats, spread_ref, table, coef, out_hbm, gs_hbm,
               *scratch)


def next_final_kernel(
    step, index, v_ref, y_ref, xs, zs, mats, spread_ref, table, coef, out_in, gs_in,
    out_hbm, gs_hbm, *scratch,
):
    final_body(step, index, v_ref, y_ref, xs, zs, mats, spread_ref, table, coef, out_hbm, gs_hbm,
               *scratch)


def weights_kernel(scale, one_ref, two_ref, in_ref, out_ref, co_ref):
    for f in range(7):
        total = (one_ref[f].astype(F32) + two_ref[f].astype(F32)) * scale
        in_ref[f] = total[:, 0:C]
        out_ref[f] = total[:, C : 2 * C].T
        co_ref[f] = total[:, 2 * C : 3 * C]


SMEM = functools.partial(pl.BlockSpec, memory_space=pltpu.SMEM)


VMEM = functools.partial(pl.BlockSpec, memory_space=pltpu.VMEM)
HBM = functools.partial(pl.BlockSpec, memory_space=pltpu.HBM)


def params(limit=VMEM_LIMIT):
    return pltpu.CompilerParams(vmem_limit_bytes=limit)


def shape_of(shape, dtype=BF):
    return jax.ShapeDtypeStruct(shape, dtype)


def cost(micros):
    return pl.CostEstimate(
        flops=int(micros * 1e6), bytes_accessed=int(micros * 3.0e6), transcendentals=0
    )


def pairs(kind, devices):
    if kind == "inner":
        links = [(2 * c, 2 * c + 1) for c in range(devices // 2)]
    else:
        links = [(2 * c + 1, 2 * c + 2) for c in range(devices // 2 - 1)]
    return links + [(b, a) for a, b in links]


def trade(block, kind):
    return lax.ppermute(block, "patch", pairs(kind, lax.axis_size("patch")))


def relay_out(outer, got_a):
    return trade(jnp.concatenate([outer, got_a[:FAR]], axis=0), "outer")


def relay_in(got_b, first):
    got_b, first = lax.optimization_barrier((got_b, first))
    return trade(got_b[:FAR], "inner"), first


def add(one, two):
    return (one.astype(F32) + two.astype(F32)).astype(BF)


def swap(block, mask):
    devices = lax.axis_size("patch")
    return lax.ppermute(block, "patch", [(i, i ^ mask) for i in range(devices)])


def on_device(
    fine_state, weight_in, weight_out, weight_coarse, cotangent,
    owner_count, neighbour, level_tag, octant,
):
    devices = lax.axis_size("patch")
    spread, rest, up, place = [jnp.asarray(item) for item in constants()]

    field = (SLOTS, C, CELLS)
    stack = (SLOTS, 7 * C, CELLS)
    near = (NEAR, C, 128)
    far = (FAR, C, 128)
    par_rows = (NPAR * 8, C, 128)
    sel_shape = (6, CELLS, 256)
    rows_scratch = [pltpu.VMEM((16, C, CELLS), BF)] * 2 + [pltpu.VMEM((2, NEAR, C, 128), BF)]
    table_shape = (ROWS, C, 128)
    coef_shape = (12, 2, 16, CELLS)
    picked_scratch = pltpu.VMEM((PB, C, 256), BF)

    inner, outer, sel = pl.pallas_call(
        layers_kernel,
        in_specs=[HBM()] * 3,
        out_specs=[VMEM()] * 3,
        out_shape=[shape_of(near), shape_of(near), shape_of(sel_shape)],
        scratch_shapes=rows_scratch
        + [pltpu.VMEM(field, BF), pltpu.VMEM(field, BF)]
        + [pltpu.SMEM(owner_count.shape, jnp.int32)]
        + [pltpu.SemaphoreType.DMA((2, CHUNKS)), pltpu.SemaphoreType.DMA],
        compiler_params=params(),
        cost_estimate=cost(4),
        name="face_rows",
    )(
        pltpu.with_memory_space_constraint(owner_count, pltpu.HBM),
        pltpu.with_memory_space_constraint(fine_state, pltpu.HBM),
        pltpu.with_memory_space_constraint(cotangent, pltpu.HBM),
    )
    got_a = trade(inner, "inner")
    got_b = relay_out(outer, got_a)

    meta, index, xs, zs, mats, table = pl.pallas_call(
        prepare_kernel,
        in_specs=[SMEM()] * 2 + [VMEM()] * 8,
        out_specs=[SMEM()] + [VMEM()] * 5,
        out_shape=[shape_of((META,), jnp.int32), shape_of((12, SLOTS), jnp.int32)]
        + [shape_of(field), shape_of(field), shape_of((2, C, 7 * C)), shape_of((BASE_B, C, 128))],
        compiler_params=params(),
        cost_estimate=cost(4),
        name="prepare",
    )(
        owner_count, octant, neighbour.T, level_tag.T, got_a, fine_state, cotangent, sel,
        weight_in, weight_out,
    )
    got_c, meta = relay_in(got_b, meta)

    taps_a, taps_b, hidden, slope, grad_merged, par, pin, pout = pl.pallas_call(
        fine_kernel,
        in_specs=[SMEM()] * 2 + [VMEM()] * 8,
        out_specs=[VMEM()] * 8,
        out_shape=[shape_of(stack), shape_of(stack), shape_of(field), shape_of(field)]
        + [shape_of(field), shape_of(par_rows), shape_of(far), shape_of(far)],
        scratch_shapes=[
            pltpu.VMEM(table_shape, BF),
            pltpu.VMEM(coef_shape, BF),
            pltpu.VMEM((BIG, C, 256), BF),
            pltpu.VMEM((NPAR * 8 + 8, C, 128), BF),
            pltpu.VMEM((2, 16, C, 128), BF),
        ],
        compiler_params=params(),
        cost_estimate=cost(8),
        name="fine_level",
    )(meta, index, xs, zs, table, got_b, got_c, mats, spread, rest)
    child_out = trade(pout, "outer")
    child_in = trade(pin, "inner")

    mats, dw_part, means = pl.pallas_call(
        window_kernel,
        in_specs=[VMEM()] * 6,
        out_specs=[VMEM()] * 3,
        out_shape=[shape_of((4, C, 7 * C)), shape_of((7 * C, C), F32)]
        + [shape_of((SLOTS, 7 * C, 128))],
        compiler_params=params(),
        cost_estimate=cost(3),
        name="window",
    )(hidden, taps_b, rest, weight_in, weight_out, weight_coarse)

    merged, grad_pre, sums, inner, outer = pl.pallas_call(
        merge_kernel,
        in_specs=[SMEM()] + [VMEM()] * 13,
        out_specs=[VMEM()] * 5,
        out_shape=[shape_of(field), shape_of(field), shape_of((DWR, C, 128))]
        + [shape_of((NEAR + DWR, C, 128)), shape_of(near)],
        scratch_shapes=[
            pltpu.VMEM((NPAR * 8 + 8, C, 128), BF),
            pltpu.VMEM((NPAR, 7 * C, CELLS), BF),
            pltpu.VMEM((NPAR * 8 + 8, C, 128), BF),
            pltpu.VMEM((BIG, C, 128), BF),
        ]
        + rows_scratch
        + [pltpu.VMEM((7 * C, 128), F32)],
        compiler_params=params(),
        cost_estimate=cost(9),
        name="coarse_and_merge",
    )(
        meta, taps_a, means, dw_part, hidden, slope, grad_merged, par, child_in, child_out, mats,
        place, up, sel,
    )
    got_a = trade(inner, "inner")
    got_b = relay_out(outer, got_a)
    sums = add(sums, got_a[NEAR:])
    sums = add(sums, swap(sums, 2))

    table = pl.pallas_call(
        second_table_kernel,
        in_specs=[VMEM()] * 4,
        out_specs=VMEM(),
        out_shape=shape_of((BASE_B, C, 128)),
        compiler_params=params(),
        cost_estimate=cost(2),
        name="face_table",
    )(merged, grad_pre, sel, got_a)
    got_c, table = relay_in(got_b, table)

    last_scratch = [
        picked_scratch,
        pltpu.VMEM((PB, 7 * C, CELLS), BF),
        pltpu.VMEM((PB, 7 * C, CELLS), BF),
        pltpu.VMEM((PB, C, CELLS), BF),
        pltpu.VMEM((PB, C, CELLS), BF),
        pltpu.SemaphoreType.DMA((2, 2)),
    ]
    fixed = (index, merged, grad_pre, xs, zs, mats, spread)
    sums, got_c = lax.optimization_barrier((add(sums, swap(sums, 6)), got_c))
    partner = swap(sums, 8)
    table, coef, output, grad_state = pl.pallas_call(
        first_final_kernel,
        in_specs=[SMEM()] + [VMEM()] * 9,
        out_specs=[VMEM(), VMEM(), HBM(), HBM()],
        out_shape=[shape_of(table_shape), shape_of(coef_shape), shape_of(field), shape_of(field)],
        scratch_shapes=last_scratch,
        compiler_params=params(),
        cost_estimate=cost(2),
        name="last_level",
    )(*fixed, table, got_b, got_c)
    for step, mask in ((1, 24), (2, 32), (3, 96)):
        sums, coef, output = lax.optimization_barrier((add(sums, partner), coef, output))
        partner = swap(sums, mask)
        output, grad_state = pl.pallas_call(
            functools.partial(next_final_kernel, step),
            in_specs=[SMEM()] + [VMEM()] * 8 + [HBM(), HBM()],
            out_specs=[HBM(), HBM()],
            out_shape=[shape_of(field), shape_of(field)],
            input_output_aliases={9: 0, 10: 1},
            scratch_shapes=last_scratch,
            compiler_params=params(),
            cost_estimate=cost(2),
            name="last_level",
        )(*fixed, table, coef, output, grad_state)

    scale = 1.0 / math.sqrt(float(devices * SLOTS * CELLS))
    mat = shape_of((7, C, C), F32)
    grads = pl.pallas_call(
        functools.partial(weights_kernel, scale),
        in_specs=[VMEM()] * 2,
        out_specs=[VMEM()] * 3,
        compiler_params=params(),
        out_shape=[mat, mat, mat],
        cost_estimate=cost(1),
        name="weight_sums",
    )(sums, partner)
    return (output, grad_state, *grads)


def solution(mesh):
    in_specs = (
        P("patch", None, None),
        P(),
        P(),
        P(),
        P("patch", None, None),
        P(),
        P("patch", None),
        P("patch", None),
        P("patch"),
    )
    out_specs = (P("patch", None, None), P("patch", None, None), P(), P(), P())
    return jax.shard_map(
        on_device, mesh=mesh, in_specs=in_specs, out_specs=out_specs, check_vma=False
    )
```

```python
import functools
import math

import numpy as np
import jax
import jax.numpy as jnp
from jax import lax
from jax.experimental import pallas as pl
from jax.experimental.pallas import tpu as pltpu
from jax.sharding import PartitionSpec as P

BF = jnp.bfloat16
F32 = jnp.float32
EDGE = 8
CELLS = 512
SLOTS = 32
C = 32
PB = 8
STEPS = SLOTS // PB
BIG = 32
BIG_STEPS = SLOTS // BIG
NPAR = 5
STRIDES = (64, 8, 1)
MORTON = (3, 8, 16)
ROW0 = (24, 16, 0)
NEAR = 27
FAR = 8
BASE_A = 6 * SLOTS
BASE_B = BASE_A + NEAR
BASE_C = BASE_B + NEAR + FAR
ROWS = BASE_C + FAR
VMEM_LIMIT = 14 * 1024 * 1024
DST, LEAD, TRAIL, SCAL = 0, 32, 64, 96
N_COUNT, N_ODD, N_LAST, N_OWNED = SCAL, SCAL + 1, SCAL + 2, SCAL + 3
META = 128
IN_F, OUT_B = range(2)
OUT_F, IN_B, CO_F, CO_B = range(4)
CHUNKS = 8
DWR = 7


def cell_coords():
    ids = np.arange(CELLS)
    return [ids // 64, ids // 8 % 8, ids % 8]


def constants():
    c0, c1, c2 = cell_coords()
    group = (c0 // 2) * 16 + (c1 // 2) * 4 + c2 // 2
    rest = np.zeros((2, CELLS, 128), np.float32)
    for cell in range(CELLS):
        rest[0, cell, group[cell]] = 0.125
        rest[1, cell, 64 + group[cell]] = 1
    place = np.zeros((256, 2 * CELLS), np.float32)
    for o2 in range(2):
        for a in range(64):
            cell = (a // 16) * 64 + (a // 4 % 4) * 8 + a % 4 + 4 * o2
            place[128 * o2 + a, cell] = 1
            place[128 * o2 + 64 + a, CELLS + cell] = 1
    as_bf = lambda item: np.asarray(item, jnp.bfloat16)
    return (
        as_bf(rest),
        as_bf(place),
    )


def dot(a, b):
    return jnp.dot(a, b, preferred_element_type=F32)


def dot_nt(a, b):
    return lax.dot_general(a, b, (((1,), (1,)), ((), ())), preferred_element_type=F32)


def coord_of(dim):
    lane = lax.broadcasted_iota(jnp.int32, (16, CELLS), 1)
    return (lane // STRIDES[dim]) % EDGE


def on_face(face):
    edge = EDGE - 1 if face % 2 else 0
    return jnp.where(coord_of(face // 2) == edge, 1.0, 0.0)


def halves(field):
    return field.reshape(field.shape[0] // 16, 16, CELLS)


def times(field, mask):
    return (halves(field) * mask[None]).reshape(field.shape)


def toward(field, face):
    stride = STRIDES[face // 2]
    shift = CELLS - stride if face % 2 else stride
    return pltpu.roll(field, shift, 1)


def send_rows(
    count, odd, v_ref, y_ref, sel_ref, v_rows, y_rows, sides, inner_ref, outer_ref, waits=((), ())
):
    for side in range(2):
        for copy in waits[side]:
            copy.wait()
        if side:
            for i in range(16):
                slot = jnp.clip(count - 16 + i, 0, SLOTS - 1)
                v_rows[i] = v_ref[slot]
                y_rows[i] = y_ref[slot]
        for dim in (2, 1, 0):
            depth = MORTON[dim]
            v_part = v_rows[16 - depth : 16] if side else v_ref[0:depth]
            y_part = y_rows[16 - depth : 16] if side else y_ref[0:depth]
            cols = slice(side * 128, side * 128 + 128)
            layers = dot(v_part.reshape(depth * C, CELLS), sel_ref[2 * dim, :, cols])
            layers += dot(y_part.reshape(depth * C, CELLS), sel_ref[2 * dim + 1, :, cols])
            layers = layers.astype(BF).reshape(depth, C, 128)
            if dim == 2 and side:
                sides[side, 0:8] = layers[8:16]
                sides[side, 8:16] = layers[0:8]
            else:
                sides[side, ROW0[dim] : ROW0[dim] + depth] = layers
    inner_ref[...] = sides[1 - odd]
    outer_ref[...] = sides[odd]


def make_selection(sel_ref):
    cell = lax.broadcasted_iota(jnp.int32, (CELLS, 256), 0)
    lane = lax.broadcasted_iota(jnp.int32, (CELLS, 256), 1)
    at = lane % 64
    edge = jnp.where(lane < 128, 0, EDGE - 1)
    first_half = lane % 128 < 64
    for dim in range(3):
        if dim == 0:
            want = edge * 64 + at
        elif dim == 1:
            want = at // 8 * 64 + edge * 8 + at % 8
        else:
            want = at * 8 + edge
        hit = cell == want
        sel_ref[2 * dim] = jnp.where(hit & first_half, 1.0, 0.0).astype(BF)
        sel_ref[2 * dim + 1] = jnp.where(hit & ~first_half, 1.0, 0.0).astype(BF)


def layers_kernel(
    counts_hbm, x_hbm, z_hbm, inner_ref, outer_ref, sel_ref,
    v_rows, y_rows, sides, x_ref, z_ref, counts, sems, counts_sem,
):
    rank = lax.axis_index("patch")
    size = SLOTS // CHUNKS
    count_copy = pltpu.make_async_copy(counts_hbm, counts, counts_sem)
    count_copy.start()
    copies = []
    for k in range(CHUNKS):
        part = pl.ds(k * size, size)
        copies.append(pltpu.make_async_copy(x_hbm.at[part], x_ref.at[part], sems.at[0, k]))
        copies.append(pltpu.make_async_copy(z_hbm.at[part], z_ref.at[part], sems.at[1, k]))
    for copy in copies:
        copy.start()
    make_selection(sel_ref)
    count_copy.wait()
    send_rows(
        counts[rank], rank % 2, x_ref, z_ref, sel_ref, v_rows, y_rows, sides, inner_ref, outer_ref,
        waits=(copies[:CHUNKS], copies[CHUNKS:]),
    )


def fill_table(v_ref, y_ref, sel_ref, table):
    for dim in range(3):
        layers = dot(v_ref[...].reshape(SLOTS * C, CELLS), sel_ref[2 * dim])
        layers += dot(y_ref[...].reshape(SLOTS * C, CELLS), sel_ref[2 * dim + 1])
        layers = layers.astype(BF)
        for high in range(2):
            face = 2 * dim + high
            table[face * SLOTS : (face + 1) * SLOTS] = layers[
                :, high * 128 : high * 128 + 128
            ].reshape(SLOTS, C, 128)


def fill_mats(mats, weights):
    for k, (weight, turned) in enumerate(weights):
        for f in range(7):
            one = weight[f].astype(F32)
            mats[k, :, f * C : (f + 1) * C] = (one.T if turned else one).astype(BF)


def prepare_kernel(
    counts, octant, neighbour, level_tag,
    got_ref, x_ref, z_ref, sel_ref, w_in, w_out,
    meta, index, xs, zs, mats, table,
):
    rank = lax.axis_index("patch")
    odd = rank % 2

    def count_at(device):
        here = counts[jnp.clip(device, 0, counts.shape[0] - 1)]
        return jnp.where(device < 0, 0, here)

    first = lax.fori_loop(0, rank, lambda d, s: s + counts[d], jnp.int32(0))
    count = count_at(rank)
    count_1 = count_at(rank - 1)
    count_2 = count_at(rank - 2)
    stop = first + count
    meta[N_COUNT] = count
    meta[N_ODD] = odd
    meta[N_LAST] = jnp.where(stop % 8 != 0, stop // 8 - first // 8, NPAR)
    meta[N_OWNED] = jnp.where(first % 8 == 0, 1, 0)
    lead_count = (8 - first % 8) % 8
    for p in range(SLOTS):
        live = p < count
        parent = (first % 8 + p) // 8
        o = jnp.clip(octant[p], 0, 7)
        meta[DST + p] = jnp.where(live, parent * 8 + o, NPAR * 8)
        meta[LEAD + p] = jnp.where(live & (p < lead_count), o, 8)
        meta[TRAIL + p] = jnp.where(live & (p >= count - stop % 8), o, 8)

    near_left = jnp.where(odd == 1, BASE_A, BASE_B)
    near_right = jnp.where(odd == 1, BASE_B, BASE_A)
    far_left = jnp.where(odd == 1, BASE_C, BASE_B + NEAR)
    far_right = jnp.where(odd == 1, BASE_B + NEAR, BASE_C)
    face = lax.broadcasted_iota(jnp.int32, (6, SLOTS), 0)
    own = lax.broadcasted_iota(jnp.int32, (6, SLOTS), 1)
    depth = jnp.where(face < 2, MORTON[0], jnp.where(face < 4, MORTON[1], MORTON[2]))
    row0 = jnp.where(face < 2, ROW0[0], jnp.where(face < 4, ROW0[1], ROW0[2]))
    high = (face & 1) == 1
    other = neighbour[...]
    away = (other >> 5) - rank
    slot = other & 31
    back = slot - (count_1 - depth)
    left = jnp.where(face >= 4, (back + 8) & 15, row0 + back) + near_left
    near = jnp.where(high, near_right + row0 + slot, left)
    far = jnp.where(high, far_right + slot, far_left + slot - (count_2 - 8))
    row = jnp.where(away == 0, (face ^ 1) * SLOTS + slot, near)
    row = jnp.where((away == 2) | (away == -2), far, row)
    row = jnp.where(level_tag[...] == 1, face * SLOTS + own, row)
    index[0:6] = jnp.clip(row, 0, ROWS - 1)
    index[6:12] = level_tag[...]

    fill_mats(mats, ((w_in, True), (w_out, False)))
    for p in range(SLOTS):
        live = (p < count).astype(F32)
        xs[p] = (x_ref[p].astype(F32) * live).astype(BF)
        zs[p] = (z_ref[p].astype(F32) * live).astype(BF)
    fill_table(xs, zs, sel_ref, table)
    table[BASE_A:BASE_B] = got_ref[...]


def window_kernel(hidden_ref, tb_ref, rest_ref, w_in, w_out, w_co, mats, dw_ref, means_ref):
    fill_mats(mats, ((w_out, True), (w_in, False), (w_co, True), (w_co, False)))
    dw_ref[...] = jnp.zeros_like(dw_ref)

    @pl.loop(0, BIG_STEPS)
    def _(step):
        dw = jnp.zeros((7 * C, C), F32)
        for p in range(BIG):
            here = step * BIG + p
            dw += dot_nt(tb_ref[here], hidden_ref[here])
            means_ref[here] = dot(tb_ref[here], rest_ref[0]).astype(BF)
        dw_ref[...] += dw


def table_kernel(v_ref, y_ref, sel_ref, table):
    fill_table(v_ref, y_ref, sel_ref, table)


def join_table(parts, coef, table):
    start = 0
    for part in parts:
        size = part.shape[0]
        table[start : start + size] = part[...]
        start += size
    for dim in range(3):
        low, high = on_face(2 * dim), on_face(2 * dim + 1)
        for t_low in range(2):
            for t_high in range(2):
                row = dim * 4 + t_low * 2 + t_high
                coef[row, 0] = (low * (1 - t_low) + high * t_high).astype(BF)
                coef[row, 1] = (high * (1 - t_high) + low * t_low).astype(BF)


def block_taps(start, index, v_ref, y_ref, sel_ref, table, coef, picked, ta, tb):
    size = v_ref.shape[0]
    for dim in range(3):
        low, high = 2 * dim, 2 * dim + 1
        edges = [on_face(low), on_face(high)]
        edges = [edge.astype(BF) for edge in edges]
        if dim:
            for p in range(size):
                picked[p, :, 0:128] = table[index[low, start + p]]
                picked[p, :, 128:256] = table[index[high, start + p]]
            rows_in = picked[...].reshape(size * C, 256)
            v_spread = dot_nt(rows_in, sel_ref[2 * dim]).astype(BF)
            y_spread = dot_nt(rows_in, sel_ref[2 * dim + 1]).astype(BF)
        for p in range(size):
            if dim:
                rows = slice(p * C, (p + 1) * C)
                v_edge = v_spread[rows]
                y_edge = y_spread[rows]
            else:
                r_low = table[index[low, start + p]]
                r_high = table[index[high, start + p]]
                blank = jnp.zeros((C, 256), BF)
                v_edge = jnp.concatenate([r_low, blank, pltpu.roll(r_high, 64, 1)], axis=1)
                y_edge = jnp.concatenate([pltpu.roll(r_low, 64, 1), blank, r_high], axis=1)
            field = v_ref[p]
            other = y_ref[p]
            if dim == 0:
                ta[p, 0:C] = field
                tb[p, 0:C] = other
            row = (
                dim * 4
                + index[6 + low, start + p] * 2
                + index[6 + high, start + p]
            )
            for k, face in enumerate((low, high)):
                ta[p, C * (face + 1) : C * (face + 2)] = jnp.where(
                    edges[k][None] > 0, halves(v_edge), halves(toward(field, face))
                ).reshape(C, CELLS)
                back = face ^ 1
                kept = jnp.where(edges[k][None] > 0, 0.0, halves(toward(other, face)))
                tb[p, C * (back + 1) : C * (back + 2)] = (
                    kept + halves(y_edge) * coef[row, k][None]
                ).reshape(C, CELLS)


def silu_pair(pre):
    sigma = 1.0 / (1.0 + jnp.exp(-pre))
    return pre * sigma, sigma * (1.0 + pre * (1.0 - sigma))


def fine_kernel(
    meta, index, xs, zs, t_ref, b_ref, c_ref, mats, sel_ref, rest_ref,
    ta_ref, tb_ref, hidden_ref, slope_ref, gm_ref, par_ref, inner_ref, outer_ref,
    table, coef, picked, par, ends,
):
    join_table((t_ref, b_ref, c_ref), coef, table)
    par[...] = jnp.zeros_like(par)
    ends[...] = jnp.zeros_like(ends)

    @pl.loop(0, BIG_STEPS)
    def _(step):
        start = step * BIG
        x_at, z_at, ta, tb, hidden_at, slope_at, gm_at = [
            item.at[pl.ds(start, BIG)]
            for item in (xs, zs, ta_ref, tb_ref, hidden_ref, slope_ref, gm_ref)
        ]
        block_taps(start, index, x_at, z_at, sel_ref, table, coef, picked, ta, tb)
        for p in range(BIG):
            hidden, slope = silu_pair(dot(mats[IN_F], ta[p]))
            hidden_at[p] = hidden.astype(BF)
            slope_at[p] = slope.astype(BF)
            gm_at[p] = dot(mats[OUT_B], tb[p]).astype(BF)
        child = dot(hidden_at[...].reshape(BIG * C, CELLS), rest_ref[0])
        child += dot(gm_at[...].reshape(BIG * C, CELLS), rest_ref[1])
        child = child.astype(BF)
        for p in range(BIG):
            row = child[p * C : (p + 1) * C]
            par[meta[DST + start + p]] = row
            ends[0, meta[LEAD + start + p]] = row
            ends[1, meta[TRAIL + start + p]] = row

    par_ref[...] = par[: NPAR * 8]
    odd = meta[N_ODD]
    inner_ref[...] = ends[1 - odd, 0:8]
    outer_ref[...] = ends[odd, 0:8]


def coarse_level(meta, par_ref, inner_ref, outer_ref, wa, wb, place_ref, par, taps, up_rows, dw_ref):
    par[: NPAR * 8] = par_ref[...]
    par[NPAR * 8 :] = jnp.zeros((8, C, 128), BF)
    last = meta[N_LAST] * 8
    odd = meta[N_ODD]
    inner_at = jnp.where(odd == 1, 0, last)
    outer_at = jnp.where(odd == 1, last, 0)
    for o in range(8):
        par[inner_at + o] = par[inner_at + o] + inner_ref[o]
    for o in range(8):
        par[outer_at + o] = par[outer_at + o] + outer_ref[o]

    rows = NPAR * C
    both = jnp.zeros((rows, 2 * CELLS), BF)
    for o in range(0, 8, 2):
        lhs = jnp.concatenate(
            [
                jnp.concatenate([par[q * 8 + o], par[q * 8 + o + 1]], axis=1)
                for q in range(NPAR)
            ],
            axis=0,
        )
        put = dot(lhs, place_ref[...]).astype(BF)
        shift = (o // 4) * 256 + (o // 2 % 2) * 32
        if shift:
            put = jnp.concatenate(
                [
                    pltpu.roll(put[:, :CELLS], shift, 1),
                    pltpu.roll(put[:, CELLS:], shift, 1),
                ],
                axis=1,
            )
        both += put
    field = both[:, :CELLS]
    cotan = both[:, CELLS:].astype(F32)
    edges = [on_face(face).astype(BF) for face in range(6)]
    inside = [(1.0 - on_face(face)).astype(BF) for face in range(6)]

    def store(face, value):
        taps[:, C * face : C * (face + 1)] = value.reshape(NPAR, C, CELLS)

    store(0, field)
    for face in range(6):
        store(face + 1, times(toward(field, face), inside[face]) + times(field, edges[face]))
    pre = jnp.concatenate([dot(wa, taps[q]) for q in range(NPAR)], axis=0)
    act, slope = silu_pair(pre)
    act = act.astype(BF)
    grad = (cotan * slope).astype(BF)
    dw = jnp.zeros((7 * C, C), F32)
    for q in range(NPAR):
        part = dot_nt(taps[q], grad[q * C : (q + 1) * C])
        if q == 0:
            part = part * meta[N_OWNED].astype(F32)
        dw += part
    store(0, grad)
    for face in range(6):
        back = face ^ 1
        store(face + 1, times(toward(grad, back), inside[back]) + times(grad, edges[face]))
    down = jnp.concatenate([dot(wb, taps[q]) for q in range(NPAR)], axis=0).astype(BF)
    for o in range(0, 8, 2):
        one, two = act, down
        shift = (o // 4) * 256 + (o // 2 % 2) * 32
        if shift:
            one = pltpu.roll(act, CELLS - shift, 1)
            two = pltpu.roll(down, CELLS - shift, 1)
        got = dot_nt(one, place_ref[:, :CELLS]) + dot_nt(two, place_ref[:, CELLS:])
        got = got.astype(BF)
        for q in range(NPAR):
            up_rows[q * 8 + o] = got[q * C : (q + 1) * C, :128]
            up_rows[q * 8 + o + 1] = got[q * C : (q + 1) * C, 128:]
    up_rows[NPAR * 8] = jnp.zeros((C, 128), BF)
    dw_ref[:, 2 * C : 3 * C] = dw


def merge_kernel(
    meta,
    ta_ref, means_ref, dw0_ref, hidden_ref, slope_ref, gm_ref, par_ref, pin_ref, pout_ref,
    mats, place_ref, rest_ref, sel_ref,
    merged_ref, gpa_ref, sum_ref, inner_ref, outer_ref,
    par, taps, up_rows, picked, v_rows, y_rows, sides, dw_ref,
):
    dw_ref[...] = jnp.zeros_like(dw_ref)
    dw_ref[:, C : 2 * C] = dw0_ref[...]
    coarse_level(
        meta, par_ref, pin_ref, pout_ref, mats[CO_F], mats[CO_B],
        place_ref, par, taps, up_rows, dw_ref,
    )

    @pl.loop(0, BIG_STEPS)
    def _(step):
        start = step * BIG
        for p in range(BIG):
            picked[p] = up_rows[meta[DST + start + p]]
        rows_in = picked[...].reshape(BIG * C, 128)
        up = dot_nt(rows_in, rest_ref[0]) * 8.0
        down = dot_nt(rows_in, rest_ref[1]) * 0.125
        dw_in = jnp.zeros((7 * C, C), F32)
        dw_out = jnp.zeros((7 * C, C), F32)
        for p in range(BIG):
            rows = slice(p * C, (p + 1) * C)
            here = start + p
            merged = (hidden_ref[here].astype(F32) + up[rows]).astype(BF)
            grad = gm_ref[here].astype(F32) + down[rows]
            gpa = (grad * slope_ref[here].astype(F32)).astype(BF)
            merged_ref[here] = merged
            gpa_ref[here] = gpa
            dw_in += dot_nt(ta_ref[here], gpa)
            dw_out += dot_nt(means_ref[here], picked[p])
        dw_ref[:, 0:C] += dw_in
        dw_ref[:, C : 2 * C] += dw_out * 8.0

    send_rows(
        meta[N_COUNT], meta[N_ODD], merged_ref, gpa_ref, sel_ref,
        v_rows, y_rows, sides, inner_ref.at[0:NEAR], outer_ref,
    )
    rounded = dw_ref[...].astype(BF).reshape(DWR, C, 128)
    sum_ref[...] = rounded
    inner_ref[NEAR : NEAR + DWR] = rounded


def second_table_kernel(v_ref, y_ref, sel_ref, got_ref, table):
    fill_table(v_ref, y_ref, sel_ref, table)
    table[BASE_A:BASE_B] = got_ref[0:NEAR]


def final_body(step, index, v_ref, y_ref, xs, zs, mats, sel_ref, table, coef, out_hbm, gs_hbm,
               picked, ta, tb, out_ref, gs_ref, sems):
    start = step * PB
    part = pl.ds(start, PB)
    block_taps(
        start, index, v_ref.at[part], y_ref.at[part], sel_ref, table, coef, picked, ta, tb
    )
    half = PB // 2
    copies = []
    for k in range(2):
        for p in range(k * half, (k + 1) * half):
            out_ref[p] = (xs[start + p].astype(F32) + dot(mats[OUT_F], ta[p])).astype(BF)
            gs_ref[p] = (zs[start + p].astype(F32) + dot(mats[IN_B], tb[p])).astype(BF)
        here, there = pl.ds(k * half, half), pl.ds(start + k * half, half)
        new = [
            pltpu.make_async_copy(out_ref.at[here], out_hbm.at[there], sems.at[k, 0]),
            pltpu.make_async_copy(gs_ref.at[here], gs_hbm.at[there], sems.at[k, 1]),
        ]
        for copy in new:
            copy.start()
        copies += new
    for copy in copies:
        copy.wait()


def first_final_kernel(
    index, v_ref, y_ref, xs, zs, mats, sel_ref, t_ref, b_ref, c_ref,
    table, coef, out_hbm, gs_hbm, *scratch,
):
    join_table((t_ref, b_ref, c_ref), coef, table)
    final_body(0, index, v_ref, y_ref, xs, zs, mats, sel_ref, table, coef, out_hbm, gs_hbm,
               *scratch)


def next_final_kernel(
    step, index, v_ref, y_ref, xs, zs, mats, sel_ref, table, coef, out_in, gs_in,
    out_hbm, gs_hbm, *scratch,
):
    final_body(step, index, v_ref, y_ref, xs, zs, mats, sel_ref, table, coef, out_hbm, gs_hbm,
               *scratch)


def weights_kernel(scale, one_ref, two_ref, in_ref, out_ref, co_ref):
    for f in range(7):
        total = (one_ref[f].astype(F32) + two_ref[f].astype(F32)) * scale
        in_ref[f] = total[:, 0:C]
        out_ref[f] = total[:, C : 2 * C].T
        co_ref[f] = total[:, 2 * C : 3 * C]


SMEM = functools.partial(pl.BlockSpec, memory_space=pltpu.SMEM)


VMEM = functools.partial(pl.BlockSpec, memory_space=pltpu.VMEM)
HBM = functools.partial(pl.BlockSpec, memory_space=pltpu.HBM)


def params(limit=VMEM_LIMIT):
    return pltpu.CompilerParams(vmem_limit_bytes=limit)


def shape_of(shape, dtype=BF):
    return jax.ShapeDtypeStruct(shape, dtype)


def cost(micros):
    return pl.CostEstimate(
        flops=int(micros * 1e6), bytes_accessed=int(micros * 3.0e6), transcendentals=0
    )


def pairs(kind, devices):
    if kind == "inner":
        links = [(2 * c, 2 * c + 1) for c in range(devices // 2)]
    else:
        links = [(2 * c + 1, 2 * c + 2) for c in range(devices // 2 - 1)]
    return links + [(b, a) for a, b in links]


def trade(block, kind):
    return lax.ppermute(block, "patch", pairs(kind, lax.axis_size("patch")))


def relay_out(outer, got_a):
    return trade(jnp.concatenate([outer, got_a[:FAR]], axis=0), "outer")


def relay_in(got_b, first):
    got_b, first = lax.optimization_barrier((got_b, first))
    return trade(got_b[:FAR], "inner"), first


def add(one, two):
    return (one.astype(F32) + two.astype(F32)).astype(BF)


def swap(block, mask):
    devices = lax.axis_size("patch")
    return lax.ppermute(block, "patch", [(i, i ^ mask) for i in range(devices)])


def on_device(
    fine_state, weight_in, weight_out, weight_coarse, cotangent,
    owner_count, neighbour, level_tag, octant,
):
    devices = lax.axis_size("patch")
    rest, place = [jnp.asarray(item) for item in constants()]

    field = (SLOTS, C, CELLS)
    stack = (SLOTS, 7 * C, CELLS)
    near = (NEAR, C, 128)
    far = (FAR, C, 128)
    par_rows = (NPAR * 8, C, 128)
    sel_shape = (6, CELLS, 256)
    rows_scratch = [pltpu.VMEM((16, C, CELLS), BF)] * 2 + [pltpu.VMEM((2, NEAR, C, 128), BF)]
    table_shape = (ROWS, C, 128)
    coef_shape = (12, 2, 16, CELLS)
    picked_scratch = pltpu.VMEM((PB, C, 256), BF)

    inner, outer, sel = pl.pallas_call(
        layers_kernel,
        in_specs=[HBM()] * 3,
        out_specs=[VMEM()] * 3,
        out_shape=[shape_of(near), shape_of(near), shape_of(sel_shape)],
        scratch_shapes=rows_scratch
        + [pltpu.VMEM(field, BF), pltpu.VMEM(field, BF)]
        + [pltpu.SMEM(owner_count.shape, jnp.int32)]
        + [pltpu.SemaphoreType.DMA((2, CHUNKS)), pltpu.SemaphoreType.DMA],
        compiler_params=params(),
        cost_estimate=cost(4),
        name="face_rows",
    )(
        pltpu.with_memory_space_constraint(owner_count, pltpu.HBM),
        pltpu.with_memory_space_constraint(fine_state, pltpu.HBM),
        pltpu.with_memory_space_constraint(cotangent, pltpu.HBM),
    )
    got_a = trade(inner, "inner")
    got_b = relay_out(outer, got_a)

    meta, index, xs, zs, mats, table = pl.pallas_call(
        prepare_kernel,
        in_specs=[SMEM()] * 2 + [VMEM()] * 8,
        out_specs=[SMEM()] + [VMEM()] * 5,
        out_shape=[shape_of((META,), jnp.int32), shape_of((12, SLOTS), jnp.int32)]
        + [shape_of(field), shape_of(field), shape_of((2, C, 7 * C)), shape_of((BASE_B, C, 128))],
        compiler_params=params(),
        cost_estimate=cost(4),
        name="prepare",
    )(
        owner_count, octant, neighbour.T, level_tag.T, got_a, fine_state, cotangent, sel,
        weight_in, weight_out,
    )
    got_c, meta = relay_in(got_b, meta)

    taps_a, taps_b, hidden, slope, grad_merged, par, pin, pout = pl.pallas_call(
        fine_kernel,
        in_specs=[SMEM()] * 2 + [VMEM()] * 8,
        out_specs=[VMEM()] * 8,
        out_shape=[shape_of(stack), shape_of(stack), shape_of(field), shape_of(field)]
        + [shape_of(field), shape_of(par_rows), shape_of(far), shape_of(far)],
        scratch_shapes=[
            pltpu.VMEM(table_shape, BF),
            pltpu.VMEM(coef_shape, BF),
            pltpu.VMEM((BIG, C, 256), BF),
            pltpu.VMEM((NPAR * 8 + 8, C, 128), BF),
            pltpu.VMEM((2, 16, C, 128), BF),
        ],
        compiler_params=params(),
        cost_estimate=cost(8),
        name="fine_level",
    )(meta, index, xs, zs, table, got_b, got_c, mats, sel, rest)
    child_out = trade(pout, "outer")
    child_in = trade(pin, "inner")

    mats, dw_part, means = pl.pallas_call(
        window_kernel,
        in_specs=[VMEM()] * 6,
        out_specs=[VMEM()] * 3,
        out_shape=[shape_of((4, C, 7 * C)), shape_of((7 * C, C), F32)]
        + [shape_of((SLOTS, 7 * C, 128))],
        compiler_params=params(),
        cost_estimate=cost(3),
        name="window",
    )(hidden, taps_b, rest, weight_in, weight_out, weight_coarse)

    merged, grad_pre, sums, inner, outer = pl.pallas_call(
        merge_kernel,
        in_specs=[SMEM()] + [VMEM()] * 13,
        out_specs=[VMEM()] * 5,
        out_shape=[shape_of(field), shape_of(field), shape_of((DWR, C, 128))]
        + [shape_of((NEAR + DWR, C, 128)), shape_of(near)],
        scratch_shapes=[
            pltpu.VMEM((NPAR * 8 + 8, C, 128), BF),
            pltpu.VMEM((NPAR, 7 * C, CELLS), BF),
            pltpu.VMEM((NPAR * 8 + 8, C, 128), BF),
            pltpu.VMEM((BIG, C, 128), BF),
        ]
        + rows_scratch
        + [pltpu.VMEM((7 * C, 128), F32)],
        compiler_params=params(),
        cost_estimate=cost(9),
        name="coarse_and_merge",
    )(
        meta, taps_a, means, dw_part, hidden, slope, grad_merged, par, child_in, child_out, mats,
        place, rest, sel,
    )
    got_a = trade(inner, "inner")
    got_b = relay_out(outer, got_a)
    sums = add(sums, got_a[NEAR:])
    sums = add(sums, swap(sums, 2))

    table = pl.pallas_call(
        second_table_kernel,
        in_specs=[VMEM()] * 4,
        out_specs=VMEM(),
        out_shape=shape_of((BASE_B, C, 128)),
        compiler_params=params(),
        cost_estimate=cost(2),
        name="face_table",
    )(merged, grad_pre, sel, got_a)
    got_c, table = relay_in(got_b, table)

    last_scratch = [
        picked_scratch,
        pltpu.VMEM((PB, 7 * C, CELLS), BF),
        pltpu.VMEM((PB, 7 * C, CELLS), BF),
        pltpu.VMEM((PB, C, CELLS), BF),
        pltpu.VMEM((PB, C, CELLS), BF),
        pltpu.SemaphoreType.DMA((2, 2)),
    ]
    fixed = (index, merged, grad_pre, xs, zs, mats, sel)
    sums, got_c = lax.optimization_barrier((add(sums, swap(sums, 6)), got_c))
    partner = swap(sums, 8)
    table, coef, output, grad_state = pl.pallas_call(
        first_final_kernel,
        in_specs=[SMEM()] + [VMEM()] * 9,
        out_specs=[VMEM(), VMEM(), HBM(), HBM()],
        out_shape=[shape_of(table_shape), shape_of(coef_shape), shape_of(field), shape_of(field)],
        scratch_shapes=last_scratch,
        compiler_params=params(),
        cost_estimate=cost(2),
        name="last_level",
    )(*fixed, table, got_b, got_c)
    for step, mask in ((1, 24), (2, 32), (3, 96)):
        sums, coef, output = lax.optimization_barrier((add(sums, partner), coef, output))
        partner = swap(sums, mask)
        output, grad_state = pl.pallas_call(
            functools.partial(next_final_kernel, step),
            in_specs=[SMEM()] + [VMEM()] * 8 + [HBM(), HBM()],
            out_specs=[HBM(), HBM()],
            out_shape=[shape_of(field), shape_of(field)],
            input_output_aliases={9: 0, 10: 1},
            scratch_shapes=last_scratch,
            compiler_params=params(),
            cost_estimate=cost(2),
            name="last_level",
        )(*fixed, table, coef, output, grad_state)

    scale = 1.0 / math.sqrt(float(devices * SLOTS * CELLS))
    mat = shape_of((7, C, C), F32)
    grads = pl.pallas_call(
        functools.partial(weights_kernel, scale),
        in_specs=[VMEM()] * 2,
        out_specs=[VMEM()] * 3,
        compiler_params=params(),
        out_shape=[mat, mat, mat],
        cost_estimate=cost(1),
        name="weight_sums",
    )(sums, partner)
    return (output, grad_state, *grads)


def solution(mesh):
    in_specs = (
        P("patch", None, None),
        P(),
        P(),
        P(),
        P("patch", None, None),
        P(),
        P("patch", None),
        P("patch", None),
        P("patch"),
    )
    out_specs = (P("patch", None, None), P("patch", None, None), P(), P(), P())
    return jax.shard_map(
        on_device, mesh=mesh, in_specs=in_specs, out_specs=out_specs, check_vma=False
    )
```

```python
import functools
import math

import numpy as np
import jax
import jax.numpy as jnp
from jax import lax
from jax.experimental import pallas as pl
from jax.experimental.pallas import tpu as pltpu
from jax.sharding import PartitionSpec as P

BF = jnp.bfloat16
F32 = jnp.float32
EDGE = 8
CELLS = 512
SLOTS = 32
C = 32
PB = 8
STEPS = SLOTS // PB
BIG = 32
BIG_STEPS = SLOTS // BIG
NPAR = 5
STRIDES = (64, 8, 1)
MORTON = (3, 8, 16)
ROW0 = (24, 16, 0)
NEAR = 27
FAR = 8
BASE_A = 6 * SLOTS
BASE_B = BASE_A + NEAR
BASE_C = BASE_B + NEAR + FAR
ROWS = BASE_C + FAR
VMEM_LIMIT = 14 * 1024 * 1024
DST, LEAD, TRAIL, SCAL = 0, 32, 64, 96
N_COUNT, N_ODD, N_LAST, N_OWNED = SCAL, SCAL + 1, SCAL + 2, SCAL + 3
META = 128
IN_F, OUT_B = range(2)
OUT_F, IN_B, CO_F, CO_B = range(4)
CHUNKS = 8
DWR = 7


def cell_coords():
    ids = np.arange(CELLS)
    return [ids // 64, ids // 8 % 8, ids % 8]


def constants():
    c0, c1, c2 = cell_coords()
    group = (c0 // 2) * 16 + (c1 // 2) * 4 + c2 // 2
    rest = np.zeros((2, CELLS, 128), np.float32)
    for cell in range(CELLS):
        rest[0, cell, group[cell]] = 0.125
        rest[1, cell, 64 + group[cell]] = 1
    place = np.zeros((256, 2 * CELLS), np.float32)
    for o2 in range(2):
        for a in range(64):
            cell = (a // 16) * 64 + (a // 4 % 4) * 8 + a % 4 + 4 * o2
            place[128 * o2 + a, cell] = 1
            place[128 * o2 + 64 + a, CELLS + cell] = 1
    as_bf = lambda item: np.asarray(item, jnp.bfloat16)
    return (
        as_bf(rest),
        as_bf(place),
    )


def dot(a, b):
    return jnp.dot(a, b, preferred_element_type=F32)


def dot_nt(a, b):
    return lax.dot_general(a, b, (((1,), (1,)), ((), ())), preferred_element_type=F32)


def coord_of(dim):
    lane = lax.broadcasted_iota(jnp.int32, (16, CELLS), 1)
    return (lane // STRIDES[dim]) % EDGE


def on_face(face):
    edge = EDGE - 1 if face % 2 else 0
    return jnp.where(coord_of(face // 2) == edge, 1.0, 0.0)


def halves(field):
    return field.reshape(field.shape[0] // 16, 16, CELLS)


def times(field, mask):
    return (halves(field) * mask[None]).reshape(field.shape)


def toward(field, face):
    stride = STRIDES[face // 2]
    shift = CELLS - stride if face % 2 else stride
    return pltpu.roll(field, shift, 1)


def send_rows(
    count, odd, v_ref, y_ref, sel_ref, v_rows, y_rows, sides, inner_ref, outer_ref, waits=((), ())
):
    for side in range(2):
        for copy in waits[side]:
            copy.wait()
        if side:
            for i in range(16):
                slot = jnp.clip(count - 16 + i, 0, SLOTS - 1)
                v_rows[i] = v_ref[slot]
                y_rows[i] = y_ref[slot]
        for dim in (2, 1, 0):
            depth = MORTON[dim]
            v_part = v_rows[16 - depth : 16] if side else v_ref[0:depth]
            y_part = y_rows[16 - depth : 16] if side else y_ref[0:depth]
            cols = slice(side * 128, side * 128 + 128)
            layers = dot(v_part.reshape(depth * C, CELLS), sel_ref[2 * dim, :, cols])
            layers += dot(y_part.reshape(depth * C, CELLS), sel_ref[2 * dim + 1, :, cols])
            layers = layers.astype(BF).reshape(depth, C, 128)
            if dim == 2 and side:
                sides[side, 0:8] = layers[8:16]
                sides[side, 8:16] = layers[0:8]
            else:
                sides[side, ROW0[dim] : ROW0[dim] + depth] = layers
    inner_ref[...] = sides[1 - odd]
    outer_ref[...] = sides[odd]


def make_selection(sel_ref):
    cell = lax.broadcasted_iota(jnp.int32, (CELLS, 256), 0)
    lane = lax.broadcasted_iota(jnp.int32, (CELLS, 256), 1)
    at = lane % 64
    edge = jnp.where(lane < 128, 0, EDGE - 1)
    first_half = lane % 128 < 64
    for dim in range(3):
        if dim == 0:
            want = edge * 64 + at
        elif dim == 1:
            want = at // 8 * 64 + edge * 8 + at % 8
        else:
            want = at * 8 + edge
        hit = cell == want
        sel_ref[2 * dim] = jnp.where(hit & first_half, 1.0, 0.0).astype(BF)
        sel_ref[2 * dim + 1] = jnp.where(hit & ~first_half, 1.0, 0.0).astype(BF)


def layers_kernel(
    counts_hbm, x_hbm, z_hbm, inner_ref, outer_ref, sel_ref,
    v_rows, y_rows, sides, x_ref, z_ref, counts, sems, counts_sem,
):
    rank = lax.axis_index("patch")
    size = SLOTS // CHUNKS
    count_copy = pltpu.make_async_copy(counts_hbm, counts, counts_sem)
    count_copy.start()
    copies = []
    for k in range(CHUNKS):
        part = pl.ds(k * size, size)
        copies.append(pltpu.make_async_copy(x_hbm.at[part], x_ref.at[part], sems.at[0, k]))
        copies.append(pltpu.make_async_copy(z_hbm.at[part], z_ref.at[part], sems.at[1, k]))
    for copy in copies:
        copy.start()
    make_selection(sel_ref)
    count_copy.wait()
    send_rows(
        counts[rank], rank % 2, x_ref, z_ref, sel_ref, v_rows, y_rows, sides, inner_ref, outer_ref,
        waits=(copies[:CHUNKS], copies[CHUNKS:]),
    )


def fill_table(v_ref, y_ref, sel_ref, table):
    for dim in range(3):
        layers = dot(v_ref[...].reshape(SLOTS * C, CELLS), sel_ref[2 * dim])
        layers += dot(y_ref[...].reshape(SLOTS * C, CELLS), sel_ref[2 * dim + 1])
        layers = layers.astype(BF)
        for high in range(2):
            face = 2 * dim + high
            table[face * SLOTS : (face + 1) * SLOTS] = layers[
                :, high * 128 : high * 128 + 128
            ].reshape(SLOTS, C, 128)


def fill_mats(mats, weights):
    for k, (weight, turned) in enumerate(weights):
        for f in range(7):
            one = weight[f].astype(F32)
            mats[k, :, f * C : (f + 1) * C] = (one.T if turned else one).astype(BF)


def prepare_kernel(
    counts, octant, neighbour, level_tag,
    got_ref, x_ref, z_ref, sel_ref, w_in, w_out,
    meta, index, xs, zs, mats, table, coef,
):
    rank = lax.axis_index("patch")
    odd = rank % 2

    def count_at(device):
        here = counts[jnp.clip(device, 0, counts.shape[0] - 1)]
        return jnp.where(device < 0, 0, here)

    first = lax.fori_loop(0, rank, lambda d, s: s + counts[d], jnp.int32(0))
    count = count_at(rank)
    count_1 = count_at(rank - 1)
    count_2 = count_at(rank - 2)
    stop = first + count
    meta[N_COUNT] = count
    meta[N_ODD] = odd
    meta[N_LAST] = jnp.where(stop % 8 != 0, stop // 8 - first // 8, NPAR)
    meta[N_OWNED] = jnp.where(first % 8 == 0, 1, 0)
    lead_count = (8 - first % 8) % 8
    for p in range(SLOTS):
        live = p < count
        parent = (first % 8 + p) // 8
        o = jnp.clip(octant[p], 0, 7)
        meta[DST + p] = jnp.where(live, parent * 8 + o, NPAR * 8)
        meta[LEAD + p] = jnp.where(live & (p < lead_count), o, 8)
        meta[TRAIL + p] = jnp.where(live & (p >= count - stop % 8), o, 8)

    near_left = jnp.where(odd == 1, BASE_A, BASE_B)
    near_right = jnp.where(odd == 1, BASE_B, BASE_A)
    far_left = jnp.where(odd == 1, BASE_C, BASE_B + NEAR)
    far_right = jnp.where(odd == 1, BASE_B + NEAR, BASE_C)
    face = lax.broadcasted_iota(jnp.int32, (6, SLOTS), 0)
    own = lax.broadcasted_iota(jnp.int32, (6, SLOTS), 1)
    depth = jnp.where(face < 2, MORTON[0], jnp.where(face < 4, MORTON[1], MORTON[2]))
    row0 = jnp.where(face < 2, ROW0[0], jnp.where(face < 4, ROW0[1], ROW0[2]))
    high = (face & 1) == 1
    other = neighbour[...]
    away = (other >> 5) - rank
    slot = other & 31
    back = slot - (count_1 - depth)
    left = jnp.where(face >= 4, (back + 8) & 15, row0 + back) + near_left
    near = jnp.where(high, near_right + row0 + slot, left)
    far = jnp.where(high, far_right + slot, far_left + slot - (count_2 - 8))
    row = jnp.where(away == 0, (face ^ 1) * SLOTS + slot, near)
    row = jnp.where((away == 2) | (away == -2), far, row)
    row = jnp.where(level_tag[...] == 1, face * SLOTS + own, row)
    index[0:6] = jnp.clip(row, 0, ROWS - 1)
    index[6:12] = level_tag[...]

    fill_mats(mats, ((w_in, True), (w_out, False)))
    fill_coef(coef)
    for p in range(SLOTS):
        live = (p < count).astype(F32)
        xs[p] = (x_ref[p].astype(F32) * live).astype(BF)
        zs[p] = (z_ref[p].astype(F32) * live).astype(BF)
    fill_table(xs, zs, sel_ref, table)
    table[BASE_A:BASE_B] = got_ref[...]


def window_kernel(hidden_ref, tb_ref, rest_ref, w_in, w_out, w_co, mats, dw_ref, means_ref):
    fill_mats(mats, ((w_out, True), (w_in, False), (w_co, True), (w_co, False)))
    dw_ref[...] = jnp.zeros_like(dw_ref)

    @pl.loop(0, BIG_STEPS)
    def _(step):
        dw = jnp.zeros((7 * C, C), F32)
        for p in range(BIG):
            here = step * BIG + p
            dw += dot_nt(tb_ref[here], hidden_ref[here])
            means_ref[here] = dot(tb_ref[here], rest_ref[0]).astype(BF)
        dw_ref[...] += dw


def table_kernel(v_ref, y_ref, sel_ref, table):
    fill_table(v_ref, y_ref, sel_ref, table)


def join_table(parts, table):
    start = 0
    for part in parts:
        size = part.shape[0]
        table[start : start + size] = part[...]
        start += size


def fill_coef(coef):
    for dim in range(3):
        low, high = on_face(2 * dim), on_face(2 * dim + 1)
        for t_low in range(2):
            for t_high in range(2):
                row = dim * 4 + t_low * 2 + t_high
                coef[row, 0] = (low * (1 - t_low) + high * t_high).astype(BF)
                coef[row, 1] = (high * (1 - t_high) + low * t_low).astype(BF)


def block_taps(start, index, v_ref, y_ref, sel_ref, table, coef, picked, ta, tb):
    size = v_ref.shape[0]
    for dim in range(3):
        low, high = 2 * dim, 2 * dim + 1
        edges = [on_face(low), on_face(high)]
        edges = [edge.astype(BF) for edge in edges]
        if dim:
            for p in range(size):
                picked[p, :, 0:128] = table[index[low, start + p]]
                picked[p, :, 128:256] = table[index[high, start + p]]
            rows_in = picked[...].reshape(size * C, 256)
            v_spread = dot_nt(rows_in, sel_ref[2 * dim]).astype(BF)
            y_spread = dot_nt(rows_in, sel_ref[2 * dim + 1]).astype(BF)
        for p in range(size):
            if dim:
                rows = slice(p * C, (p + 1) * C)
                v_edge = v_spread[rows]
                y_edge = y_spread[rows]
            else:
                r_low = table[index[low, start + p]]
                r_high = table[index[high, start + p]]
                blank = jnp.zeros((C, 256), BF)
                v_edge = jnp.concatenate([r_low, blank, pltpu.roll(r_high, 64, 1)], axis=1)
                y_edge = jnp.concatenate([pltpu.roll(r_low, 64, 1), blank, r_high], axis=1)
            field = v_ref[p]
            other = y_ref[p]
            if dim == 0:
                ta[p, 0:C] = field
                tb[p, 0:C] = other
            row = (
                dim * 4
                + index[6 + low, start + p] * 2
                + index[6 + high, start + p]
            )
            for k, face in enumerate((low, high)):
                ta[p, C * (face + 1) : C * (face + 2)] = jnp.where(
                    edges[k][None] > 0, halves(v_edge), halves(toward(field, face))
                ).reshape(C, CELLS)
                back = face ^ 1
                kept = jnp.where(edges[k][None] > 0, 0.0, halves(toward(other, face)))
                tb[p, C * (back + 1) : C * (back + 2)] = (
                    kept + halves(y_edge) * coef[row, k][None]
                ).reshape(C, CELLS)


def silu_pair(pre):
    sigma = 1.0 / (1.0 + jnp.exp(-pre))
    return pre * sigma, sigma * (1.0 + pre * (1.0 - sigma))


def fine_kernel(
    meta, index, xs, zs, t_ref, b_ref, c_ref, coef, mats, sel_ref, rest_ref,
    ta_ref, tb_ref, hidden_ref, slope_ref, gm_ref, par_ref, inner_ref, outer_ref,
    table, picked, par, ends,
):
    join_table((t_ref, b_ref, c_ref), table)
    par[...] = jnp.zeros_like(par)
    ends[...] = jnp.zeros_like(ends)

    @pl.loop(0, BIG_STEPS)
    def _(step):
        start = step * BIG
        x_at, z_at, ta, tb, hidden_at, slope_at, gm_at = [
            item.at[pl.ds(start, BIG)]
            for item in (xs, zs, ta_ref, tb_ref, hidden_ref, slope_ref, gm_ref)
        ]
        block_taps(start, index, x_at, z_at, sel_ref, table, coef, picked, ta, tb)
        for p in range(BIG):
            hidden, slope = silu_pair(dot(mats[IN_F], ta[p]))
            hidden_at[p] = hidden.astype(BF)
            slope_at[p] = slope.astype(BF)
            gm_at[p] = dot(mats[OUT_B], tb[p]).astype(BF)
        child = dot(hidden_at[...].reshape(BIG * C, CELLS), rest_ref[0])
        child += dot(gm_at[...].reshape(BIG * C, CELLS), rest_ref[1])
        child = child.astype(BF)
        for p in range(BIG):
            row = child[p * C : (p + 1) * C]
            par[meta[DST + start + p]] = row
            ends[0, meta[LEAD + start + p]] = row
            ends[1, meta[TRAIL + start + p]] = row

    par_ref[...] = par[: NPAR * 8]
    odd = meta[N_ODD]
    inner_ref[...] = ends[1 - odd, 0:8]
    outer_ref[...] = ends[odd, 0:8]


def coarse_level(meta, par_ref, inner_ref, outer_ref, wa, wb, place_ref, par, taps, up_rows, dw_ref):
    par[: NPAR * 8] = par_ref[...]
    par[NPAR * 8 :] = jnp.zeros((8, C, 128), BF)
    last = meta[N_LAST] * 8
    odd = meta[N_ODD]
    inner_at = jnp.where(odd == 1, 0, last)
    outer_at = jnp.where(odd == 1, last, 0)
    for o in range(8):
        par[inner_at + o] = par[inner_at + o] + inner_ref[o]
    for o in range(8):
        par[outer_at + o] = par[outer_at + o] + outer_ref[o]

    rows = NPAR * C
    both = jnp.zeros((rows, 2 * CELLS), BF)
    for o in range(0, 8, 2):
        lhs = jnp.concatenate(
            [
                jnp.concatenate([par[q * 8 + o], par[q * 8 + o + 1]], axis=1)
                for q in range(NPAR)
            ],
            axis=0,
        )
        put = dot(lhs, place_ref[...]).astype(BF)
        shift = (o // 4) * 256 + (o // 2 % 2) * 32
        if shift:
            put = jnp.concatenate(
                [
                    pltpu.roll(put[:, :CELLS], shift, 1),
                    pltpu.roll(put[:, CELLS:], shift, 1),
                ],
                axis=1,
            )
        both += put
    field = both[:, :CELLS]
    cotan = both[:, CELLS:].astype(F32)
    edges = [on_face(face).astype(BF) for face in range(6)]
    inside = [(1.0 - on_face(face)).astype(BF) for face in range(6)]

    def store(face, value):
        taps[:, C * face : C * (face + 1)] = value.reshape(NPAR, C, CELLS)

    store(0, field)
    for face in range(6):
        store(face + 1, times(toward(field, face), inside[face]) + times(field, edges[face]))
    pre = jnp.concatenate([dot(wa, taps[q]) for q in range(NPAR)], axis=0)
    act, slope = silu_pair(pre)
    act = act.astype(BF)
    grad = (cotan * slope).astype(BF)
    dw = jnp.zeros((7 * C, C), F32)
    for q in range(NPAR):
        part = dot_nt(taps[q], grad[q * C : (q + 1) * C])
        if q == 0:
            part = part * meta[N_OWNED].astype(F32)
        dw += part
    store(0, grad)
    for face in range(6):
        back = face ^ 1
        store(face + 1, times(toward(grad, back), inside[back]) + times(grad, edges[face]))
    down = jnp.concatenate([dot(wb, taps[q]) for q in range(NPAR)], axis=0).astype(BF)
    for o in range(0, 8, 2):
        one, two = act, down
        shift = (o // 4) * 256 + (o // 2 % 2) * 32
        if shift:
            one = pltpu.roll(act, CELLS - shift, 1)
            two = pltpu.roll(down, CELLS - shift, 1)
        got = dot_nt(one, place_ref[:, :CELLS]) + dot_nt(two, place_ref[:, CELLS:])
        got = got.astype(BF)
        for q in range(NPAR):
            up_rows[q * 8 + o] = got[q * C : (q + 1) * C, :128]
            up_rows[q * 8 + o + 1] = got[q * C : (q + 1) * C, 128:]
    up_rows[NPAR * 8] = jnp.zeros((C, 128), BF)
    dw_ref[:, 2 * C : 3 * C] = dw


def merge_kernel(
    meta,
    ta_ref, means_ref, dw0_ref, hidden_ref, slope_ref, gm_ref, par_ref, pin_ref, pout_ref,
    mats, place_ref, rest_ref, sel_ref,
    merged_ref, gpa_ref, sum_ref, inner_ref, outer_ref,
    par, taps, up_rows, picked, v_rows, y_rows, sides, dw_ref,
):
    dw_ref[...] = jnp.zeros_like(dw_ref)
    dw_ref[:, C : 2 * C] = dw0_ref[...]
    coarse_level(
        meta, par_ref, pin_ref, pout_ref, mats[CO_F], mats[CO_B],
        place_ref, par, taps, up_rows, dw_ref,
    )

    @pl.loop(0, BIG_STEPS)
    def _(step):
        start = step * BIG
        for p in range(BIG):
            picked[p] = up_rows[meta[DST + start + p]]
        rows_in = picked[...].reshape(BIG * C, 128)
        up = dot_nt(rows_in, rest_ref[0]) * 8.0
        down = dot_nt(rows_in, rest_ref[1]) * 0.125
        dw_in = jnp.zeros((7 * C, C), F32)
        dw_out = jnp.zeros((7 * C, C), F32)
        for p in range(BIG):
            rows = slice(p * C, (p + 1) * C)
            here = start + p
            merged = (hidden_ref[here].astype(F32) + up[rows]).astype(BF)
            grad = gm_ref[here].astype(F32) + down[rows]
            gpa = (grad * slope_ref[here].astype(F32)).astype(BF)
            merged_ref[here] = merged
            gpa_ref[here] = gpa
            dw_in += dot_nt(ta_ref[here], gpa)
            dw_out += dot_nt(means_ref[here], picked[p])
        dw_ref[:, 0:C] += dw_in
        dw_ref[:, C : 2 * C] += dw_out * 8.0

    send_rows(
        meta[N_COUNT], meta[N_ODD], merged_ref, gpa_ref, sel_ref,
        v_rows, y_rows, sides, inner_ref.at[0:NEAR], outer_ref,
    )
    rounded = dw_ref[...].astype(BF).reshape(DWR, C, 128)
    sum_ref[...] = rounded
    inner_ref[NEAR : NEAR + DWR] = rounded


def second_table_kernel(v_ref, y_ref, sel_ref, got_ref, table):
    fill_table(v_ref, y_ref, sel_ref, table)
    table[BASE_A:BASE_B] = got_ref[0:NEAR]


def final_body(step, index, v_ref, y_ref, xs, zs, mats, sel_ref, table, coef, out_hbm, gs_hbm,
               picked, ta, tb, out_ref, gs_ref, sems):
    start = step * PB
    part = pl.ds(start, PB)
    block_taps(
        start, index, v_ref.at[part], y_ref.at[part], sel_ref, table, coef, picked, ta, tb
    )
    half = PB // 2
    copies = []
    for k in range(2):
        for p in range(k * half, (k + 1) * half):
            out_ref[p] = (xs[start + p].astype(F32) + dot(mats[OUT_F], ta[p])).astype(BF)
            gs_ref[p] = (zs[start + p].astype(F32) + dot(mats[IN_B], tb[p])).astype(BF)
        here, there = pl.ds(k * half, half), pl.ds(start + k * half, half)
        new = [
            pltpu.make_async_copy(out_ref.at[here], out_hbm.at[there], sems.at[k, 0]),
            pltpu.make_async_copy(gs_ref.at[here], gs_hbm.at[there], sems.at[k, 1]),
        ]
        for copy in new:
            copy.start()
        copies += new
    for copy in copies:
        copy.wait()


def first_final_kernel(
    index, v_ref, y_ref, xs, zs, mats, sel_ref, t_ref, b_ref, c_ref, coef,
    table, out_hbm, gs_hbm, *scratch,
):
    join_table((t_ref, b_ref, c_ref), table)
    final_body(0, index, v_ref, y_ref, xs, zs, mats, sel_ref, table, coef, out_hbm, gs_hbm,
               *scratch)


def next_final_kernel(
    step, index, v_ref, y_ref, xs, zs, mats, sel_ref, table, coef, out_in, gs_in,
    out_hbm, gs_hbm, *scratch,
):
    final_body(step, index, v_ref, y_ref, xs, zs, mats, sel_ref, table, coef, out_hbm, gs_hbm,
               *scratch)


def weights_kernel(scale, one_ref, two_ref, in_ref, out_ref, co_ref):
    for f in range(7):
        total = (one_ref[f].astype(F32) + two_ref[f].astype(F32)) * scale
        in_ref[f] = total[:, 0:C]
        out_ref[f] = total[:, C : 2 * C].T
        co_ref[f] = total[:, 2 * C : 3 * C]


SMEM = functools.partial(pl.BlockSpec, memory_space=pltpu.SMEM)


VMEM = functools.partial(pl.BlockSpec, memory_space=pltpu.VMEM)
HBM = functools.partial(pl.BlockSpec, memory_space=pltpu.HBM)


def params(limit=VMEM_LIMIT):
    return pltpu.CompilerParams(vmem_limit_bytes=limit)


def shape_of(shape, dtype=BF):
    return jax.ShapeDtypeStruct(shape, dtype)


def cost(micros):
    return pl.CostEstimate(
        flops=int(micros * 1e6), bytes_accessed=int(micros * 3.0e6), transcendentals=0
    )


def pairs(kind, devices):
    if kind == "inner":
        links = [(2 * c, 2 * c + 1) for c in range(devices // 2)]
    else:
        links = [(2 * c + 1, 2 * c + 2) for c in range(devices // 2 - 1)]
    return links + [(b, a) for a, b in links]


def trade(block, kind):
    return lax.ppermute(block, "patch", pairs(kind, lax.axis_size("patch")))


def relay_out(outer, got_a):
    return trade(jnp.concatenate([outer, got_a[:FAR]], axis=0), "outer")


def relay_in(got_b, first):
    got_b, first = lax.optimization_barrier((got_b, first))
    return trade(got_b[:FAR], "inner"), first


def add(one, two):
    return (one.astype(F32) + two.astype(F32)).astype(BF)


def swap(block, mask):
    devices = lax.axis_size("patch")
    return lax.ppermute(block, "patch", [(i, i ^ mask) for i in range(devices)])


def on_device(
    fine_state, weight_in, weight_out, weight_coarse, cotangent,
    owner_count, neighbour, level_tag, octant,
):
    devices = lax.axis_size("patch")
    rest, place = [jnp.asarray(item) for item in constants()]

    field = (SLOTS, C, CELLS)
    stack = (SLOTS, 7 * C, CELLS)
    near = (NEAR, C, 128)
    far = (FAR, C, 128)
    par_rows = (NPAR * 8, C, 128)
    sel_shape = (6, CELLS, 256)
    rows_scratch = [pltpu.VMEM((16, C, CELLS), BF)] * 2 + [pltpu.VMEM((2, NEAR, C, 128), BF)]
    table_shape = (ROWS, C, 128)
    coef_shape = (12, 2, 16, CELLS)
    picked_scratch = pltpu.VMEM((PB, C, 256), BF)

    inner, outer, sel = pl.pallas_call(
        layers_kernel,
        in_specs=[HBM()] * 3,
        out_specs=[VMEM()] * 3,
        out_shape=[shape_of(near), shape_of(near), shape_of(sel_shape)],
        scratch_shapes=rows_scratch
        + [pltpu.VMEM(field, BF), pltpu.VMEM(field, BF)]
        + [pltpu.SMEM(owner_count.shape, jnp.int32)]
        + [pltpu.SemaphoreType.DMA((2, CHUNKS)), pltpu.SemaphoreType.DMA],
        compiler_params=params(),
        cost_estimate=cost(4),
        name="face_rows",
    )(
        pltpu.with_memory_space_constraint(owner_count, pltpu.HBM),
        pltpu.with_memory_space_constraint(fine_state, pltpu.HBM),
        pltpu.with_memory_space_constraint(cotangent, pltpu.HBM),
    )
    got_a = trade(inner, "inner")
    got_b = relay_out(outer, got_a)

    meta, index, xs, zs, mats, table, coef = pl.pallas_call(
        prepare_kernel,
        in_specs=[SMEM()] * 2 + [VMEM()] * 8,
        out_specs=[SMEM()] + [VMEM()] * 6,
        out_shape=[shape_of((META,), jnp.int32), shape_of((12, SLOTS), jnp.int32)]
        + [shape_of(field), shape_of(field), shape_of((2, C, 7 * C)), shape_of((BASE_B, C, 128))]
        + [shape_of(coef_shape)],
        compiler_params=params(),
        cost_estimate=cost(4),
        name="prepare",
    )(
        owner_count, octant, neighbour.T, level_tag.T, got_a, fine_state, cotangent, sel,
        weight_in, weight_out,
    )
    got_c, meta = relay_in(got_b, meta)

    taps_a, taps_b, hidden, slope, grad_merged, par, pin, pout = pl.pallas_call(
        fine_kernel,
        in_specs=[SMEM()] * 2 + [VMEM()] * 9,
        out_specs=[VMEM()] * 8,
        out_shape=[shape_of(stack), shape_of(stack), shape_of(field), shape_of(field)]
        + [shape_of(field), shape_of(par_rows), shape_of(far), shape_of(far)],
        scratch_shapes=[
            pltpu.VMEM(table_shape, BF),
            pltpu.VMEM((BIG, C, 256), BF),
            pltpu.VMEM((NPAR * 8 + 8, C, 128), BF),
            pltpu.VMEM((2, 16, C, 128), BF),
        ],
        compiler_params=params(),
        cost_estimate=cost(8),
        name="fine_level",
    )(meta, index, xs, zs, table, got_b, got_c, coef, mats, sel, rest)
    child_out = trade(pout, "outer")
    child_in = trade(pin, "inner")

    mats, dw_part, means = pl.pallas_call(
        window_kernel,
        in_specs=[VMEM()] * 6,
        out_specs=[VMEM()] * 3,
        out_shape=[shape_of((4, C, 7 * C)), shape_of((7 * C, C), F32)]
        + [shape_of((SLOTS, 7 * C, 128))],
        compiler_params=params(),
        cost_estimate=cost(3),
        name="window",
    )(hidden, taps_b, rest, weight_in, weight_out, weight_coarse)

    merged, grad_pre, sums, inner, outer = pl.pallas_call(
        merge_kernel,
        in_specs=[SMEM()] + [VMEM()] * 13,
        out_specs=[VMEM()] * 5,
        out_shape=[shape_of(field), shape_of(field), shape_of((DWR, C, 128))]
        + [shape_of((NEAR + DWR, C, 128)), shape_of(near)],
        scratch_shapes=[
            pltpu.VMEM((NPAR * 8 + 8, C, 128), BF),
            pltpu.VMEM((NPAR, 7 * C, CELLS), BF),
            pltpu.VMEM((NPAR * 8 + 8, C, 128), BF),
            pltpu.VMEM((BIG, C, 128), BF),
        ]
        + rows_scratch
        + [pltpu.VMEM((7 * C, 128), F32)],
        compiler_params=params(),
        cost_estimate=cost(9),
        name="coarse_and_merge",
    )(
        meta, taps_a, means, dw_part, hidden, slope, grad_merged, par, child_in, child_out, mats,
        place, rest, sel,
    )
    got_a = trade(inner, "inner")
    got_b = relay_out(outer, got_a)
    sums = add(sums, got_a[NEAR:])
    sums = add(sums, swap(sums, 2))

    table = pl.pallas_call(
        second_table_kernel,
        in_specs=[VMEM()] * 4,
        out_specs=VMEM(),
        out_shape=shape_of((BASE_B, C, 128)),
        compiler_params=params(),
        cost_estimate=cost(2),
        name="face_table",
    )(merged, grad_pre, sel, got_a)
    got_c, table = relay_in(got_b, table)

    last_scratch = [
        picked_scratch,
        pltpu.VMEM((PB, 7 * C, CELLS), BF),
        pltpu.VMEM((PB, 7 * C, CELLS), BF),
        pltpu.VMEM((PB, C, CELLS), BF),
        pltpu.VMEM((PB, C, CELLS), BF),
        pltpu.SemaphoreType.DMA((2, 2)),
    ]
    fixed = (index, merged, grad_pre, xs, zs, mats, sel)
    sums, got_c = lax.optimization_barrier((add(sums, swap(sums, 6)), got_c))
    partner = swap(sums, 8)
    table, output, grad_state = pl.pallas_call(
        first_final_kernel,
        in_specs=[SMEM()] + [VMEM()] * 10,
        out_specs=[VMEM(), HBM(), HBM()],
        out_shape=[shape_of(table_shape), shape_of(field), shape_of(field)],
        scratch_shapes=last_scratch,
        compiler_params=params(),
        cost_estimate=cost(2),
        name="last_level",
    )(*fixed, table, got_b, got_c, coef)
    for step, mask in ((1, 24), (2, 32), (3, 96)):
        sums, output = lax.optimization_barrier((add(sums, partner), output))
        partner = swap(sums, mask)
        output, grad_state = pl.pallas_call(
            functools.partial(next_final_kernel, step),
            in_specs=[SMEM()] + [VMEM()] * 8 + [HBM(), HBM()],
            out_specs=[HBM(), HBM()],
            out_shape=[shape_of(field), shape_of(field)],
            input_output_aliases={9: 0, 10: 1},
            scratch_shapes=last_scratch,
            compiler_params=params(),
            cost_estimate=cost(2),
            name="last_level",
        )(*fixed, table, coef, output, grad_state)

    scale = 1.0 / math.sqrt(float(devices * SLOTS * CELLS))
    mat = shape_of((7, C, C), F32)
    grads = pl.pallas_call(
        functools.partial(weights_kernel, scale),
        in_specs=[VMEM()] * 2,
        out_specs=[VMEM()] * 3,
        compiler_params=params(),
        out_shape=[mat, mat, mat],
        cost_estimate=cost(1),
        name="weight_sums",
    )(sums, partner)
    return (output, grad_state, *grads)


def solution(mesh):
    in_specs = (
        P("patch", None, None),
        P(),
        P(),
        P(),
        P("patch", None, None),
        P(),
        P("patch", None),
        P("patch", None),
        P("patch"),
    )
    out_specs = (P("patch", None, None), P("patch", None, None), P(), P(), P())
    return jax.shard_map(
        on_device, mesh=mesh, in_specs=in_specs, out_specs=out_specs, check_vma=False
    )
```
